32 devices in a mesh: grp: 4 (over x, core), ep: 8 (over z, y).
Axes of the slice: x: 2, y: 2, z: 4, core: 2. Of those that a mesh axis runs over, the one named last changes fastest.
Arguments:
- tokens: bfloat16 [16384, 1024], P(('grp', 'ep')), may hold values from -6 to 6
- cotangent: bfloat16 [16384, 1024], P(('grp', 'ep')), may hold values from -6 to 6
- w_qkv: bfloat16 [1024, 3072], replicated, may hold values from -0.1875 to 0.1875
- w_out_attn: bfloat16 [1024, 1024], replicated, may hold values from -1.5 to 1.5
- rel_bias: bfloat16 [16, 512, 512], replicated, may hold values from -3 to 3
- norm_gains: float32 [2, 1024], replicated, may hold values from 0.1 to 1.9
- w_router: bfloat16 [1024, 8], replicated, may hold values from -0.125 to 0.125
- w_gate_up: bfloat16 [8, 1024, 5632], P('ep'), may hold values from -0.1875 to 0.1875
- w_expert_out: bfloat16 [8, 2816, 1024], P('ep'), may hold values from -0.75 to 0.75
- routes: int32 [16384, 2], P(('grp', 'ep')), may hold values from 0 to 7, all different within a row; in each aligned block of 512 rows (0 to 511, 512 to 1023, ...) at most 160 rows name the same one
- spans: int32 [32, 2], P(('grp', 'ep')), may hold values from 0 to 384, as said below
Outputs:
- output: float32 [16384, 1024], P(('grp', 'ep'))
- grad_tokens: float32 [16384, 1024], P(('grp', 'ep'))
- grad_w_qkv: float32 [1024, 3072], P('grp', 'ep')
- grad_w_out_attn: float32 [1024, 1024], P('grp', 'ep')
- grad_rel_bias: float32 [16, 512, 512], P('ep', 'grp')
- grad_norm_gains: float32 [2, 1024], replicated
- grad_w_router: float32 [1024, 8], replicated
- grad_w_gate_up: float32 [8, 1024, 5632], P('ep', 'grp')
- grad_w_expert_out: float32 [8, 2816, 1024], P('ep', 'grp')
The draws below stay inside these ranges and needn't reach their ends.
Inputs may be any that keep to these rules, and one draw needn't show every extreme that they name: `routes`: each row names 2 different experts; within each aligned block of 512 rows (the rows of one device) no expert is named more than 160 times. `spans`: row s is the start and the length of sequence s's picture span: the length lies between 128 and 256, start + length <= 512; sequence 0's span starts at 0 with length 256, and sequence 1's span has length 128 and ends at 512.
All inputs are finite; a program needn't handle non-finite values.
Results may differ from the reference program's by a relative error of at most 0.02.
Values may be sent and summed in bfloat16 or wider, within the bound.
No kernel may reach another device: no remote copies, remote signals or barrier semaphores. Data moves between devices by JAX's collectives and lax.ppermute only.
A program may use at most 256 MiB of HBM per device.

```python
import math
from functools import partial
import jax
import jax.numpy as jnp
import numpy as np
from jax import lax

D = 1024
HEADS = 16
HEAD_DIM = 64
FF = 2816
EXPERTS = 8
TOPK = 2
SEQ_DEV = 1
LENGTH = 512
PIC = 256
TOK = 512
SEQS = 32
TOKENS = 16384
CAP = 160
N_GRP = 4
N_EP = 8


def draw_spans(key, part):
    key_length = jax.random.fold_in(key, 11)
    key_start = jax.random.fold_in(key, 12)
    seq_ids = jnp.arange(SEQS, dtype=jnp.int32)
    span_lengths = jax.random.randint(key_length, (SEQS,), PIC // 2, PIC + 1, dtype=jnp.int32)
    span_lengths = jnp.where(seq_ids == 0, PIC, span_lengths).astype(jnp.int32)
    span_lengths = jnp.where(seq_ids == 1, PIC // 2, span_lengths).astype(jnp.int32)
    span_starts = jax.random.randint(key_start, (SEQS,), 0, LENGTH - span_lengths + 1, dtype=jnp.int32)
    span_starts = jnp.where(seq_ids == 0, 0, span_starts).astype(jnp.int32)
    span_starts = jnp.where(seq_ids == 1, LENGTH - PIC // 2, span_starts).astype(jnp.int32)
    return jnp.stack([span_starts, span_lengths], axis=1).astype(jnp.int32)


def block_levels(own_key, shape, cuts, low, top_value):
    def one(axis_at, parts):
        heights = jax.random.uniform(jax.random.fold_in(jax.random.fold_in(own_key, 6), axis_at), (parts,), jnp.float32, low / len(cuts), top_value / len(cuts))
        return jnp.repeat(jnp.exp(heights), shape[axis_at] // parts).reshape((-1,) + (1,) * (len(shape) - axis_at - 1))

    loudness = one(*cuts[0])
    for cut in cuts[1:]:
        loudness = loudness * one(*cut)
    return loudness


def deal_out(rng, own, number, rows, count, top, limit, lean):
    sequence = jax.random.permutation(rng, count)
    packed, ordinary = shares(count, rows * top, limit, lean, True), shares(count, rows * top, limit, lean, False)
    places = jnp.arange(count)

    def named(tallies, rotation):
        used = int((tallies > 0).sum())
        fixed = max(1, used // 4)
        moved = fixed + (places - fixed + rotation * (used - fixed)) % max(1, count - fixed)
        return jnp.zeros((count,), jnp.int32).at[sequence[jnp.where(places < fixed, places, moved)]].set(jnp.asarray(tallies, jnp.int32))

    tallies = jnp.where(number % 4 == 0, named(packed, number // 4), named(ordinary, number - number // 4 - 1))
    mixed = jax.random.permutation(jax.random.fold_in(own, 3), count)
    giver, sink = mixed[0:count // 2 * 2:2], mixed[1:count // 2 * 2:2]
    slack = jnp.minimum(tallies[giver] - 1, limit - tallies[sink]) // 2
    slack = jnp.where((giver == sequence[0]) | (sink == sequence[0]) | (tallies[sink] == 0), 0, jnp.maximum(slack, 0))
    moved = jax.random.randint(jax.random.fold_in(own, 4), (count // 2,), 0, 1 << 20) % (slack + 1)
    tallies = tallies.at[giver].add(-moved).at[sink].add(moved)
    members = jnp.searchsorted(jnp.cumsum(tallies), jnp.arange(rows * top), side="right").astype(jnp.int32)
    table = members.reshape(top, rows).T
    table = table[jax.random.permutation(jax.random.fold_in(own, 1), rows)]
    rotation = jax.random.randint(jax.random.fold_in(own, 2), (rows, 1), 0, top)
    return jnp.take_along_axis(table, (jnp.arange(top)[None, :] + rotation) % top, axis=1)


def shares(amount, total, bound, lean, full):
    loads = [(1 << 20) // math.isqrt(rank ** lean) + 1 for rank in range(1, amount + 1)]
    largest = bound if full else min(bound, max(-(-total // amount), total * loads[0] // sum(loads)))
    least = 1 if total - largest >= amount - 1 else 0
    holding, surplus = [largest] + [least] * (amount - 1), total - largest - least * (amount - 1)
    while surplus > 0:
        candidates = [i for i in range(1, amount) if holding[i] < largest] or [i for i in range(1, amount) if holding[i] < bound]
        whole, remaining = sum([loads[i] for i in candidates]), surplus
        for i in candidates:
            extra = min(bound - holding[i], max(1, remaining * loads[i] // whole), surplus)
            holding[i] = holding[i] + extra
            surplus = surplus - extra
    return np.array(holding)


def gaussian(rng, extent, scale, most, pieces=(), held_as=jnp.bfloat16):
    result = scale * jax.random.normal(rng, extent, jnp.float32)
    if pieces:
        result = result * block_levels(rng, extent, pieces, -0.22, 0.18)
    return jnp.clip(result, -most, most).astype(held_as)


def setup_inputs(seed: int = 0) -> dict:
    key_list = jax.random.split(jax.random.key(seed), 12)
    tokens = gaussian(key_list[0], (TOKENS, D), 1.0, 6.0, ((0, 32),))
    cotangent = gaussian(key_list[1], (TOKENS, D), 1.0, 6.0, ((0, 32),))
    w_qkv = gaussian(key_list[2], (D, 3 * D), D ** -0.5, 0.1875)
    w_out_attn = gaussian(key_list[3], (D, D), (D // 64) ** -0.5, 1.5)
    rel_bias = gaussian(key_list[4], (HEADS, LENGTH, LENGTH), 0.5, 3.0)
    norm_gains = jnp.clip(1.0 + 0.18 * jax.random.normal(key_list[5], (2, D), jnp.float32), 0.1, 1.9)
    w_router = gaussian(key_list[6], (D, EXPERTS), (2 * D) ** -0.5, 0.125)
    w_gate_up = gaussian(key_list[7], (EXPERTS, D, 2 * FF), D ** -0.5, 0.1875, ((0, 8),))
    w_expert_out = gaussian(key_list[8], (EXPERTS, FF, D), (max(1, FF * 3 // (2 * EXPERTS * EXPERTS))) ** -0.5, 0.75, ((0, 8),))
    routes_keys = jax.random.split(jax.random.fold_in(key_list[9], 1), TOKENS // TOK)
    routes_turns = jax.random.permutation(jax.random.fold_in(key_list[9], 3), TOKENS // TOK)
    routes = jax.vmap(lambda own, number: deal_out(jax.random.fold_in(key_list[9], 2), own, number, TOK, EXPERTS, TOPK, CAP, 1))(routes_keys, routes_turns).reshape((TOKENS, TOPK))
    spans = draw_spans(jax.random.fold_in(key_list[11], 71), 0)
    return dict(tokens=tokens, cotangent=cotangent, w_qkv=w_qkv, w_out_attn=w_out_attn, rel_bias=rel_bias, norm_gains=norm_gains, w_router=w_router, w_gate_up=w_gate_up, w_expert_out=w_expert_out, routes=routes, spans=spans)


@jax.custom_vjp
def low(v):
    return lax.optimization_barrier(v.astype(jnp.bfloat16)).astype(jnp.float32)

@jax.custom_vjp
def low_back(v):
    return v

def low_keep(v):
    return (low(v), None)

def low_pass(kept, grad):
    return (grad,)

def back_keep(v):
    return (v, None)

def back_low(kept, grad):
    return (low(grad),)
low.defvjp(low_keep, low_pass)
low_back.defvjp(back_keep, back_low)
EPSILON = 1e-06
HIGHEST = lax.Precision.HIGHEST

def rms_scaled(values, norm_gain):
    return values * lax.rsqrt(lax.optimization_barrier(jnp.mean(values * values, axis=-1, keepdims=True)) + EPSILON) * norm_gain

def slot_positions(block_routes):
    flat_routes = block_routes.reshape(-1).astype(jnp.int32)
    expert_ids = jnp.arange(EXPERTS, dtype=jnp.int32)
    one_hot = (flat_routes[:, None] == expert_ids[None, :]).astype(jnp.int32)
    earlier = (jnp.cumsum(one_hot, axis=0).astype(jnp.int32) - one_hot).astype(jnp.int32)
    slot_counts = lax.optimization_barrier(jnp.sum(earlier * one_hot, axis=1)).astype(jnp.int32)
    return (flat_routes * CAP + slot_counts).astype(jnp.int32).reshape(block_routes.shape)

def allowed_mask(seq_span):
    query_index = lax.broadcasted_iota(jnp.int32, (LENGTH, LENGTH), 0)
    key_index = lax.broadcasted_iota(jnp.int32, (LENGTH, LENGTH), 1)
    span_start = seq_span[0].astype(jnp.int32)
    span_end = (seq_span[0] + seq_span[1]).astype(jnp.int32)
    inside = (query_index >= span_start) & (query_index < span_end) & (key_index >= span_start) & (key_index < span_end)
    return (key_index <= query_index) | inside

def attend_sequence(bias_table, seq_item):
    qkv_seq, seq_span = seq_item
    split_view = qkv_seq.reshape(LENGTH, 3, HEADS, HEAD_DIM)
    query_heads = split_view[:, 0]
    key_heads = split_view[:, 1]
    value_heads = split_view[:, 2]
    score_scale = 1.0 / math.sqrt(HEAD_DIM)
    raw_scores = jnp.einsum('qhd,khd->hqk', query_heads, key_heads, precision=HIGHEST) * score_scale + bias_table
    scores = jnp.where(allowed_mask(seq_span)[None], low_back(raw_scores), -1e+30)
    attn_probs = jax.nn.softmax(scores, axis=-1)
    mixed_heads = jnp.einsum('hqk,khd->qhd', low(attn_probs), value_heads, precision=HIGHEST)
    return mixed_heads.reshape(LENGTH, D)

def group_forward(weights, group_item):
    w_qkv, w_attn, bias_table, gains, w_route, w_gate, w_expert = weights
    hidden, group_routes, group_spans = group_item
    group_tokens = N_EP * TOK
    a_one = low(rms_scaled(hidden, gains[0]))
    qkv_rows = low_back(low(jnp.dot(a_one, w_qkv, precision=HIGHEST)))
    sequences = qkv_rows.reshape(N_EP * SEQ_DEV, LENGTH, 3 * D)
    mixed_heads = lax.map(jax.checkpoint(partial(attend_sequence, bias_table)), (sequences, group_spans))
    mixed_low = low_back(low(mixed_heads.reshape(group_tokens, D)))
    after_attn = hidden + low_back(jnp.dot(mixed_low, w_attn, precision=HIGHEST))
    a_two = low(rms_scaled(after_attn, gains[1]))
    logits = low_back(jnp.dot(a_two, w_route, precision=HIGHEST))
    router_probs = jax.nn.softmax(logits, axis=-1)
    position = jax.vmap(slot_positions)(group_routes.reshape(N_EP, TOK, TOPK))
    device_ids = jnp.arange(N_EP, dtype=jnp.int32)[:, None, None]
    token_ids = jnp.arange(TOK, dtype=jnp.int32)[None, :, None]
    flat_position = (device_ids * (EXPERTS * CAP) + position).astype(jnp.int32).reshape(-1)
    source_ids = jnp.broadcast_to(device_ids * TOK + token_ids, position.shape).astype(jnp.int32).reshape(-1)
    slot_total = N_EP * EXPERTS * CAP
    source_index = jnp.zeros((slot_total,), jnp.int32).at[flat_position].set(source_ids)
    filled = jnp.zeros((slot_total,), jnp.float32).at[flat_position].set(1.0)
    slot_rows = low_back(a_two[source_index] * filled[:, None])
    slot_rows = slot_rows.reshape(N_EP, EXPERTS, CAP, D).transpose(1, 0, 2, 3).reshape(EXPERTS, N_EP * CAP, D)
    gate_up = low_back(jnp.einsum('erd,edf->erf', slot_rows, w_gate, precision=HIGHEST))
    activation = low(jax.nn.gelu(gate_up[..., :FF]) * gate_up[..., FF:])
    expert_rows = low_back(low(jnp.einsum('erf,efd->erd', activation, w_expert, precision=HIGHEST)))
    expert_rows = expert_rows.reshape(EXPERTS, N_EP, CAP, D).transpose(1, 0, 2, 3).reshape(slot_total, D)
    picked = expert_rows[flat_position].reshape(group_tokens, TOPK, D)
    route_gates = jnp.take_along_axis(router_probs, group_routes, axis=1)
    return after_attn + lax.optimization_barrier(jnp.sum(route_gates[:, :, None] * picked, axis=1))

def reference(tokens, cotangent, w_qkv, w_out_attn, rel_bias, norm_gains, w_router, w_gate_up, w_expert_out, routes, spans):
    primals = (tokens.astype(jnp.float32), w_qkv.astype(jnp.float32), w_out_attn.astype(jnp.float32), rel_bias.astype(jnp.float32), norm_gains.astype(jnp.float32), w_router.astype(jnp.float32), w_gate_up.astype(jnp.float32), w_expert_out.astype(jnp.float32))

    def forward(hidden, w_qkv_f, w_attn_f, bias_f, gains_f, w_route_f, w_gate_f, w_expert_f):
        weights = (w_qkv_f, w_attn_f, bias_f, gains_f, w_route_f, w_gate_f, w_expert_f)
        grouped_tokens = hidden.reshape(N_GRP, N_EP * TOK, D)
        grouped_routes = routes.reshape(N_GRP, N_EP * TOK, TOPK)
        grouped_spans = spans.reshape(N_GRP, N_EP * SEQ_DEV, 2)
        result_rows = lax.map(jax.checkpoint(partial(group_forward, weights)), (grouped_tokens, grouped_routes, grouped_spans))
        return result_rows.reshape(TOKENS, D)
    result_rows, pullback = jax.vjp(forward, *primals)
    gradients = pullback(cotangent.astype(jnp.float32))
    return (result_rows, gradients[0], gradients[1], gradients[2], gradients[3], gradients[4], gradients[5], gradients[6], gradients[7])
```

```python
import functools
import math

import jax
import jax.numpy as jnp
from jax import lax
from jax.experimental import pallas as pl
from jax.experimental.pallas import tpu as pltpu
from jax.sharding import PartitionSpec as P

HEADS = 16
LENGTH = 512
EPSILON = 1e-06
LANES = 128
GELU_C = math.sqrt(2.0 / math.pi)
GELU_A = 0.044715
F32 = jnp.float32
BF16 = jnp.bfloat16
VMEM_LIMIT = 60 * 1024 * 1024


def params(**kw):
    return pltpu.CompilerParams(vmem_limit_bytes=VMEM_LIMIT, **kw)


def cost(flops, nbytes, trans=0):
    return pl.CostEstimate(flops=int(flops), bytes_accessed=int(nbytes), transcendentals=int(trans))


def dot_f32(a, b, dims):
    return lax.dot_general(a, b, (dims, ((), ())), preferred_element_type=F32)


NN = ((1,), (0,))
NT = ((1,), (1,))
TN = ((0,), (0,))


def xor_send(v, axis, k):
    n = lax.axis_size(axis)
    return lax.ppermute(v, axis, [(i, i ^ k) for i in range(n)])


def halving_steps(n_g, n_e):
    g_bits = [("grp", 1 << i) for i in range(n_g.bit_length() - 1)]
    e_bits = [("ep", 1 << i) for i in range(n_e.bit_length() - 1)]
    steps = g_bits[:1]
    rest_g, rest_e = g_bits[1:], e_bits
    while rest_g or rest_e:
        steps += rest_e[:1] + rest_g[:1]
        rest_e, rest_g = rest_e[1:], rest_g[1:]
    return steps


def halve(keep, send, steps):
    total = None
    for i, (axis, k) in enumerate(steps):
        got = xor_send(send, axis, k)
        total = keep.astype(F32) + got.astype(F32)
        if i + 1 < len(steps):
            low = total.astype(BF16)
            keep, send = low[0], low[1]
    return total


def butterfly(v, n_g, n_e):
    for axis, k in halving_steps(n_g, n_e):
        v = v + xor_send(v, axis, k)
    return v


def split_steps(steps, blocks, n_g, n_e):
    def build(i, r_g, r_e):
        if i == len(steps):
            return blocks[(r_g, r_e)]
        axis, k = steps[i]
        parts = []
        for b in (0, 1):
            parts.append(
                build(i + 1, r_g | (k * b if axis == "grp" else 0), r_e | (k * b if axis == "ep" else 0))
            )
        return jnp.stack(parts)

    axis, k = steps[0]
    keep = build(1, 0, 0)
    send = build(1, k if axis == "grp" else 0, k if axis == "ep" else 0)
    return keep, send


def dispatch_kernel(cap, pos_ref, v_ref, *outs):
    tok = v_ref.shape[0]
    first = pos_ref[0:1, :]
    second = pos_ref[1:2, :]
    rows = lax.broadcasted_iota(jnp.int32, (cap, tok), 0)
    for k, out in enumerate(outs):
        here = rows + k * cap
        pick = jnp.where((here == first) | (here == second), 1.0, 0.0).astype(BF16)
        out[...] = dot_f32(pick, v_ref[...], NN).astype(BF16)


def dispatch(pos_rows, values, cap, n_e):
    tok, width = values.shape
    return pl.pallas_call(
        functools.partial(dispatch_kernel, cap),
        out_shape=[jax.ShapeDtypeStruct((cap, width), BF16)] * n_e,
        compiler_params=params(),
        cost_estimate=cost(2 * n_e * cap * tok * width, 2 * tok * width + 2 * n_e * cap * width),
        name="dispatch_rows",
    )(pos_rows, values)


def gathered(pos_ref, parts, cap):
    first = pos_ref[:, 0:1]
    second = pos_ref[:, 1:2]
    lanes = lax.broadcasted_iota(jnp.int32, (pos_ref.shape[0], cap), 1)
    total = None
    for k, part in enumerate(parts):
        here = lanes + k * cap
        pick = jnp.where((here == first) | (here == second), 1.0, 0.0).astype(BF16)
        term = dot_f32(pick, part[...], NN)
        total = term if total is None else total + term
    return total


def combine_kernel(cap, pos_ref, x_ref, *refs):
    parts, out_ref = refs[:-1], refs[-1]
    out_ref[...] = x_ref[...] + gathered(pos_ref, parts, cap)


def combine(pos_cols, after_attn, parts, cap):
    tok, width = after_attn.shape
    blk = 256
    return pl.pallas_call(
        functools.partial(combine_kernel, cap),
        grid=(tok // blk,),
        in_specs=[
            pl.BlockSpec((blk, 2), lambda i: (i, 0)),
            pl.BlockSpec((blk, width), lambda i: (i, 0)),
        ]
        + [pl.BlockSpec((cap, width), lambda i: (0, 0))] * len(parts),
        out_specs=pl.BlockSpec((blk, width), lambda i: (i, 0)),
        out_shape=jax.ShapeDtypeStruct((tok, width), F32),
        compiler_params=params(),
        cost_estimate=cost(2 * tok * cap * len(parts) * width, 10 * tok * width),
        name="combine_rows",
    )(pos_cols, after_attn, *parts)


def return_kernel(cap, pos_ref, x_ref, cot_ref, gain_ref, *refs):
    parts, (dx_ref, low_ref, gg_ref) = refs[:-3], refs[-3:]
    grad = gathered(pos_ref, parts, cap)
    x = x_ref[...]
    inverse = lax.rsqrt(jnp.mean(x * x, axis=-1, keepdims=True) + EPSILON)
    normed = x * inverse
    grad_normed = grad * gain_ref[...]
    dx = cot_ref[...].astype(F32) + inverse * (
        grad_normed - normed * jnp.mean(grad_normed * normed, axis=-1, keepdims=True)
    )
    dx_ref[...] = dx
    low_ref[...] = dx.astype(BF16)

    @pl.when(pl.program_id(0) == 0)
    def _():
        gg_ref[...] = jnp.zeros_like(gg_ref)

    gg_ref[...] += jnp.sum(grad * normed, axis=0, keepdims=True)


def return_grads(pos_cols, after_attn, cotangent, gain, parts, cap):
    tok, width = after_attn.shape
    blk = 256
    row = pl.BlockSpec((blk, width), lambda i: (i, 0))
    one = pl.BlockSpec((1, width), lambda i: (0, 0))
    return pl.pallas_call(
        functools.partial(return_kernel, cap),
        grid=(tok // blk,),
        in_specs=[pl.BlockSpec((blk, 2), lambda i: (i, 0)), row, row, one]
        + [pl.BlockSpec((cap, width), lambda i: (0, 0))] * len(parts),
        out_specs=[row, row, one],
        out_shape=[
            jax.ShapeDtypeStruct((tok, width), F32),
            jax.ShapeDtypeStruct((tok, width), BF16),
            jax.ShapeDtypeStruct((1, width), F32),
        ],
        compiler_params=params(),
        cost_estimate=cost(2 * tok * cap * len(parts) * width, 16 * tok * width),
        name="return_rows",
    )(pos_cols, after_attn, cotangent, gain, *parts)


def expert_kernel(cap, n_blk, experts, aliased, *refs):
    me_ref, x_ref, d_ref, wg_ref, wu_ref, wr_ref, wrt_ref = refs[:7]
    refs = refs[7 + (3 if aliased else 0) :]
    act_ref, dg_ref, du_ref, dl_ref, p_ref = refs[:5]
    outs = refs[5 : 5 + n_blk]
    acc_ref, gate_ref, prob_ref = refs[5 + n_blk :]
    j = pl.program_id(0)
    rows_all = x_ref.shape[0]
    lane = lax.broadcasted_iota(jnp.int32, (rows_all, LANES), 1)

    @pl.when(j == 0)
    def _():
        logits = dot_f32(x_ref[...], wr_ref[...], NN)
        logits = jnp.where(lane < experts, logits, -1e30)
        exps = jnp.exp(logits - jnp.max(logits, axis=-1, keepdims=True))
        probs = exps / jnp.sum(exps, axis=-1, keepdims=True)
        prob_ref[...] = probs
        own = jnp.sum(jnp.where(lane == me_ref[0], probs, 0.0), axis=-1, keepdims=True)
        p_ref[...] = jnp.broadcast_to(own, p_ref.shape)
        acc_ref[...] = jnp.zeros_like(acc_ref)
        gate_ref[...] = jnp.zeros_like(gate_ref)

    for b in range(n_blk):
        rows = slice(b * cap, (b + 1) * cap)
        x = x_ref[rows, :]
        z = dot_f32(x, wg_ref[...], NN)
        up = dot_f32(x, wu_ref[...], NN)
        back = d_ref[rows, :].astype(F32)
        reps = z.shape[1] // LANES
        own = jnp.concatenate([p_ref[rows, :]] * reps, axis=1)
        zz = z * z
        th = jnp.tanh(GELU_C * z * (1.0 + GELU_A * zz))
        half = 0.5 + 0.5 * th
        gelu = z * half
        slope = half + 0.5 * GELU_C * z * (1.0 - th * th) * (1.0 + 3.0 * GELU_A * zz)
        act = (gelu * up).astype(BF16)
        act_ref[rows, :] = act
        share = act.astype(F32) * back
        gate_ref[rows, :] += sum(share[:, i * LANES : (i + 1) * LANES] for i in range(reps))
        dact = back * own
        dg = (dact * up * slope).astype(BF16)
        du = (dact * gelu).astype(BF16)
        dg_ref[rows, :] = dg
        du_ref[rows, :] = du
        acc_ref[rows, :] += dot_f32(dg, wg_ref[...], NT) + dot_f32(du, wu_ref[...], NT)

    @pl.when(j == pl.num_programs(0) - 1)
    def _():
        dgate = jnp.sum(gate_ref[...], axis=-1, keepdims=True)
        dl = dgate * p_ref[...] * (jnp.where(lane == me_ref[0], 1.0, 0.0) - prob_ref[...])
        dl = dl.astype(BF16)
        dl_ref[...] = dl
        total = acc_ref[...] + dot_f32(dl, wrt_ref[...], NN)
        for b, out in enumerate(outs):
            out[...] = total[b * cap : (b + 1) * cap, :].astype(BF16)


def expert_chunk(me, rows, dact, w_gate_up, wr_pad, wr_pad_t, experts, cap, start, total_rows, earlier):
    ff = dact.shape[1]
    tile = 256
    steps = ff // tile
    n_rows, width = rows.shape
    n_blk = n_rows // cap
    at = start // n_rows
    whole = pl.BlockSpec(memory_space=pl.ANY)
    part = pl.BlockSpec((n_rows, tile), lambda j, m: (at, j))
    wide = pl.BlockSpec((n_rows, LANES), lambda j, m: (0, 0))
    aliased = earlier is not None
    call = pl.pallas_call(
        functools.partial(expert_kernel, cap, n_blk, experts, aliased),
        grid_spec=pltpu.PrefetchScalarGridSpec(
            num_scalar_prefetch=1,
            grid=(steps,),
            in_specs=[
                pl.BlockSpec((n_rows, width), lambda j, m: (0, 0)),
                part,
                pl.BlockSpec((width, tile), lambda j, m: (0, j)),
                pl.BlockSpec((width, tile), lambda j, m: (0, j + steps)),
                pl.BlockSpec((width, LANES), lambda j, m: (0, 0)),
                pl.BlockSpec((LANES, width), lambda j, m: (0, 0)),
            ]
            + ([whole] * 3 if aliased else []),
            out_specs=[part, part, part, wide, wide]
            + [pl.BlockSpec((cap, width), lambda j, m: (0, 0))] * n_blk,
            scratch_shapes=[
                pltpu.VMEM((n_rows, width), F32),
                pltpu.VMEM((n_rows, LANES), F32),
                pltpu.VMEM((n_rows, LANES), F32),
            ],
        ),
        out_shape=[jax.ShapeDtypeStruct((total_rows, ff), BF16)] * 3
        + [
            jax.ShapeDtypeStruct((n_rows, LANES), BF16),
            jax.ShapeDtypeStruct((n_rows, LANES), F32),
        ]
        + [jax.ShapeDtypeStruct((cap, width), BF16)] * n_blk,
        input_output_aliases={7: 0, 8: 1, 9: 2} if aliased else {},
        compiler_params=params(),
        cost_estimate=cost(
            8 * n_rows * width * ff, 4 * width * ff + 10 * n_rows * ff + 4 * n_rows * width, n_rows * ff
        ),
        name="expert_rows",
    )
    args = (me, rows, dact, w_gate_up, w_gate_up, wr_pad, wr_pad_t)
    out = call(*args, *(earlier if aliased else ()))
    return out[:3], out[3], out[4], out[5:]


def relative(v, axis, me, n):
    return jnp.stack([lax.dynamic_index_in_dim(v, me ^ r, axis, keepdims=False) for r in range(n)], axis)


def blocks_of(full, n_g, n_e, me_g, me_e):
    rows, cols = full.shape
    view = full.reshape(n_g, rows // n_g, n_e, cols // n_e)
    out = {}
    for r_g in range(n_g):
        one = lax.dynamic_index_in_dim(view, me_g ^ r_g, 0, keepdims=False)
        for r_e in range(n_e):
            out[(r_g, r_e)] = lax.dynamic_index_in_dim(one, me_e ^ r_e, 1, keepdims=False)
    return out


def wgrad_kernel(n_g, steps, me_ref, a_ref, b_ref, keep_ref, send_ref, full_ref):
    full_ref[...] = dot_f32(a_ref[...], b_ref[...], TN)
    rows = full_ref.shape[0] // n_g
    for r_g in range(n_g):
        at = pl.multiple_of((me_ref[0] ^ r_g) * rows, rows)
        where = tuple(
            (1 if r_g & k else 0) if axis == "grp" else 0 for axis, k in steps[1:]
        )
        out = send_ref if r_g & 1 else keep_ref
        out[where] = full_ref[pl.ds(at, rows), :].astype(BF16)


def wgrad(me, a, b, n_g, n_e, steps):
    tok, m = a.shape
    n = b.shape[1]
    if (n // n_e) % LANES or n_e == 1:
        full = dot_f32(a, b, TN).astype(BF16)
        return split_steps(steps, blocks_of(full, n_g, n_e, me[0], me[1]), n_g, n_e)
    rows, cols = m // n_g, n // n_e
    lead = tuple(2 for _ in steps[1:])
    block = tuple(2 if axis == "grp" else 1 for axis, _ in steps[1:]) + (rows, cols)

    def out_index(r, me_ref):
        return tuple(
            (1 - (r & k == 0)) if axis == "grp" and False else (0 if axis == "grp" else (r // k) % 2)
            for axis, k in steps[1:]
        ) + (0, 0)

    spec = pl.BlockSpec(block, out_index)
    return pl.pallas_call(
        functools.partial(wgrad_kernel, n_g, steps),
        grid_spec=pltpu.PrefetchScalarGridSpec(
            num_scalar_prefetch=1,
            grid=(n_e,),
            in_specs=[
                pl.BlockSpec((tok, m), lambda r, me_ref: (0, 0)),
                pl.BlockSpec((tok, cols), lambda r, me_ref: (0, me_ref[1] ^ r)),
            ],
            out_specs=[spec, spec],
            scratch_shapes=[pltpu.VMEM((m, cols), F32)],
        ),
        out_shape=[jax.ShapeDtypeStruct(lead + (rows, cols), BF16)] * 2,
        compiler_params=params(),
        cost_estimate=cost(2 * tok * m * n, 2 * tok * (m + n) + 2 * m * n),
        name="weight_grad",
    )(me, a, b)


def gate_up_kernel(n_g, half, me_ref, a_ref, g_ref, u_ref, keep_ref, send_ref, full_ref):
    j = pl.program_id(0)

    @pl.when(j < half)
    def _():
        full_ref[...] = dot_f32(a_ref[...], g_ref[...], TN)

    @pl.when(j >= half)
    def _():
        full_ref[...] = dot_f32(a_ref[...], u_ref[...], TN)

    rows = full_ref.shape[0] // n_g
    for r_g in range(n_g):
        at = pl.multiple_of((me_ref[0] ^ r_g) * rows, rows)
        out = send_ref if r_g & 1 else keep_ref
        out[r_g // 2] = full_ref[pl.ds(at, rows), :].astype(BF16)


def gate_up_grad(me, rows, dg, du, n_g):
    total, width = rows.shape
    ff = dg.shape[1]
    tile = 256
    half = ff // tile
    spec = pl.BlockSpec((n_g // 2, width // n_g, tile), lambda j, m: (0, 0, j))
    return pl.pallas_call(
        functools.partial(gate_up_kernel, n_g, half),
        grid_spec=pltpu.PrefetchScalarGridSpec(
            num_scalar_prefetch=1,
            grid=(2 * half,),
            in_specs=[
                pl.BlockSpec((total, width), lambda j, m: (0, 0)),
                pl.BlockSpec((total, tile), lambda j, m: (0, jnp.minimum(j, half - 1))),
                pl.BlockSpec((total, tile), lambda j, m: (0, jnp.maximum(j - half, 0))),
            ],
            out_specs=[spec, spec],
            scratch_shapes=[pltpu.VMEM((width, tile), F32)],
        ),
        out_shape=[jax.ShapeDtypeStruct((n_g // 2, width // n_g, 2 * ff), BF16)] * 2,
        compiler_params=params(),
        cost_estimate=cost(4 * total * width * ff, 2 * total * (width + 2 * ff) + 4 * width * ff),
        name="gate_up_grad",
    )(me, rows, dg, du)


def halve_groups(keep, send, n_g):
    bits = [1 << i for i in range(n_g.bit_length() - 1)]
    got = xor_send(send, "grp", bits[0])
    total = keep.astype(F32) + got.astype(F32)
    for k in bits[:0:-1]:
        low = total.astype(BF16)
        half = low.shape[0] // 2
        got = xor_send(low[half:], "grp", k)
        total = low[:half].astype(F32) + got.astype(F32)
    return total[0]


def allowed_mask(seq_span):
    query_index = lax.broadcasted_iota(jnp.int32, (LENGTH, LENGTH), 0)
    key_index = lax.broadcasted_iota(jnp.int32, (LENGTH, LENGTH), 1)
    span_end = seq_span[0] + seq_span[1]
    inside = (
        (query_index >= seq_span[0])
        & (query_index < span_end)
        & (key_index >= seq_span[0])
        & (key_index < span_end)
    )
    return (key_index <= query_index) | inside


def split_heads(qkv_seq):
    split_view = qkv_seq.reshape(qkv_seq.shape[0], 3, HEADS, qkv_seq.shape[1] // (3 * HEADS))
    return (split_view[:, 0], split_view[:, 1], split_view[:, 2])


def scores_of(query_heads, key_heads, rel_bias, seq_span, score_scale):
    raw_scores = (
        jnp.einsum("qhd,khd->hqk", query_heads, key_heads, preferred_element_type=F32) * score_scale
        + rel_bias
    )
    return jnp.where(allowed_mask(seq_span)[None], raw_scores, -1e30)


def attention_forward(qkv_seq, seq_span, rel_bias, score_scale):
    query_heads, key_heads, value_heads = split_heads(qkv_seq)
    scores = scores_of(query_heads, key_heads, rel_bias, seq_span, score_scale)
    row_max = jnp.max(scores, axis=-1, keepdims=True)
    exp_scores = jnp.exp(scores - row_max)
    row_total = jnp.sum(exp_scores, axis=-1, keepdims=True)
    attn_probs = (exp_scores / row_total).astype(BF16)
    mixed_heads = jnp.einsum("hqk,khd->qhd", attn_probs, value_heads, preferred_element_type=F32)
    return (
        mixed_heads.reshape(LENGTH, -1).astype(BF16),
        row_max[..., 0] + jnp.log(row_total[..., 0]),
    )


def attention_backward(qkv_seq, grad_seq, seq_span, seq_total, rel_bias, score_scale):
    query_heads, key_heads, value_heads = split_heads(qkv_seq)
    grad_heads = grad_seq.reshape(LENGTH, HEADS, -1)
    scores = scores_of(query_heads, key_heads, rel_bias, seq_span, score_scale)
    attn_probs = jnp.exp(scores - seq_total[..., None])
    probs_low = attn_probs.astype(BF16)
    grad_value = jnp.einsum(
        "hqk,qhd->khd", probs_low, grad_heads, preferred_element_type=F32
    ).astype(BF16)
    grad_probs = jnp.einsum("qhd,khd->hqk", grad_heads, value_heads, preferred_element_type=F32)
    grad_scores = attn_probs * (
        grad_probs - jnp.sum(attn_probs * grad_probs, axis=-1, keepdims=True)
    )
    grad_low = grad_scores.astype(BF16)
    grad_query = (
        jnp.einsum("hqk,khd->qhd", grad_low, key_heads, preferred_element_type=F32) * score_scale
    ).astype(BF16)
    grad_key = (
        jnp.einsum("hqk,qhd->khd", grad_low, query_heads, preferred_element_type=F32) * score_scale
    ).astype(BF16)
    joined = jnp.stack([grad_query, grad_key, grad_value], axis=1).reshape(LENGTH, -1)
    return (grad_low, joined)


def norm_forward(values):
    inverse = lax.rsqrt(jnp.mean(values * values, axis=-1, keepdims=True) + EPSILON)
    return (values * inverse, inverse)


def norm_backward(grad_out, normed, inverse, norm_gain):
    grad_normed = grad_out * norm_gain
    grad_gain = jnp.sum(grad_out * normed, axis=0)
    grad_input = inverse * (
        grad_normed - normed * jnp.mean(grad_normed * normed, axis=-1, keepdims=True)
    )
    return (grad_input, grad_gain)


def body(
    tokens,
    cotangent,
    w_qkv,
    w_out_attn,
    rel_bias,
    norm_gains,
    w_router,
    w_gate_up,
    w_expert_out,
    routes,
    spans,
):
    tok, width = tokens.shape
    n_g, n_e = lax.axis_size("grp"), lax.axis_size("ep")
    assert w_gate_up.shape[0] == 1 and spans.shape[0] == 1 and tok == LENGTH
    assert n_g & (n_g - 1) == 0 and n_e & (n_e - 1) == 0 and n_g > 1 and n_e > 3
    experts = n_e
    ff = w_expert_out.shape[1]
    cap = 5 * routes.shape[1] * tok // (4 * experts)
    slots = experts * cap
    score_scale = 1.0 / math.sqrt(width // HEADS)
    me_g, me_e = lax.axis_index("grp"), lax.axis_index("ep")
    me = jnp.stack([me_g, me_e]).astype(jnp.int32)
    steps = halving_steps(n_g, n_e)
    w_gu, w_eo = w_gate_up[0], w_expert_out[0]

    flipped = (routes ^ me_e).T
    ids = lax.broadcasted_iota(jnp.int32, (experts, tok), 0)
    named = [ids == flipped[k : k + 1] for k in range(2)]
    counts = (named[0] | named[1]).astype(BF16)
    before = lax.broadcasted_iota(jnp.int32, (tok, tok), 0) < lax.broadcasted_iota(
        jnp.int32, (tok, tok), 1
    )
    earlier = dot_f32(counts, before.astype(BF16), NN)
    pos_rows = jnp.stack(
        [
            jnp.sum(jnp.where(one, earlier, 0.0), axis=0).astype(jnp.int32) + flipped[k] * cap
            for k, one in enumerate(named)
        ]
    )
    pos_cols = pos_rows.T

    cot_parts = dispatch(pos_rows, cotangent, cap, n_e)
    cot_rows = jnp.concatenate(
        [cot_parts[0]] + [xor_send(cot_parts[k], "ep", k) for k in range(1, n_e)]
    )

    hidden = tokens.astype(F32)
    normed_one, inverse_one = norm_forward(hidden)
    a_one = (normed_one * norm_gains[0]).astype(BF16)
    qkv_rows = dot_f32(a_one, w_qkv, NN).astype(BF16)
    mixed_heads, log_total = attention_forward(qkv_rows, spans[0], rel_bias, score_scale)
    after_attn = hidden + dot_f32(mixed_heads, w_out_attn, NN)
    normed_two, _ = norm_forward(after_attn)
    a_two = (normed_two * norm_gains[1]).astype(BF16)

    parts = dispatch(pos_rows, a_two, cap, n_e)
    parts = [parts[0]] + [xor_send(parts[k], "ep", k) for k in range(1, n_e)]
    dact = dot_f32(cot_rows, w_eo, NT)
    wr_pad = jnp.pad(w_router, ((0, 0), (0, LANES - experts)))
    wr_pad_t = wr_pad.T
    state, dls, owns, back = None, [], [], []
    for lo, hi in ((0, n_e // 2), (n_e // 2, 3 * n_e // 4), (3 * n_e // 4, n_e)):
        state, dl, own, outs = expert_chunk(
            me[1:], jnp.concatenate(parts[lo:hi]), dact, w_gu, wr_pad, wr_pad_t, experts, cap, lo * cap, slots, state
        )
        dls.append(dl)
        owns.append(own)
        for k in range(lo, hi):
            back.append(outs[k - lo] if k == 0 else xor_send(outs[k - lo], "ep", k))
    act, dg, du = state
    rows = jnp.concatenate(parts)
    own = jnp.concatenate(owns)[:, :1]
    grad_route = dot_f32(rows, jnp.concatenate(dls), TN)[:, :experts]

    gated = (dot_f32(act, w_eo, NN) * own).astype(BF16).reshape(n_e, cap, width)
    gated = [gated[0]] + [xor_send(gated[k], "ep", k) for k in range(1, n_e)]
    deo = (cot_rows.astype(F32) * own).astype(BF16)
    grad_eo = dot_f32(act, deo, TN).astype(BF16)
    grad_eo = grad_eo.reshape(n_g, ff // n_g, width)
    grad_eo = [lax.dynamic_index_in_dim(grad_eo, me_g ^ r, 0, keepdims=False) for r in range(n_g)]
    grad_w_expert = halve_groups(jnp.stack(grad_eo[0::2]), jnp.stack(grad_eo[1::2]), n_g)[None]
    grad_w_gate = halve_groups(*gate_up_grad(me[:1], rows, dg, du, n_g), n_g)[None]

    grad_after, grad_attn_low, grad_gain_two = return_grads(
        pos_cols, after_attn, cotangent, norm_gains[1:], back, cap
    )
    output = combine(pos_cols, after_attn, gated, cap)
    g_attn = wgrad(me, mixed_heads, grad_attn_low, n_g, n_e, steps)
    grad_mixed = dot_f32(grad_attn_low, w_out_attn, NT).astype(BF16)
    grad_bias, grad_qkv = attention_backward(
        qkv_rows, grad_mixed, spans[0], log_total, rel_bias, score_scale
    )
    hpe, rpg = HEADS // n_e, LENGTH // n_g
    bias_view = grad_bias.reshape(n_e, hpe, n_g, rpg, LENGTH)
    bias_view = relative(relative(bias_view, 0, me_e, n_e), 2, me_g, n_g)
    bias_blocks = {
        (r_g, r_e): bias_view[r_e, :, r_g] for r_g in range(n_g) for r_e in range(n_e)
    }
    g_bias = split_steps(steps, bias_blocks, n_g, n_e)
    g_qkv = wgrad(me, a_one, grad_qkv, n_g, n_e, steps)
    grad_a_one = dot_f32(grad_qkv, w_qkv, NT)
    grad_norm_one, grad_gain_one = norm_backward(grad_a_one, normed_one, inverse_one, norm_gains[0])
    grad_tokens = grad_after + grad_norm_one
    early = butterfly(jnp.concatenate([grad_gain_two, grad_route.T]), n_g, n_e)
    late = butterfly(grad_gain_one[None], n_g, n_e)
    return (
        output,
        grad_tokens,
        halve(*g_qkv, steps),
        halve(*g_attn, steps),
        halve(*g_bias, steps),
        jnp.concatenate([late, early[:1]]),
        early[1:].T,
        grad_w_gate,
        grad_w_expert,
    )


def solution(mesh):
    placed = (
        P(("grp", "ep"), None),
        P(("grp", "ep"), None),
        P(),
        P(),
        P(),
        P(),
        P(),
        P("ep", None, None),
        P("ep", None, None),
        P(("grp", "ep"), None),
        P(("grp", "ep"), None),
    )
    return jax.shard_map(
        body,
        mesh=mesh,
        in_specs=placed,
        out_specs=(
            P(("grp", "ep"), None),
            P(("grp", "ep"), None),
            P("grp", "ep"),
            P("grp", "ep"),
            P("ep", "grp", None),
            P(),
            P(),
            P("ep", "grp", None),
            P("ep", "grp", None),
        ),
        check_vma=False,
    )
```

```python
import functools
import math

import jax
import jax.numpy as jnp
from jax import lax
from jax.experimental import pallas as pl
from jax.experimental.pallas import tpu as pltpu
from jax.sharding import PartitionSpec as P

HEADS = 16
LENGTH = 512
EPSILON = 1e-06
LANES = 128
GELU_C = math.sqrt(2.0 / math.pi)
GELU_A = 0.044715
F32 = jnp.float32
BF16 = jnp.bfloat16
VMEM_LIMIT = 60 * 1024 * 1024


def params(**kw):
    return pltpu.CompilerParams(vmem_limit_bytes=VMEM_LIMIT, **kw)


def cost(flops, nbytes, trans=0):
    return pl.CostEstimate(flops=int(flops), bytes_accessed=int(nbytes), transcendentals=int(trans))


def dot_f32(a, b, dims):
    return lax.dot_general(a, b, (dims, ((), ())), preferred_element_type=F32)


NN = ((1,), (0,))
NT = ((1,), (1,))
TN = ((0,), (0,))


def xor_send(v, axis, k):
    n = lax.axis_size(axis)
    return lax.ppermute(v, axis, [(i, i ^ k) for i in range(n)])


def swap_rows(v):
    return lax.all_to_all(v, "ep", split_axis=0, concat_axis=0, tiled=True)


def bits_of(n):
    return [1 << i for i in range(n.bit_length() - 1)]


def total_of(terms):
    return sum(t.astype(F32) for t in terms)


def after(value, *others):
    return lax.optimization_barrier((value, *others))[0]


def next_send(way):
    terms, order, names = way
    at = names.index(order[0])
    return total_of([lax.index_in_dim(t, 1, at, keepdims=False) for t in terms]).astype(BF16)


def exchange(way, send):
    terms, order, names = way
    at = names.index(order[0])
    got = xor_send(send, *order[0])
    kept = [lax.index_in_dim(t, 0, at, keepdims=False) for t in terms]
    return kept + [got], order[1:], names[:at] + names[at + 1 :]


def finish(way):
    while way[1]:
        way = exchange(way, next_send(way))
    return total_of(way[0])


def three_ways(keep, got, n_g, n_e):
    g_bits = [("grp", k) for k in bits_of(n_g)]
    e_bits = [("ep", k) for k in bits_of(n_e)]
    names = e_bits[::-1] + g_bits[:0:-1]
    rest, first, others = g_bits[1:], e_bits[:1], e_bits[1:]
    orders = [first + rest + others, others + first + rest, rest + first + others]
    rows, cols = keep.shape[2:]
    cuts = [0, 3 * rows // 8, 5 * rows // 8, rows]
    view = (2,) * len(names) + (rows, cols)
    both = [keep.reshape(view), got.reshape(view)]
    return [
        ([t[..., cuts[i] : cuts[i + 1], :] for t in both], order, names)
        for i, order in enumerate(orders)
    ]


def group_way(keep, got, n_g):
    g_bits = [("grp", k) for k in bits_of(n_g)]
    names = g_bits[:0:-1]
    view = (2,) * len(names) + keep.shape[1:]
    return [keep.reshape(view), got.reshape(view)], g_bits[1:], names


def place_kernel(experts, cap, chunks, routes_ref, v_ref, pos_ref, out_ref):
    tok = v_ref.shape[0]
    short = cap // chunks
    ids = lax.broadcasted_iota(jnp.int32, (LANES, tok), 0)
    named = [ids == routes_ref[k : k + 1, :] for k in range(2)]
    counts = jnp.where(named[0] | named[1], 1.0, 0.0).astype(BF16)
    before = lax.broadcasted_iota(jnp.int32, (tok, tok), 0) < lax.broadcasted_iota(
        jnp.int32, (tok, tok), 1
    )
    earlier = dot_f32(counts, jnp.where(before, 1.0, 0.0).astype(BF16), NN)
    for k in range(2):
        slot = jnp.sum(jnp.where(named[k], earlier, 0.0), axis=0, keepdims=True).astype(jnp.int32)
        owner = routes_ref[k : k + 1, :]
        pos_ref[k : k + 1, :] = owner * cap + slot
        chunk = jnp.zeros_like(slot)
        for c in range(1, chunks):
            chunk += jnp.where(slot >= c * short, 1, 0)
        pos_ref[2 + k : 3 + k, :] = chunk * (experts * short) + owner * short + slot - chunk * short
    first, second = pos_ref[0:1, :], pos_ref[1:2, :]
    rows = lax.broadcasted_iota(jnp.int32, (cap, tok), 0)
    for e in range(experts):
        here = rows + e * cap
        pick = jnp.where((here == first) | (here == second), 1.0, 0.0).astype(BF16)
        out_ref[e * cap : (e + 1) * cap, :] = dot_f32(pick, v_ref[...], NN).astype(BF16)


def place(routes_t, values, experts, cap, chunks):
    tok, width = values.shape
    return pl.pallas_call(
        functools.partial(place_kernel, experts, cap, chunks),
        out_shape=[
            jax.ShapeDtypeStruct((4, tok), jnp.int32),
            jax.ShapeDtypeStruct((experts * cap, width), BF16),
        ],
        compiler_params=params(),
        cost_estimate=cost(2 * experts * cap * tok * width, 2 * tok * width + 2 * experts * cap * width),
        name="place_rows",
    )(routes_t, values)


def dispatch_kernel(pos_ref, v_ref, *outs):
    tok = v_ref.shape[0]
    first, second = pos_ref[2:3, :], pos_ref[3:4, :]
    at = 0
    for out in outs:
        total = out.shape[0]
        step = total // 4
        rows = lax.broadcasted_iota(jnp.int32, (step, tok), 0)
        for b in range(4):
            here = rows + at
            pick = jnp.where((here == first) | (here == second), 1.0, 0.0).astype(BF16)
            out[b * step : (b + 1) * step, :] = dot_f32(pick, v_ref[...], NN).astype(BF16)
            at += step


def dispatch(pos, values, slots, chunks):
    tok, width = values.shape
    return pl.pallas_call(
        dispatch_kernel,
        out_shape=[jax.ShapeDtypeStruct((slots // chunks, width), BF16)] * chunks,
        compiler_params=params(),
        cost_estimate=cost(2 * slots * tok * width, 2 * tok * width + 2 * slots * width),
        name="dispatch_rows",
    )(pos, values)


def gathered(first, second, parts):
    total, at = None, 0
    for part in parts:
        n = part.shape[0]
        here = lax.broadcasted_iota(jnp.int32, (first.shape[0], n), 1) + at
        pick = jnp.where((here == first) | (here == second), 1.0, 0.0).astype(BF16)
        term = dot_f32(pick, part[...], NN)
        total = term if total is None else total + term
        at += n
    return total


def combine_kernel(pos_ref, x_ref, part_ref, out_ref):
    out_ref[...] = x_ref[...] + gathered(pos_ref[:, 0:1], pos_ref[:, 1:2], [part_ref])


def combine(pos_cols, after_attn, gated):
    tok, width = after_attn.shape
    blk = 256
    return pl.pallas_call(
        combine_kernel,
        grid=(tok // blk,),
        in_specs=[
            pl.BlockSpec((blk, 4), lambda i: (i, 0)),
            pl.BlockSpec((blk, width), lambda i: (i, 0)),
            pl.BlockSpec(gated.shape, lambda i: (0, 0)),
        ],
        out_specs=pl.BlockSpec((blk, width), lambda i: (i, 0)),
        out_shape=jax.ShapeDtypeStruct((tok, width), F32),
        compiler_params=params(),
        cost_estimate=cost(2 * tok * gated.shape[0] * width, 10 * tok * width),
        name="combine_rows",
    )(pos_cols, after_attn, gated)


def return_kernel(pos_ref, x_ref, cot_ref, gain_ref, *refs):
    parts, (dx_ref, low_ref, gg_ref) = refs[:-3], refs[-3:]
    grad = gathered(pos_ref[:, 2:3], pos_ref[:, 3:4], parts)
    x = x_ref[...]
    inverse = lax.rsqrt(jnp.mean(x * x, axis=-1, keepdims=True) + EPSILON)
    normed = x * inverse
    grad_normed = grad * gain_ref[...]
    dx = cot_ref[...].astype(F32) + inverse * (
        grad_normed - normed * jnp.mean(grad_normed * normed, axis=-1, keepdims=True)
    )
    dx_ref[...] = dx
    low_ref[...] = dx.astype(BF16)

    @pl.when(pl.program_id(0) == 0)
    def _():
        gg_ref[...] = jnp.zeros_like(gg_ref)

    gg_ref[...] += jnp.sum(grad * normed, axis=0, keepdims=True)


def return_grads(pos_cols, after_attn, cotangent, gain, parts):
    tok, width = after_attn.shape
    blk = 256
    row = pl.BlockSpec((blk, width), lambda i: (i, 0))
    one = pl.BlockSpec((1, width), lambda i: (0, 0))
    slots = sum(p.shape[0] for p in parts)
    return pl.pallas_call(
        return_kernel,
        grid=(tok // blk,),
        in_specs=[pl.BlockSpec((blk, 4), lambda i: (i, 0)), row, row, one]
        + [pl.BlockSpec(p.shape, lambda i: (0, 0)) for p in parts],
        out_specs=[row, row, one],
        out_shape=[
            jax.ShapeDtypeStruct((tok, width), F32),
            jax.ShapeDtypeStruct((tok, width), BF16),
            jax.ShapeDtypeStruct((1, width), F32),
        ],
        compiler_params=params(),
        cost_estimate=cost(2 * tok * slots * width, 16 * tok * width),
        name="return_rows",
    )(pos_cols, after_attn, cotangent, gain, *parts)


def expert_kernel(experts, aliased, *refs):
    me_ref, x_ref, c_ref, d_ref, wg_ref, wu_ref, wr_ref, wrt_ref = refs[:8]
    refs = refs[8 + (3 if aliased else 0) :]
    act_ref, dg_ref, du_ref, out_ref, deo_ref, own_ref, gr_ref = refs[:7]
    acc_ref, gate_ref, prob_ref, p_ref = refs[7:]
    j = pl.program_id(0)
    rows_all = x_ref.shape[0]
    n_src, _, short, tile = d_ref.shape
    width = x_ref.shape[1]
    lane = lax.broadcasted_iota(jnp.int32, (rows_all, LANES), 1)

    @pl.when(j == 0)
    def _():
        logits = dot_f32(x_ref[...], wr_ref[...], NN)
        logits = jnp.where(lane < experts, logits, -1e30)
        exps = jnp.exp(logits - jnp.max(logits, axis=-1, keepdims=True))
        probs = exps / jnp.sum(exps, axis=-1, keepdims=True)
        prob_ref[...] = probs
        own = jnp.sum(jnp.where(lane == me_ref[1], probs, 0.0), axis=-1, keepdims=True)
        p_ref[...] = jnp.broadcast_to(own, p_ref.shape)
        own_ref[...] = p_ref[...].reshape(n_src, 1, short, LANES)
        wide = jnp.concatenate([p_ref[...]] * (width // LANES), axis=1)
        deo_ref[...] = (c_ref[...].reshape(rows_all, width).astype(F32) * wide).astype(BF16)
        acc_ref[...] = jnp.zeros_like(acc_ref)
        gate_ref[...] = jnp.zeros_like(gate_ref)

    n_blk = n_src // 2
    for b in range(n_blk):
        rows = slice(2 * b * short, 2 * (b + 1) * short)
        x = x_ref[rows, :]
        z = dot_f32(x, wg_ref[...], NN)
        up = dot_f32(x, wu_ref[...], NN)
        back = d_ref[2 * b : 2 * b + 2].reshape(2 * short, tile).astype(F32)
        reps = tile // LANES
        own = jnp.concatenate([p_ref[rows, :]] * reps, axis=1)
        zz = z * z
        th = jnp.tanh(GELU_C * z * (1.0 + GELU_A * zz))
        half = 0.5 + 0.5 * th
        gelu = z * half
        slope = half + 0.5 * GELU_C * z * (1.0 - th * th) * (1.0 + 3.0 * GELU_A * zz)
        act = (gelu * up).astype(BF16)
        act_ref[rows, :] = act
        share = act.astype(F32) * back
        gate_ref[rows, :] += sum(share[:, i * LANES : (i + 1) * LANES] for i in range(reps))
        dact = back * own
        dg = (dact * up * slope).astype(BF16)
        du = (dact * gelu).astype(BF16)
        dg_ref[rows, :] = dg
        du_ref[rows, :] = du
        acc_ref[rows, :] += dot_f32(dg, wg_ref[...], NT) + dot_f32(du, wu_ref[...], NT)

    @pl.when(j == pl.num_programs(0) - 1)
    def _():
        dgate = jnp.sum(gate_ref[...], axis=-1, keepdims=True)
        dl = dgate * p_ref[...] * (jnp.where(lane == me_ref[1], 1.0, 0.0) - prob_ref[...])
        dl = dl.astype(BF16)
        out_ref[...] = (acc_ref[...] + dot_f32(dl, wrt_ref[...], NN)).astype(BF16)
        gr_ref[...] = dot_f32(dl, x_ref[...], TN)[: gr_ref.shape[0], :]


def expert_chunk(me, rows, cot, dact, w_gate_up, wr_pad, wr_pad_t, experts, c, total_rows, earlier):
    n_src, chunks, short, width = cot.shape
    ff = dact.shape[-1]
    tile = 256
    steps = ff // tile
    n_rows = rows.shape[0]
    whole = pl.BlockSpec(memory_space=pl.ANY)
    part = pl.BlockSpec((n_rows, tile), lambda j, m: (c, j))
    aliased = earlier is not None
    few = -(-experts // 8) * 8
    call = pl.pallas_call(
        functools.partial(expert_kernel, experts, aliased),
        grid_spec=pltpu.PrefetchScalarGridSpec(
            num_scalar_prefetch=1,
            grid=(steps,),
            in_specs=[
                pl.BlockSpec((n_rows, width), lambda j, m: (0, 0)),
                pl.BlockSpec((n_src, 1, short, width), lambda j, m: (0, c, 0, 0)),
                pl.BlockSpec((n_src, 1, short, tile), lambda j, m: (0, c, 0, j)),
                pl.BlockSpec((width, tile), lambda j, m: (0, j)),
                pl.BlockSpec((width, tile), lambda j, m: (0, j + steps)),
                pl.BlockSpec((width, LANES), lambda j, m: (0, 0)),
                pl.BlockSpec((LANES, width), lambda j, m: (0, 0)),
            ]
            + ([whole] * 3 if aliased else []),
            out_specs=[
                part,
                part,
                part,
                pl.BlockSpec((n_rows, width), lambda j, m: (0, 0)),
                pl.BlockSpec((n_rows, width), lambda j, m: (0, 0)),
                pl.BlockSpec((n_src, 1, short, LANES), lambda j, m: (0, 0, 0, 0)),
                pl.BlockSpec((few, width), lambda j, m: (0, 0)),
            ],
            scratch_shapes=[
                pltpu.VMEM((n_rows, width), F32),
                pltpu.VMEM((n_rows, LANES), F32),
                pltpu.VMEM((n_rows, LANES), F32),
                pltpu.VMEM((n_rows, LANES), F32),
            ],
        ),
        out_shape=[jax.ShapeDtypeStruct((total_rows, ff), BF16)] * 3
        + [
            jax.ShapeDtypeStruct((n_rows, width), BF16),
            jax.ShapeDtypeStruct((n_rows, width), BF16),
            jax.ShapeDtypeStruct((n_src, 1, short, LANES), F32),
            jax.ShapeDtypeStruct((few, width), F32),
        ],
        input_output_aliases={8: 0, 9: 1, 10: 2} if aliased else {},
        compiler_params=params(),
        cost_estimate=cost(
            8 * n_rows * width * ff, 4 * width * ff + 10 * n_rows * ff + 4 * n_rows * width, n_rows * ff
        ),
        name="expert_rows",
    )
    out = call(me, rows, cot, dact, w_gate_up, w_gate_up, wr_pad, wr_pad_t, *(earlier if aliased else ()))
    return out[:3], out[3:]


def gated_kernel(chunks, act_ref, w_ref, *refs):
    own_refs, out_ref = refs[:-1], refs[-1]
    n_src, _, short, width = out_ref.shape
    n_rows = n_src * short
    for c in range(chunks):

        @pl.when(pl.program_id(0) == c)
        def _():
            own = jnp.concatenate([own_refs[c][...].reshape(n_rows, LANES)] * (width // LANES), axis=1)
            eo = dot_f32(act_ref[...], w_ref[...], NN) * own
            out_ref[...] = eo.astype(BF16).reshape(n_src, 1, short, width)


def gated_rows(act, w_eo, owns):
    chunks = len(owns)
    n_src, _, short, _ = owns[0].shape
    total, ff = act.shape
    width = w_eo.shape[1]
    return pl.pallas_call(
        functools.partial(gated_kernel, chunks),
        grid=(chunks,),
        in_specs=[
            pl.BlockSpec((total // chunks, ff), lambda c: (c, 0)),
            pl.BlockSpec((ff, width), lambda c: (0, 0)),
        ]
        + [pl.BlockSpec(o.shape, lambda c: (0, 0, 0, 0)) for o in owns],
        out_specs=pl.BlockSpec((n_src, 1, short, width), lambda c: (0, c, 0, 0)),
        out_shape=jax.ShapeDtypeStruct((n_src, chunks, short, width), BF16),
        compiler_params=params(),
        cost_estimate=cost(2 * total * ff * width, 2 * total * (ff + width) + 2 * ff * width),
        name="gated_rows",
    )(act, w_eo, *owns)


def share_rows(me_g, n_g, full_ref, keep_ref, send_ref):
    rows = full_ref.shape[0] // n_g
    for r_g in range(n_g):
        at = pl.multiple_of((me_g ^ r_g) * rows, rows)
        out = send_ref if r_g & 1 else keep_ref
        block = full_ref[pl.ds(at, rows), :].astype(BF16)
        if len(out.shape) == 4:
            out[0, r_g // 2] = block
        else:
            out[r_g // 2] = block


def weight_kernel(n_g, me_ref, a_ref, o_ref, b0_ref, b1_ref, b2_ref, d_ref, keep_ref, send_ref, full_ref, at_ref, ot_ref):
    @pl.when(pl.program_id(0) == 0)
    def _():
        at_ref[...] = a_ref[...].T
        ot_ref[...] = o_ref[...].T

    for i, b in enumerate((b0_ref, b1_ref, b2_ref)):
        full_ref[:, i * LANES : (i + 1) * LANES] = dot_f32(at_ref[...], b[0], NN)
    full_ref[:, 3 * LANES :] = dot_f32(ot_ref[...], d_ref[...], NN)
    share_rows(me_ref[0], n_g, full_ref, keep_ref, send_ref)


def weight_grads(me, a_one, mixed, grad_qkv, grad_low, n_g, n_e):
    tok, width = a_one.shape
    heads_wide = width // LANES
    block = pl.BlockSpec((1, n_g // 2, width // n_g, 4 * LANES), lambda r, m: (r, 0, 0, 0))

    def plane(t):
        def index(r, m):
            at = 3 * (m[1] ^ r) + t
            return (at // heads_wide, 0, at % heads_wide)

        return pl.BlockSpec((1, tok, LANES), index)

    return pl.pallas_call(
        functools.partial(weight_kernel, n_g),
        grid_spec=pltpu.PrefetchScalarGridSpec(
            num_scalar_prefetch=1,
            grid=(n_e,),
            in_specs=[
                pl.BlockSpec((tok, width), lambda r, m: (0, 0)),
                pl.BlockSpec((tok, width), lambda r, m: (0, 0)),
                plane(0),
                plane(1),
                plane(2),
                pl.BlockSpec((tok, LANES), lambda r, m: (0, m[1] ^ r)),
            ],
            out_specs=[block, block],
            scratch_shapes=[
                pltpu.VMEM((width, 4 * LANES), F32),
                pltpu.VMEM((width, tok), BF16),
                pltpu.VMEM((width, tok), BF16),
            ],
        ),
        out_shape=[jax.ShapeDtypeStruct((n_e, n_g // 2, width // n_g, 4 * LANES), BF16)] * 2,
        compiler_params=params(),
        cost_estimate=cost(8 * tok * width * width, 12 * tok * width + 8 * width * width),
        name="weight_grads",
    )(me, a_one, mixed, grad_qkv, grad_qkv, grad_qkv, grad_low)


def relative(v, axis, me, n):
    return jnp.stack([lax.dynamic_index_in_dim(v, me ^ r, axis, keepdims=False) for r in range(n)], axis)


def own_blocks(view, me_g, me_e, n_g, n_e):
    view = relative(relative(view, 0, me_e, n_e), 1, me_g, n_g)
    return view[:, 0::2], view[:, 1::2]


def gate_up_kernel(n_g, half, n_part, me_ref, *refs):
    parts, (g_ref, u_ref, keep_ref, send_ref, full_ref, t_ref) = refs[:n_part], refs[n_part:]
    j = pl.program_id(0)

    @pl.when(j == 0)
    def _():
        at = 0
        for part in parts:
            t_ref[:, at : at + part.shape[0]] = part[...].T
            at += part.shape[0]

    @pl.when(j < half)
    def _():
        full_ref[...] = dot_f32(t_ref[...], g_ref[...], NN)

    @pl.when(j >= half)
    def _():
        full_ref[...] = dot_f32(t_ref[...], u_ref[...], NN)

    share_rows(me_ref[0], n_g, full_ref, keep_ref, send_ref)


def gate_up_grad(me, parts, dg, du, n_g):
    total, ff = dg.shape
    width = parts[0].shape[1]
    tile = 256
    half = ff // tile
    spec = pl.BlockSpec((n_g // 2, width // n_g, tile), lambda j, m: (0, 0, j))
    return pl.pallas_call(
        functools.partial(gate_up_kernel, n_g, half, len(parts)),
        grid_spec=pltpu.PrefetchScalarGridSpec(
            num_scalar_prefetch=1,
            grid=(2 * half,),
            in_specs=[pl.BlockSpec(p.shape, lambda j, m: (0, 0)) for p in parts]
            + [
                pl.BlockSpec((total, tile), lambda j, m: (0, jnp.minimum(j, half - 1))),
                pl.BlockSpec((total, tile), lambda j, m: (0, jnp.maximum(j - half, 0))),
            ],
            out_specs=[spec, spec],
            scratch_shapes=[pltpu.VMEM((width, tile), F32), pltpu.VMEM((width, total), BF16)],
        ),
        out_shape=[jax.ShapeDtypeStruct((n_g // 2, width // n_g, 2 * ff), BF16)] * 2,
        compiler_params=params(),
        cost_estimate=cost(4 * total * width * ff, 2 * total * (width + 2 * ff) + 4 * width * ff),
        name="gate_up_grad",
    )(me, *parts, dg, du)


def out_grad_kernel(n_g, n_part, me_ref, act_ref, *refs):
    parts, (keep_ref, send_ref, full_ref, t_ref) = refs[:n_part], refs[n_part:]

    @pl.when(pl.program_id(0) == 0)
    def _():
        t_ref[...] = act_ref[...].T

    total, at = None, 0
    for part in parts:
        n = part.shape[0]
        term = dot_f32(t_ref[:, at : at + n], part[...], NN)
        total = term if total is None else total + term
        at += n
    full_ref[...] = total
    share_rows(me_ref[0], n_g, full_ref, keep_ref, send_ref)


def out_grad(me, act, parts, n_g):
    total, ff = act.shape
    width = parts[0].shape[1]
    tile = 256
    spec = pl.BlockSpec((n_g // 2, ff // n_g, tile), lambda j, m: (0, 0, j))
    return pl.pallas_call(
        functools.partial(out_grad_kernel, n_g, len(parts)),
        grid_spec=pltpu.PrefetchScalarGridSpec(
            num_scalar_prefetch=1,
            grid=(width // tile,),
            in_specs=[pl.BlockSpec((total, ff), lambda j, m: (0, 0))]
            + [pl.BlockSpec((p.shape[0], tile), lambda j, m: (0, j)) for p in parts],
            out_specs=[spec, spec],
            scratch_shapes=[pltpu.VMEM((ff, tile), F32), pltpu.VMEM((ff, total), BF16)],
        ),
        out_shape=[jax.ShapeDtypeStruct((n_g // 2, ff // n_g, width), BF16)] * 2,
        compiler_params=params(),
        cost_estimate=cost(2 * total * width * ff, 2 * total * (width + ff) + 2 * width * ff),
        name="out_grad",
    )(me, act, *parts)


def fill_mask(start, length, mask_ref):
    tok = mask_ref.shape[0]
    query = lax.broadcasted_iota(jnp.int32, (tok, tok), 0)
    key = lax.broadcasted_iota(jnp.int32, (tok, tok), 1)
    end = start + length
    inside = (query >= start) & (query < end) & (key >= start) & (key < end)
    mask_ref[...] = jnp.where((key <= query) | inside, 0.0, -1e30)


def half_lanes(v, h):
    lane = lax.broadcasted_iota(jnp.int32, v.shape, 1)
    return jnp.where((lane >= LANES // 2) == (h == 1), v, jnp.zeros_like(v))


def forward_kernel(blk, scale, s_ref, q_ref, k_ref, v_ref, b_ref, o_ref, lse_ref, mask_ref):
    tok = q_ref.shape[0]
    pair = pl.program_id(0)

    @pl.when(pair == 0)
    def _():
        fill_mask(s_ref[2], s_ref[3], mask_ref)
        lse_ref[...] = jnp.zeros_like(lse_ref)

    lane = lax.broadcasted_iota(jnp.int32, (blk, LANES), 1)
    values = [half_lanes(v_ref[...], h) for h in range(2)]
    for i in range(tok // blk):
        rows = slice(i * blk, (i + 1) * blk)
        mixed, lse = None, lse_ref[rows, :]
        for h in range(2):
            q = half_lanes(q_ref[rows, :] * scale, h)
            s = dot_f32(q, k_ref[...], NT) + b_ref[h, rows, :].astype(F32) + mask_ref[rows, :]
            top = jnp.max(s, axis=-1, keepdims=True)
            e = jnp.exp(s - top)
            total = jnp.sum(e, axis=-1, keepdims=True)
            p = (e * (1.0 / total)).astype(BF16)
            o = dot_f32(p, values[h], NN)
            mixed = o if mixed is None else mixed + o
            lse = jnp.where(lane == 2 * pair + h, top + jnp.log(total), lse)
        o_ref[rows, :] = mixed.astype(BF16)
        lse_ref[rows, :] = lse


def attention_forward(scalars, qkv, rel_bias, scale):
    tok, width = qkv.shape[0], qkv.shape[1] // 3
    pairs = width // LANES
    column = lambda p: pl.BlockSpec((tok, LANES), lambda i, m: (0, p * pairs + i))
    return pl.pallas_call(
        functools.partial(forward_kernel, 128, scale),
        grid_spec=pltpu.PrefetchScalarGridSpec(
            num_scalar_prefetch=1,
            grid=(pairs,),
            in_specs=[
                column(0),
                column(1),
                column(2),
                pl.BlockSpec((2, tok, tok), lambda i, m: (i, 0, 0)),
            ],
            out_specs=[
                pl.BlockSpec((tok, LANES), lambda i, m: (0, i)),
                pl.BlockSpec((tok, LANES), lambda i, m: (0, 0)),
            ],
            scratch_shapes=[pltpu.VMEM((tok, tok), F32)],
        ),
        out_shape=[
            jax.ShapeDtypeStruct((tok, width), BF16),
            jax.ShapeDtypeStruct((tok, LANES), F32),
        ],
        compiler_params=params(),
        cost_estimate=cost(8 * tok * tok * width, 8 * tok * width + 32 * tok * tok, 16 * tok * tok),
        name="attention_forward",
    )(scalars, qkv, qkv, qkv, rel_bias)


def backward_kernel(n_g, scale, per_owner, s_ref, q_ref, k_ref, v_ref, do_ref, b_ref, lse_ref, *refs):
    outs, (dqkv_ref, mask_ref) = refs[:-2], refs[-2:]
    tok = q_ref.shape[0]
    rows = tok // n_g
    pair = s_ref[1] ^ pl.program_id(0) if per_owner else pl.program_id(0)

    @pl.when(pl.program_id(0) == 0)
    def _():
        fill_mask(s_ref[2], s_ref[3], mask_ref)

    lane = lax.broadcasted_iota(jnp.int32, (rows, LANES), 1)
    keys = [half_lanes(k_ref[...], h) for h in range(2)]
    grad_k = grad_v = None
    for r_g in range(n_g):
        at = pl.multiple_of((s_ref[0] ^ r_g) * rows, rows) if per_owner else r_g * rows
        here = pl.ds(at, rows)
        grad_q = None
        for h in range(2):
            q = half_lanes(q_ref[here, :] * scale, h)
            do = half_lanes(do_ref[here, :], h)
            lse = jnp.sum(jnp.where(lane == 2 * pair + h, lse_ref[here, :], 0.0), axis=-1, keepdims=True)
            s = dot_f32(q, k_ref[...], NT) + b_ref[h, here, :].astype(F32) + mask_ref[here, :]
            p = jnp.exp(s - lse)
            dp = dot_f32(do, v_ref[...], NT)
            ds = p * (dp - jnp.sum(p * dp, axis=-1, keepdims=True))
            ds = ds.astype(BF16)
            if per_owner:
                outs[r_g & 1][0, r_g // 2, h * rows : (h + 1) * rows, :] = ds
            else:
                outs[0][h, here, :] = ds
            dv = dot_f32(p.astype(BF16), do, TN)
            dk = dot_f32(ds, q, TN)
            dq = dot_f32(ds, keys[h], NN)
            grad_v = dv if grad_v is None else grad_v + dv
            grad_k = dk if grad_k is None else grad_k + dk
            grad_q = dq if grad_q is None else grad_q + dq
        dqkv_ref[0, here, :] = (grad_q * scale).astype(BF16)
    dqkv_ref[1] = grad_k.astype(BF16)
    dqkv_ref[2] = grad_v.astype(BF16)


def attention_backward(scalars, qkv, grad_mixed, rel_bias, lse, scale, n_g, n_e, per_owner):
    tok, width = grad_mixed.shape
    pairs = width // LANES
    turn = (lambda i, m: m[1] ^ i) if per_owner else (lambda i, m: i)
    column = lambda p: pl.BlockSpec((tok, LANES), lambda i, m: (0, p * pairs + turn(i, m)))
    if per_owner:
        block = pl.BlockSpec((1, n_g // 2, 2 * tok // n_g, tok), lambda i, m: (i, 0, 0, 0))
        bias_specs = [block, block]
        bias_shapes = [jax.ShapeDtypeStruct((n_e, n_g // 2, 2 * tok // n_g, tok), BF16)] * 2
    else:
        bias_specs = [pl.BlockSpec((2, tok, tok), lambda i, m: (i, 0, 0))]
        bias_shapes = [jax.ShapeDtypeStruct((2 * pairs, tok, tok), BF16)]
    return pl.pallas_call(
        functools.partial(backward_kernel, n_g, scale, per_owner),
        grid_spec=pltpu.PrefetchScalarGridSpec(
            num_scalar_prefetch=1,
            grid=(pairs,),
            in_specs=[
                column(0),
                column(1),
                column(2),
                column(0),
                pl.BlockSpec((2, tok, tok), lambda i, m: (turn(i, m), 0, 0)),
                pl.BlockSpec((tok, LANES), lambda i, m: (0, 0)),
            ],
            out_specs=bias_specs + [pl.BlockSpec((3, tok, LANES), lambda i, m: (0, 0, turn(i, m)))],
            scratch_shapes=[pltpu.VMEM((tok, tok), F32)],
        ),
        out_shape=bias_shapes + [jax.ShapeDtypeStruct((3, tok, width), BF16)],
        compiler_params=params(),
        cost_estimate=cost(20 * tok * tok * width, 16 * tok * width + 64 * tok * tok, 16 * tok * tok),
        name="attention_backward",
    )(scalars, qkv, qkv, qkv, grad_mixed, rel_bias, lse)


def norm_forward(values):
    inverse = lax.rsqrt(jnp.mean(values * values, axis=-1, keepdims=True) + EPSILON)
    return (values * inverse, inverse)


def norm_backward(grad_out, normed, inverse, norm_gain):
    grad_normed = grad_out * norm_gain
    grad_gain = jnp.sum(grad_out * normed, axis=0)
    grad_input = inverse * (
        grad_normed - normed * jnp.mean(grad_normed * normed, axis=-1, keepdims=True)
    )
    return (grad_input, grad_gain)


def body(
    tokens,
    cotangent,
    w_qkv,
    w_out_attn,
    rel_bias,
    norm_gains,
    w_router,
    w_gate_up,
    w_expert_out,
    routes,
    spans,
):
    tok, width = tokens.shape
    n_g, n_e = lax.axis_size("grp"), lax.axis_size("ep")
    assert w_gate_up.shape[0] == 1 and spans.shape[0] == 1 and tok == LENGTH
    assert n_g & (n_g - 1) == 0 and n_e & (n_e - 1) == 0 and n_g > 1 and n_e > 3
    assert width == HEADS * LANES // 2
    experts = n_e
    cap = 5 * routes.shape[1] * tok // (4 * experts)
    chunks = 2 if cap % 32 == 0 else 1
    short = cap // chunks
    slots = experts * cap
    scale = 1.0 / math.sqrt(width // HEADS)
    me_g, me_e = lax.axis_index("grp"), lax.axis_index("ep")
    me = jnp.stack([me_g, me_e, spans[0, 0], spans[0, 1]]).astype(jnp.int32)
    w_gu, w_eo = w_gate_up[0], w_expert_out[0]

    pos, cot_out = place(routes.T, cotangent, experts, cap, chunks)
    pos_cols = pos.T
    tokens = after(tokens, cot_out)
    cot_rows = swap_rows(cot_out)

    hidden = tokens.astype(F32)
    normed_one, inverse_one = norm_forward(hidden)
    a_one = (normed_one * norm_gains[0]).astype(BF16)
    qkv_rows = dot_f32(a_one, w_qkv, NN).astype(BF16)
    mixed_heads, lse = attention_forward(me, qkv_rows, rel_bias, scale)
    after_attn = hidden + dot_f32(mixed_heads, w_out_attn, NN)
    normed_two, _ = norm_forward(after_attn)
    a_two = (normed_two * norm_gains[1]).astype(BF16)

    parts = dispatch(pos, after(a_two, cot_rows), slots, chunks)
    dact = dot_f32(cot_rows, w_eo, NT).astype(BF16)
    parts = [swap_rows(p if c == 0 else after(p, dact)) for c, p in enumerate(parts)]
    dact = dact.reshape(n_e, chunks, short, -1)
    cot_view = cot_rows.reshape(n_e, chunks, short, width)
    wr_pad = jnp.pad(w_router, ((0, 0), (0, LANES - experts)))
    wr_pad_t = wr_pad.T
    state, back, deos, owns, grad_route = None, [], [], [], 0.0
    for c in range(chunks):
        state, (dxe, deo, own, gr) = expert_chunk(
            me, parts[c], cot_view, dact, w_gu, wr_pad, wr_pad_t, experts, c, slots, state
        )
        back.append(swap_rows(dxe))
        deos.append(deo)
        owns.append(own)
        grad_route = grad_route + gr[:experts]
    act, dg, du = state

    core = ("grp", 1)
    gate_keep, gate_out = gate_up_grad(me, parts, after(dg, *back[:-1]), du, n_g)
    gate = group_way(gate_keep, xor_send(gate_out, *core), n_g)
    gated = gated_rows(after(act, gate_out, *back), w_eo, owns).reshape(slots, width)
    gate_send = next_send(gate)
    gate = exchange(gate, gate_send)

    grad_after, grad_attn_low, grad_gain_two = return_grads(
        pos_cols, after_attn, cotangent, norm_gains[1:], [after(back[0], gated, gate_send)] + back[1:]
    )
    gated = swap_rows(after(gated, *back))
    grad_mixed = dot_f32(grad_attn_low, w_out_attn, NT).astype(BF16)
    rows_g, rows_t = width // n_g, tok // n_g
    per_owner = n_e * LANES == width
    *grad_bias, grad_qkv = attention_backward(
        me, qkv_rows, grad_mixed, rel_bias, lse, scale, n_g, n_e, per_owner
    )
    if not per_owner:
        bias = grad_bias[0].reshape(n_e, HEADS // n_e, n_g, rows_t, tok).transpose(0, 2, 1, 3, 4)
        grad_bias = own_blocks(bias.reshape(n_e, n_g, -1, tok), me_g, me_e, n_g, n_e)
    bias = three_ways(grad_bias[0], xor_send(grad_bias[1], *core), n_g, n_e)
    grad_a_one = sum(
        dot_f32(grad_qkv[i], w_qkv[:, i * width : (i + 1) * width], NT) for i in range(3)
    )
    sends = [next_send(way) for way in bias]
    bias = [exchange(way, send) for way, send in zip(bias, sends)]
    grad_qkv_late = after(grad_qkv, *sends)
    if per_owner:
        weights = weight_grads(me, a_one, mixed_heads, grad_qkv_late, grad_attn_low, n_g, n_e)
    else:
        flat = jnp.concatenate([grad_qkv_late[i] for i in range(3)], axis=1)
        full = [dot_f32(a_one, flat, TN), dot_f32(mixed_heads, grad_attn_low, TN)]
        full = [f.astype(BF16).reshape(n_g, rows_g, n_e, -1) for f in full]
        full = jnp.concatenate(full, axis=-1).transpose(2, 0, 1, 3)
        weights = own_blocks(full, me_g, me_e, n_g, n_e)
    deos[0] = after(deos[0], weights[1], gate[0][-1])
    weights = three_ways(weights[0], xor_send(weights[1], *core), n_g, n_e)
    out_keep, out_send = out_grad(me, act, deos, n_g)
    expert_out = group_way(out_keep, xor_send(out_send, *core), n_g)
    sends = [after(next_send(way), out_send) for way in weights]
    weights = [exchange(way, send) for way, send in zip(weights, sends)]
    output = combine(pos_cols, after(after_attn, *sends), gated)
    out_send = next_send(expert_out)
    expert_out = exchange(expert_out, out_send)
    sends = [after(next_send(way), *sends) for way in bias]
    bias = [exchange(way, send) for way, send in zip(bias, sends)]
    grad_norm_one, grad_gain_one = norm_backward(grad_a_one, normed_one, inverse_one, norm_gains[0])
    grad_tokens = grad_after + grad_norm_one
    small = jnp.concatenate([grad_gain_one[None], grad_gain_two, grad_route])
    small = lax.all_gather(small, ("grp", "ep"))
    gate[0][-1] = after(gate[0][-1], *sends)
    grad_w_gate = finish(gate)[None]
    sends = [after(next_send(way), out_send) for way in weights]
    weights = [exchange(way, send) for way, send in zip(weights, sends)]
    sends = [after(next_send(way), grad_w_gate, output, *sends) for way in bias]
    bias = [exchange(way, send) for way, send in zip(bias, sends)]
    expert_out[0][0] = after(expert_out[0][0], *sends)
    grad_w_expert = finish(expert_out)[None]
    small = jnp.sum(after(small, *sends), axis=0)
    g_bias = jnp.concatenate([finish(way) for way in bias]).reshape(HEADS // n_e, rows_t, tok)
    g_weights = jnp.concatenate([finish(way) for way in weights])
    wide = 3 * width // n_e
    return (
        output,
        grad_tokens,
        g_weights[:, :wide],
        g_weights[:, wide:],
        g_bias,
        small[:2],
        small[2:].T,
        grad_w_gate,
        grad_w_expert,
    )


def solution(mesh):
    placed = (
        P(("grp", "ep"), None),
        P(("grp", "ep"), None),
        P(),
        P(),
        P(),
        P(),
        P(),
        P("ep", None, None),
        P("ep", None, None),
        P(("grp", "ep"), None),
        P(("grp", "ep"), None),
    )
    return jax.shard_map(
        body,
        mesh=mesh,
        in_specs=placed,
        out_specs=(
            P(("grp", "ep"), None),
            P(("grp", "ep"), None),
            P("grp", "ep"),
            P("grp", "ep"),
            P("ep", "grp", None),
            P(),
            P(),
            P("ep", "grp", None),
            P("ep", "grp", None),
        ),
        check_vma=False,
    )
```

```python
import functools
import math

import jax
import jax.numpy as jnp
from jax import lax
from jax.experimental import pallas as pl
from jax.experimental.pallas import tpu as pltpu
from jax.sharding import PartitionSpec as P

HEADS = 16
LENGTH = 512
EPSILON = 1e-06
LANES = 128
GELU_C = math.sqrt(2.0 / math.pi)
GELU_A = 0.044715
F32 = jnp.float32
BF16 = jnp.bfloat16
VMEM_LIMIT = 60 * 1024 * 1024


def params(**kw):
    return pltpu.CompilerParams(vmem_limit_bytes=VMEM_LIMIT, **kw)


def cost(flops, nbytes, trans=0):
    return pl.CostEstimate(flops=int(flops), bytes_accessed=int(nbytes), transcendentals=int(trans))


def dot_f32(a, b, dims):
    return lax.dot_general(a, b, (dims, ((), ())), preferred_element_type=F32)


NN = ((1,), (0,))
NT = ((1,), (1,))
TN = ((0,), (0,))


def xor_send(v, axis, k):
    n = lax.axis_size(axis)
    return lax.ppermute(v, axis, [(i, i ^ k) for i in range(n)])


def swap_rows(v):
    return lax.all_to_all(v, "ep", split_axis=0, concat_axis=0, tiled=True)


def bits_of(n):
    return [1 << i for i in range(n.bit_length() - 1)]


def after(value, *others):
    return lax.optimization_barrier((value, *others))[0]


def halving_orders(n_g, n_e):
    g_bits = [("grp", k) for k in bits_of(n_g)]
    e_bits = [("ep", k) for k in bits_of(n_e)]
    rest, first, others = g_bits[1:], e_bits[:1], e_bits[1:]
    return [first + rest + others, others + first + rest, rest + first + others]


def row_cuts(rows):
    unit = rows // 16
    return [0, 16 * round(3 * unit / 8), 16 * round(5 * unit / 8), rows]


def first_kernel(orders, cuts, k_ref, g_ref, *outs):
    r = pl.program_id(0)
    bit = lambda x, axis, k: (2 * x // k) % 2 if axis == "grp" else (r // k) % 2
    for x in range(k_ref.shape[1]):
        at = 0
        for order, lo, hi in zip(orders, cuts, cuts[1:]):
            if lo == hi:
                continue
            total = (k_ref[0, x, lo:hi, :].astype(F32) + g_ref[0, x, lo:hi, :].astype(F32)).astype(BF16)
            index = 0
            for step in order[1:]:
                index = 2 * index + bit(x, *step)
            goes = bit(x, *order[0])
            for side in range(2):

                @pl.when(goes == side)
                def _():
                    outs[at + side][index] = total

            at += 2


def first_sums(keep, got, orders):
    n_e, n_x, rows, cols = keep.shape
    cuts = row_cuts(rows)
    used = [(o, hi - lo) for o, lo, hi in zip(orders, cuts, cuts[1:]) if hi > lo]
    half = n_e * n_x // 2
    shapes = [jax.ShapeDtypeStruct((half, n, cols), BF16) for _, n in used for _ in range(2)]
    out = pl.pallas_call(
        functools.partial(first_kernel, orders, cuts),
        grid=(n_e,),
        in_specs=[pl.BlockSpec((1, n_x, rows, cols), lambda r: (r, 0, 0, 0))] * 2,
        out_specs=[pl.BlockSpec(s.shape, lambda r: (0, 0, 0)) for s in shapes],
        out_shape=shapes,
        compiler_params=params(),
        cost_estimate=cost(n_e * n_x * rows * cols, 6 * n_e * n_x * rows * cols),
        name="first_sums",
    )(keep, got)
    return [(out[2 * i], out[2 * i + 1], o) for i, (o, _) in enumerate(used)]


def split_kernel(n_way, n_set, *refs):
    ins, outs = refs[: 2 * n_way * n_set], refs[2 * n_way * n_set :]
    for w in range(n_way):
        keep_ref, send_ref = outs[2 * w : 2 * w + 2]
        half, at = keep_ref.shape[0], 0
        for i in range(n_set):
            k_ref, g_ref = ins[2 * (w * n_set + i) : 2 * (w * n_set + i) + 2]
            to = at + k_ref.shape[1]
            keep_ref[:, at:to, :] = (k_ref[:half].astype(F32) + g_ref[:half].astype(F32)).astype(BF16)
            send_ref[:, at:to, :] = (k_ref[half:].astype(F32) + g_ref[half:].astype(F32)).astype(BF16)
            at = to


def next_sums(sets):
    ways = list(zip(*sets))
    shapes = []
    for way in ways:
        blocks, _, cols = way[0][0].shape
        shape = jax.ShapeDtypeStruct((blocks // 2, sum(one[0].shape[1] for one in way), cols), BF16)
        shapes += [shape, shape]
    ins = [v for way in ways for one in way for v in one[:2]]
    total = sum(math.prod(s.shape) for s in shapes)
    out = pl.pallas_call(
        functools.partial(split_kernel, len(ways), len(sets)),
        out_shape=shapes,
        compiler_params=params(),
        cost_estimate=cost(total, 6 * total),
        name="split_sums",
    )(*ins)
    return [(out[2 * i], out[2 * i + 1], way[0][2]) for i, way in enumerate(ways)]


def send_all(ways):
    return [(keep, xor_send(send, *order[0]), order[1:]) for keep, send, order in ways]


def last_sums(ways):
    return [(keep[0].astype(F32) + got[0].astype(F32)) for keep, got, _ in ways]


def last_kernel(*refs):
    ins, (bias_ref, qkv_ref, out_ref) = refs[:-3], refs[-3:]
    wide = qkv_ref.shape[1]
    at = 0
    for k_ref, g_ref in zip(ins[0::2], ins[1::2]):
        n = k_ref.shape[1] // 2
        total = k_ref[0].astype(F32) + g_ref[0].astype(F32)
        bias_ref[at : at + n, :] = total[:n]
        qkv_ref[at : at + n, :] = total[n:, :wide]
        out_ref[at : at + n, :] = total[n:, wide:]
        at += n


def last_merged(ways, wide):
    rows, cols = sum(w[0].shape[1] for w in ways) // 2, ways[0][0].shape[2]
    return pl.pallas_call(
        last_kernel,
        out_shape=[jax.ShapeDtypeStruct((rows, n), F32) for n in (cols, wide, cols - wide)],
        compiler_params=params(),
        cost_estimate=cost(2 * rows * cols, 16 * rows * cols),
        name="last_sums",
    )(*[v for w in ways for v in w[:2]])


def tied(ways, *others):
    return [(after(ways[0][0], *others), *ways[0][1:])] + ways[1:]


def place_kernel(experts, cap, chunks, routes_ref, v_ref, pos_ref, out_ref):
    tok = v_ref.shape[0]
    short = cap // chunks
    ids = lax.broadcasted_iota(jnp.int32, (LANES, tok), 0)
    named = [ids == routes_ref[k : k + 1, :] for k in range(2)]
    counts = jnp.where(named[0] | named[1], 1.0, 0.0).astype(BF16)
    before = lax.broadcasted_iota(jnp.int32, (tok, tok), 0) < lax.broadcasted_iota(
        jnp.int32, (tok, tok), 1
    )
    earlier = dot_f32(counts, jnp.where(before, 1.0, 0.0).astype(BF16), NN)
    for k in range(2):
        slot = jnp.sum(jnp.where(named[k], earlier, 0.0), axis=0, keepdims=True).astype(jnp.int32)
        owner = routes_ref[k : k + 1, :]
        pos_ref[k : k + 1, :] = owner * cap + slot
        chunk = jnp.zeros_like(slot)
        for c in range(1, chunks):
            chunk += jnp.where(slot >= c * short, 1, 0)
        pos_ref[2 + k : 3 + k, :] = chunk * (experts * short) + owner * short + slot - chunk * short
    first, second = pos_ref[0:1, :], pos_ref[1:2, :]
    rows = lax.broadcasted_iota(jnp.int32, (cap, tok), 0)
    for e in range(experts):
        here = rows + e * cap
        pick = jnp.where((here == first) | (here == second), 1.0, 0.0).astype(BF16)
        out_ref[e * cap : (e + 1) * cap, :] = dot_f32(pick, v_ref[...], NN).astype(BF16)


def place(routes_t, values, experts, cap, chunks):
    tok, width = values.shape
    return pl.pallas_call(
        functools.partial(place_kernel, experts, cap, chunks),
        out_shape=[
            jax.ShapeDtypeStruct((4, tok), jnp.int32),
            jax.ShapeDtypeStruct((experts * cap, width), BF16),
        ],
        compiler_params=params(),
        cost_estimate=cost(2 * experts * cap * tok * width, 2 * tok * width + 2 * experts * cap * width),
        name="place_rows",
    )(routes_t, values)


def dispatch_kernel(pos_ref, v_ref, *outs):
    tok = v_ref.shape[0]
    first, second = pos_ref[2:3, :], pos_ref[3:4, :]
    at = 0
    for out in outs:
        total = out.shape[0]
        step = total // 4
        rows = lax.broadcasted_iota(jnp.int32, (step, tok), 0)
        for b in range(4):
            here = rows + at
            pick = jnp.where((here == first) | (here == second), 1.0, 0.0).astype(BF16)
            out[b * step : (b + 1) * step, :] = dot_f32(pick, v_ref[...], NN).astype(BF16)
            at += step


def dispatch(pos, values, slots, chunks):
    tok, width = values.shape
    return pl.pallas_call(
        dispatch_kernel,
        out_shape=[jax.ShapeDtypeStruct((slots // chunks, width), BF16)] * chunks,
        compiler_params=params(),
        cost_estimate=cost(2 * slots * tok * width, 2 * tok * width + 2 * slots * width),
        name="dispatch_rows",
    )(pos, values)


def gathered(first, second, parts):
    total, at = None, 0
    for part in parts:
        n = part.shape[0]
        here = lax.broadcasted_iota(jnp.int32, (first.shape[0], n), 1) + at
        pick = jnp.where((here == first) | (here == second), 1.0, 0.0).astype(BF16)
        term = dot_f32(pick, part[...], NN)
        total = term if total is None else total + term
        at += n
    return total


def combine_kernel(pos_ref, x_ref, part_ref, out_ref):
    out_ref[...] = x_ref[...] + gathered(pos_ref[:, 0:1], pos_ref[:, 1:2], [part_ref])


def combine(pos_cols, after_attn, gated):
    tok, width = after_attn.shape
    blk = 256
    return pl.pallas_call(
        combine_kernel,
        grid=(tok // blk,),
        in_specs=[
            pl.BlockSpec((blk, 4), lambda i: (i, 0)),
            pl.BlockSpec((blk, width), lambda i: (i, 0)),
            pl.BlockSpec(gated.shape, lambda i: (0, 0)),
        ],
        out_specs=pl.BlockSpec((blk, width), lambda i: (i, 0)),
        out_shape=jax.ShapeDtypeStruct((tok, width), F32),
        compiler_params=params(),
        cost_estimate=cost(2 * tok * gated.shape[0] * width, 10 * tok * width),
        name="combine_rows",
    )(pos_cols, after_attn, gated)


def return_kernel(pos_ref, x_ref, cot_ref, gain_ref, *refs):
    parts, (dx_ref, low_ref, gg_ref) = refs[:-3], refs[-3:]
    grad = gathered(pos_ref[:, 2:3], pos_ref[:, 3:4], parts)
    x = x_ref[...]
    inverse = lax.rsqrt(jnp.mean(x * x, axis=-1, keepdims=True) + EPSILON)
    normed = x * inverse
    grad_normed = grad * gain_ref[...]
    dx = cot_ref[...].astype(F32) + inverse * (
        grad_normed - normed * jnp.mean(grad_normed * normed, axis=-1, keepdims=True)
    )
    dx_ref[...] = dx
    low_ref[...] = dx.astype(BF16)

    @pl.when(pl.program_id(0) == 0)
    def _():
        gg_ref[...] = jnp.zeros_like(gg_ref)

    gg_ref[...] += jnp.sum(grad * normed, axis=0, keepdims=True)


def return_grads(pos_cols, after_attn, cotangent, gain, parts):
    tok, width = after_attn.shape
    blk = 256
    row = pl.BlockSpec((blk, width), lambda i: (i, 0))
    one = pl.BlockSpec((1, width), lambda i: (0, 0))
    slots = sum(p.shape[0] for p in parts)
    return pl.pallas_call(
        return_kernel,
        grid=(tok // blk,),
        in_specs=[pl.BlockSpec((blk, 4), lambda i: (i, 0)), row, row, one]
        + [pl.BlockSpec(p.shape, lambda i: (0, 0)) for p in parts],
        out_specs=[row, row, one],
        out_shape=[
            jax.ShapeDtypeStruct((tok, width), F32),
            jax.ShapeDtypeStruct((tok, width), BF16),
            jax.ShapeDtypeStruct((1, width), F32),
        ],
        compiler_params=params(),
        cost_estimate=cost(2 * tok * slots * width, 16 * tok * width),
        name="return_rows",
    )(pos_cols, after_attn, cotangent, gain, *parts)


def expert_kernel(experts, aliased, *refs):
    me_ref, x_ref, c_ref, d_ref, wg_ref, wu_ref, wr_ref, wrt_ref = refs[:8]
    refs = refs[8 + (3 if aliased else 0) :]
    act_ref, dg_ref, du_ref, out_ref, deo_ref, own_ref, gr_ref = refs[:7]
    acc_ref, gate_ref, prob_ref, p_ref = refs[7:]
    j = pl.program_id(0)
    rows_all = x_ref.shape[0]
    n_src, _, short, tile = d_ref.shape
    width = x_ref.shape[1]
    lane = lax.broadcasted_iota(jnp.int32, (rows_all, LANES), 1)

    @pl.when(j == 0)
    def _():
        logits = dot_f32(x_ref[...], wr_ref[...], NN)
        logits = jnp.where(lane < experts, logits, -1e30)
        exps = jnp.exp(logits - jnp.max(logits, axis=-1, keepdims=True))
        probs = exps / jnp.sum(exps, axis=-1, keepdims=True)
        prob_ref[...] = probs
        own = jnp.sum(jnp.where(lane == me_ref[1], probs, 0.0), axis=-1, keepdims=True)
        p_ref[...] = jnp.broadcast_to(own, p_ref.shape)
        own_ref[...] = p_ref[...].reshape(n_src, 1, short, LANES)
        wide = jnp.concatenate([p_ref[...]] * (width // LANES), axis=1)
        deo_ref[...] = (c_ref[...].reshape(rows_all, width).astype(F32) * wide).astype(BF16)
        acc_ref[...] = jnp.zeros_like(acc_ref)
        gate_ref[...] = jnp.zeros_like(gate_ref)

    n_blk = n_src // 2
    for b in range(n_blk):
        rows = slice(2 * b * short, 2 * (b + 1) * short)
        x = x_ref[rows, :]
        z = dot_f32(x, wg_ref[...], NN)
        up = dot_f32(x, wu_ref[...], NN)
        back = d_ref[2 * b : 2 * b + 2].reshape(2 * short, tile).astype(F32)
        reps = tile // LANES
        own = jnp.concatenate([p_ref[rows, :]] * reps, axis=1)
        zz = z * z
        th = jnp.tanh(GELU_C * z * (1.0 + GELU_A * zz))
        half = 0.5 + 0.5 * th
        gelu = z * half
        slope = half + 0.5 * GELU_C * z * (1.0 - th * th) * (1.0 + 3.0 * GELU_A * zz)
        act = (gelu * up).astype(BF16)
        act_ref[rows, :] = act
        share = act.astype(F32) * back
        gate_ref[rows, :] += sum(share[:, i * LANES : (i + 1) * LANES] for i in range(reps))
        dact = back * own
        dg = (dact * up * slope).astype(BF16)
        du = (dact * gelu).astype(BF16)
        dg_ref[rows, :] = dg
        du_ref[rows, :] = du
        acc_ref[rows, :] += dot_f32(dg, wg_ref[...], NT) + dot_f32(du, wu_ref[...], NT)

    @pl.when(j == pl.num_programs(0) - 1)
    def _():
        dgate = jnp.sum(gate_ref[...], axis=-1, keepdims=True)
        dl = dgate * p_ref[...] * (jnp.where(lane == me_ref[1], 1.0, 0.0) - prob_ref[...])
        dl = dl.astype(BF16)
        out_ref[...] = (acc_ref[...] + dot_f32(dl, wrt_ref[...], NN)).astype(BF16)
        gr_ref[...] = dot_f32(dl, x_ref[...], TN)[: gr_ref.shape[0], :]


def expert_chunk(me, rows, cot, dact, w_gate_up, wr_pad, wr_pad_t, experts, c, total_rows, earlier):
    n_src, chunks, short, width = cot.shape
    ff = dact.shape[-1]
    tile = 256
    steps = ff // tile
    n_rows = rows.shape[0]
    whole = pl.BlockSpec(memory_space=pl.ANY)
    part = pl.BlockSpec((n_rows, tile), lambda j, m: (c, j))
    aliased = earlier is not None
    few = -(-experts // 8) * 8
    call = pl.pallas_call(
        functools.partial(expert_kernel, experts, aliased),
        grid_spec=pltpu.PrefetchScalarGridSpec(
            num_scalar_prefetch=1,
            grid=(steps,),
            in_specs=[
                pl.BlockSpec((n_rows, width), lambda j, m: (0, 0)),
                pl.BlockSpec((n_src, 1, short, width), lambda j, m: (0, c, 0, 0)),
                pl.BlockSpec((n_src, 1, short, tile), lambda j, m: (0, c, 0, j)),
                pl.BlockSpec((width, tile), lambda j, m: (0, j)),
                pl.BlockSpec((width, tile), lambda j, m: (0, j + steps)),
                pl.BlockSpec((width, LANES), lambda j, m: (0, 0)),
                pl.BlockSpec((LANES, width), lambda j, m: (0, 0)),
            ]
            + ([whole] * 3 if aliased else []),
            out_specs=[
                part,
                part,
                part,
                pl.BlockSpec((n_rows, width), lambda j, m: (0, 0)),
                pl.BlockSpec((n_rows, width), lambda j, m: (0, 0)),
                pl.BlockSpec((n_src, 1, short, LANES), lambda j, m: (0, 0, 0, 0)),
                pl.BlockSpec((few, width), lambda j, m: (0, 0)),
            ],
            scratch_shapes=[
                pltpu.VMEM((n_rows, width), F32),
                pltpu.VMEM((n_rows, LANES), F32),
                pltpu.VMEM((n_rows, LANES), F32),
                pltpu.VMEM((n_rows, LANES), F32),
            ],
        ),
        out_shape=[jax.ShapeDtypeStruct((total_rows, ff), BF16)] * 3
        + [
            jax.ShapeDtypeStruct((n_rows, width), BF16),
            jax.ShapeDtypeStruct((n_rows, width), BF16),
            jax.ShapeDtypeStruct((n_src, 1, short, LANES), F32),
            jax.ShapeDtypeStruct((few, width), F32),
        ],
        input_output_aliases={8: 0, 9: 1, 10: 2} if aliased else {},
        compiler_params=params(),
        cost_estimate=cost(
            8 * n_rows * width * ff, 4 * width * ff + 10 * n_rows * ff + 4 * n_rows * width, n_rows * ff
        ),
        name="expert_rows",
    )
    out = call(me, rows, cot, dact, w_gate_up, w_gate_up, wr_pad, wr_pad_t, *(earlier if aliased else ()))
    return out[:3], out[3:]


def gated_kernel(chunks, act_ref, w_ref, *refs):
    own_refs, out_ref = refs[:-1], refs[-1]
    n_src, _, short, width = out_ref.shape
    n_rows = n_src * short
    for c in range(chunks):

        @pl.when(pl.program_id(0) == c)
        def _():
            own = jnp.concatenate([own_refs[c][...].reshape(n_rows, LANES)] * (width // LANES), axis=1)
            eo = dot_f32(act_ref[...], w_ref[...], NN) * own
            out_ref[...] = eo.astype(BF16).reshape(n_src, 1, short, width)


def gated_rows(act, w_eo, owns):
    chunks = len(owns)
    n_src, _, short, _ = owns[0].shape
    total, ff = act.shape
    width = w_eo.shape[1]
    return pl.pallas_call(
        functools.partial(gated_kernel, chunks),
        grid=(chunks,),
        in_specs=[
            pl.BlockSpec((total // chunks, ff), lambda c: (c, 0)),
            pl.BlockSpec((ff, width), lambda c: (0, 0)),
        ]
        + [pl.BlockSpec(o.shape, lambda c: (0, 0, 0, 0)) for o in owns],
        out_specs=pl.BlockSpec((n_src, 1, short, width), lambda c: (0, c, 0, 0)),
        out_shape=jax.ShapeDtypeStruct((n_src, chunks, short, width), BF16),
        compiler_params=params(),
        cost_estimate=cost(2 * total * ff * width, 2 * total * (ff + width) + 2 * ff * width),
        name="gated_rows",
    )(act, w_eo, *owns)


def share_rows(me_g, n_g, full_ref, keep_ref, send_ref):
    rows = full_ref.shape[0] // n_g
    for r_g in range(n_g):
        at = pl.multiple_of((me_g ^ r_g) * rows, rows)
        out = send_ref if r_g & 1 else keep_ref
        block = full_ref[pl.ds(at, rows), :].astype(BF16)
        if len(out.shape) == 4:
            out[0, r_g // 2] = block
        else:
            out[r_g // 2] = block


def weight_kernel(n_g, me_ref, a_ref, o_ref, b0_ref, b1_ref, b2_ref, d_ref, keep_ref, send_ref, full_ref, at_ref, ot_ref):
    @pl.when(pl.program_id(0) == 0)
    def _():
        at_ref[...] = a_ref[...].T
        ot_ref[...] = o_ref[...].T

    for i, b in enumerate((b0_ref, b1_ref, b2_ref)):
        full_ref[:, i * LANES : (i + 1) * LANES] = dot_f32(at_ref[...], b[0], NN)
    full_ref[:, 3 * LANES :] = dot_f32(ot_ref[...], d_ref[...], NN)
    share_rows(me_ref[0], n_g, full_ref, keep_ref, send_ref)


def weight_grads(me, a_one, mixed, grad_qkv, grad_low, n_g, n_e):
    tok, width = a_one.shape
    heads_wide = width // LANES
    block = pl.BlockSpec((1, n_g // 2, width // n_g, 4 * LANES), lambda r, m: (r, 0, 0, 0))

    def plane(t):
        def index(r, m):
            at = 3 * (m[1] ^ r) + t
            return (at // heads_wide, 0, at % heads_wide)

        return pl.BlockSpec((1, tok, LANES), index)

    return pl.pallas_call(
        functools.partial(weight_kernel, n_g),
        grid_spec=pltpu.PrefetchScalarGridSpec(
            num_scalar_prefetch=1,
            grid=(n_e,),
            in_specs=[
                pl.BlockSpec((tok, width), lambda r, m: (0, 0)),
                pl.BlockSpec((tok, width), lambda r, m: (0, 0)),
                plane(0),
                plane(1),
                plane(2),
                pl.BlockSpec((tok, LANES), lambda r, m: (0, m[1] ^ r)),
            ],
            out_specs=[block, block],
            scratch_shapes=[
                pltpu.VMEM((width, 4 * LANES), F32),
                pltpu.VMEM((width, tok), BF16),
                pltpu.VMEM((width, tok), BF16),
            ],
        ),
        out_shape=[jax.ShapeDtypeStruct((n_e, n_g // 2, width // n_g, 4 * LANES), BF16)] * 2,
        compiler_params=params(),
        cost_estimate=cost(8 * tok * width * width, 12 * tok * width + 8 * width * width),
        name="weight_grads",
    )(me, a_one, mixed, grad_qkv, grad_qkv, grad_qkv, grad_low)


def relative(v, axis, me, n):
    return jnp.stack([lax.dynamic_index_in_dim(v, me ^ r, axis, keepdims=False) for r in range(n)], axis)


def own_blocks(view, me_g, me_e, n_g, n_e):
    view = relative(relative(view, 0, me_e, n_e), 1, me_g, n_g)
    return view[:, 0::2], view[:, 1::2]


def gate_up_kernel(half, n_part, *refs):
    parts, (g_ref, u_ref, out_ref, t_ref) = refs[:n_part], refs[n_part:]
    j = pl.program_id(0)

    @pl.when(j == 0)
    def _():
        at = 0
        for part in parts:
            t_ref[:, at : at + part.shape[0]] = part[...].T
            at += part.shape[0]

    @pl.when(j < half)
    def _():
        out_ref[...] = dot_f32(t_ref[...], g_ref[...], NN).astype(BF16)

    @pl.when(j >= half)
    def _():
        out_ref[...] = dot_f32(t_ref[...], u_ref[...], NN).astype(BF16)


def gate_up_grad(parts, dg, du):
    total, ff = dg.shape
    width = parts[0].shape[1]
    tile = 256
    half = ff // tile
    return pl.pallas_call(
        functools.partial(gate_up_kernel, half, len(parts)),
        grid=(2 * half,),
        in_specs=[pl.BlockSpec(p.shape, lambda j: (0, 0)) for p in parts]
        + [
            pl.BlockSpec((total, tile), lambda j: (0, jnp.minimum(j, half - 1))),
            pl.BlockSpec((total, tile), lambda j: (0, jnp.maximum(j - half, 0))),
        ],
        out_specs=pl.BlockSpec((width, tile), lambda j: (0, j)),
        scratch_shapes=[pltpu.VMEM((width, total), BF16)],
        out_shape=jax.ShapeDtypeStruct((width, 2 * ff), BF16),
        compiler_params=params(),
        cost_estimate=cost(4 * total * width * ff, 2 * total * (width + 2 * ff) + 4 * width * ff),
        name="gate_up_grad",
    )(*parts, dg, du)


def out_grad_kernel(n_part, act_ref, *refs):
    parts, out_ref = refs[:n_part], refs[n_part]
    total, at = None, 0
    for part in parts:
        n = part.shape[0]
        term = dot_f32(act_ref[at : at + n, :], part[...], TN)
        total = term if total is None else total + term
        at += n
    out_ref[...] = total.astype(BF16)


def out_grad(act, parts):
    total, ff = act.shape
    width = parts[0].shape[1]
    tile = 256
    return pl.pallas_call(
        functools.partial(out_grad_kernel, len(parts)),
        grid=(ff // tile,),
        in_specs=[pl.BlockSpec((total, tile), lambda j: (0, j))]
        + [pl.BlockSpec(p.shape, lambda j: (0, 0)) for p in parts],
        out_specs=pl.BlockSpec((tile, width), lambda j: (j, 0)),
        out_shape=jax.ShapeDtypeStruct((ff, width), BF16),
        compiler_params=params(),
        cost_estimate=cost(2 * total * width * ff, 2 * total * (width + ff) + 2 * width * ff),
        name="out_grad",
    )(act, *parts)


def fill_mask(start, length, mask_ref):
    tok = mask_ref.shape[0]
    query = lax.broadcasted_iota(jnp.int32, (tok, tok), 0)
    key = lax.broadcasted_iota(jnp.int32, (tok, tok), 1)
    end = start + length
    inside = (query >= start) & (query < end) & (key >= start) & (key < end)
    mask_ref[...] = jnp.where((key <= query) | inside, 0.0, -1e30)


def half_lanes(v, h):
    lane = lax.broadcasted_iota(jnp.int32, v.shape, 1)
    return jnp.where((lane >= LANES // 2) == (h == 1), v, jnp.zeros_like(v))


def forward_kernel(blk, scale, s_ref, q_ref, k_ref, v_ref, b_ref, o_ref, lse_ref, mask_ref):
    tok = q_ref.shape[0]
    pair = pl.program_id(0)

    @pl.when(pair == 0)
    def _():
        fill_mask(s_ref[2], s_ref[3], mask_ref)
        lse_ref[...] = jnp.zeros_like(lse_ref)

    lane = lax.broadcasted_iota(jnp.int32, (blk, LANES), 1)
    values = [half_lanes(v_ref[...], h) for h in range(2)]
    for i in range(tok // blk):
        rows = slice(i * blk, (i + 1) * blk)
        mixed, lse = None, lse_ref[rows, :]
        for h in range(2):
            q = half_lanes(q_ref[rows, :] * scale, h)
            s = dot_f32(q, k_ref[...], NT) + b_ref[h, rows, :].astype(F32) + mask_ref[rows, :]
            top = jnp.max(s, axis=-1, keepdims=True)
            e = jnp.exp(s - top)
            total = jnp.sum(e, axis=-1, keepdims=True)
            p = (e * (1.0 / total)).astype(BF16)
            o = dot_f32(p, values[h], NN)
            mixed = o if mixed is None else mixed + o
            lse = jnp.where(lane == 2 * pair + h, top + jnp.log(total), lse)
        o_ref[rows, :] = mixed.astype(BF16)
        lse_ref[rows, :] = lse


def attention_forward(scalars, qkv, rel_bias, scale):
    tok, width = qkv.shape[0], qkv.shape[1] // 3
    pairs = width // LANES
    column = lambda p: pl.BlockSpec((tok, LANES), lambda i, m: (0, p * pairs + i))
    return pl.pallas_call(
        functools.partial(forward_kernel, 128, scale),
        grid_spec=pltpu.PrefetchScalarGridSpec(
            num_scalar_prefetch=1,
            grid=(pairs,),
            in_specs=[
                column(0),
                column(1),
                column(2),
                pl.BlockSpec((2, tok, tok), lambda i, m: (i, 0, 0)),
            ],
            out_specs=[
                pl.BlockSpec((tok, LANES), lambda i, m: (0, i)),
                pl.BlockSpec((tok, LANES), lambda i, m: (0, 0)),
            ],
            scratch_shapes=[pltpu.VMEM((tok, tok), F32)],
        ),
        out_shape=[
            jax.ShapeDtypeStruct((tok, width), BF16),
            jax.ShapeDtypeStruct((tok, LANES), F32),
        ],
        compiler_params=params(),
        cost_estimate=cost(8 * tok * tok * width, 8 * tok * width + 32 * tok * tok, 16 * tok * tok),
        name="attention_forward",
    )(scalars, qkv, qkv, qkv, rel_bias)


def backward_kernel(n_g, scale, per_owner, s_ref, q_ref, k_ref, v_ref, do_ref, b_ref, lse_ref, *refs):
    outs, (dqkv_ref, mask_ref) = refs[:-2], refs[-2:]
    tok = q_ref.shape[0]
    rows = tok // n_g
    pair = s_ref[1] ^ pl.program_id(0) if per_owner else pl.program_id(0)

    @pl.when(pl.program_id(0) == 0)
    def _():
        fill_mask(s_ref[2], s_ref[3], mask_ref)

    lane = lax.broadcasted_iota(jnp.int32, (rows, LANES), 1)
    keys = [half_lanes(k_ref[...], h) for h in range(2)]
    grad_k = grad_v = None
    for r_g in range(n_g):
        at = pl.multiple_of((s_ref[0] ^ r_g) * rows, rows) if per_owner else r_g * rows
        here = pl.ds(at, rows)
        grad_q = None
        for h in range(2):
            q = half_lanes(q_ref[here, :] * scale, h)
            do = half_lanes(do_ref[here, :], h)
            lse = jnp.sum(jnp.where(lane == 2 * pair + h, lse_ref[here, :], 0.0), axis=-1, keepdims=True)
            s = dot_f32(q, k_ref[...], NT) + b_ref[h, here, :].astype(F32) + mask_ref[here, :]
            p = jnp.exp(s - lse)
            dp = dot_f32(do, v_ref[...], NT)
            ds = p * (dp - jnp.sum(p * dp, axis=-1, keepdims=True))
            ds = ds.astype(BF16)
            if per_owner:
                outs[r_g & 1][0, r_g // 2, h * rows : (h + 1) * rows, :] = ds
            else:
                outs[0][h, here, :] = ds
            dv = dot_f32(p.astype(BF16), do, TN)
            dk = dot_f32(ds, q, TN)
            dq = dot_f32(ds, keys[h], NN)
            grad_v = dv if grad_v is None else grad_v + dv
            grad_k = dk if grad_k is None else grad_k + dk
            grad_q = dq if grad_q is None else grad_q + dq
        dqkv_ref[0, here, :] = (grad_q * scale).astype(BF16)
    dqkv_ref[1] = grad_k.astype(BF16)
    dqkv_ref[2] = grad_v.astype(BF16)


def attention_backward(scalars, qkv, grad_mixed, rel_bias, lse, scale, n_g, n_e, per_owner):
    tok, width = grad_mixed.shape
    pairs = width // LANES
    turn = (lambda i, m: m[1] ^ i) if per_owner else (lambda i, m: i)
    column = lambda p: pl.BlockSpec((tok, LANES), lambda i, m: (0, p * pairs + turn(i, m)))
    if per_owner:
        block = pl.BlockSpec((1, n_g // 2, 2 * tok // n_g, tok), lambda i, m: (i, 0, 0, 0))
        bias_specs = [block, block]
        bias_shapes = [jax.ShapeDtypeStruct((n_e, n_g // 2, 2 * tok // n_g, tok), BF16)] * 2
    else:
        bias_specs = [pl.BlockSpec((2, tok, tok), lambda i, m: (i, 0, 0))]
        bias_shapes = [jax.ShapeDtypeStruct((2 * pairs, tok, tok), BF16)]
    return pl.pallas_call(
        functools.partial(backward_kernel, n_g, scale, per_owner),
        grid_spec=pltpu.PrefetchScalarGridSpec(
            num_scalar_prefetch=1,
            grid=(pairs,),
            in_specs=[
                column(0),
                column(1),
                column(2),
                column(0),
                pl.BlockSpec((2, tok, tok), lambda i, m: (turn(i, m), 0, 0)),
                pl.BlockSpec((tok, LANES), lambda i, m: (0, 0)),
            ],
            out_specs=bias_specs + [pl.BlockSpec((3, tok, LANES), lambda i, m: (0, 0, turn(i, m)))],
            scratch_shapes=[pltpu.VMEM((tok, tok), F32)],
        ),
        out_shape=bias_shapes + [jax.ShapeDtypeStruct((3, tok, width), BF16)],
        compiler_params=params(),
        cost_estimate=cost(20 * tok * tok * width, 16 * tok * width + 64 * tok * tok, 16 * tok * tok),
        name="attention_backward",
    )(scalars, qkv, qkv, qkv, grad_mixed, rel_bias, lse)


def norm_forward(values):
    inverse = lax.rsqrt(jnp.mean(values * values, axis=-1, keepdims=True) + EPSILON)
    return (values * inverse, inverse)


def norm_backward(grad_out, normed, inverse, norm_gain):
    grad_normed = grad_out * norm_gain
    grad_gain = jnp.sum(grad_out * normed, axis=0)
    grad_input = inverse * (
        grad_normed - normed * jnp.mean(grad_normed * normed, axis=-1, keepdims=True)
    )
    return (grad_input, grad_gain)


def body(
    tokens,
    cotangent,
    w_qkv,
    w_out_attn,
    rel_bias,
    norm_gains,
    w_router,
    w_gate_up,
    w_expert_out,
    routes,
    spans,
):
    tok, width = tokens.shape
    n_g, n_e = lax.axis_size("grp"), lax.axis_size("ep")
    assert w_gate_up.shape[0] == 1 and spans.shape[0] == 1 and tok == LENGTH
    assert n_g & (n_g - 1) == 0 and n_e & (n_e - 1) == 0 and n_g > 1 and n_e > 3
    assert width == HEADS * LANES // 2
    experts = n_e
    cap = 5 * routes.shape[1] * tok // (4 * experts)
    chunks = 2 if cap % 32 == 0 else 1
    short = cap // chunks
    slots = experts * cap
    scale = 1.0 / math.sqrt(width // HEADS)
    me_g, me_e = lax.axis_index("grp"), lax.axis_index("ep")
    me = jnp.stack([me_g, me_e, spans[0, 0], spans[0, 1]]).astype(jnp.int32)
    w_gu, w_eo = w_gate_up[0], w_expert_out[0]

    pos, cot_out = place(routes.T, cotangent, experts, cap, chunks)
    pos_cols = pos.T
    tokens = after(tokens, cot_out)
    cot_rows = swap_rows(cot_out)

    hidden = tokens.astype(F32)
    normed_one, inverse_one = norm_forward(hidden)
    a_one = (normed_one * norm_gains[0]).astype(BF16)
    qkv_rows = dot_f32(a_one, w_qkv, NN).astype(BF16)
    mixed_heads, lse = attention_forward(me, qkv_rows, rel_bias, scale)
    after_attn = hidden + dot_f32(mixed_heads, w_out_attn, NN)
    normed_two, _ = norm_forward(after_attn)
    a_two = (normed_two * norm_gains[1]).astype(BF16)

    parts = dispatch(pos, after(a_two, cot_rows), slots, chunks)
    dact = dot_f32(cot_rows, w_eo, NT).astype(BF16)
    parts = [swap_rows(p if c == 0 else after(p, dact)) for c, p in enumerate(parts)]
    dact = dact.reshape(n_e, chunks, short, -1)
    cot_view = cot_rows.reshape(n_e, chunks, short, width)
    wr_pad = jnp.pad(w_router, ((0, 0), (0, LANES - experts)))
    wr_pad_t = wr_pad.T
    state, back, deos, owns, grad_route = None, [], [], [], 0.0
    for c in range(chunks):
        state, (dxe, deo, own, gr) = expert_chunk(
            me, parts[c], cot_view, dact, w_gu, wr_pad, wr_pad_t, experts, c, slots, state
        )
        back.append(swap_rows(dxe))
        deos.append(deo)
        owns.append(own)
        grad_route = grad_route + gr[:experts]
    act, dg, du = state

    core = ("grp", 1)
    share = lambda v: lax.psum_scatter(v, "grp", scatter_dimension=0, tiled=True)
    gated = gated_rows(after(act, *back[:-1]), w_eo, owns).reshape(slots, width)
    gate_full = gate_up_grad(parts, after(dg, gated), du)
    gate = share(after(gate_full, *back))

    grad_after, grad_attn_low, grad_gain_two = return_grads(
        pos_cols, after(after_attn, gate_full), cotangent, norm_gains[1:], back
    )
    gated = swap_rows(after(gated, *back))
    grad_mixed = dot_f32(grad_attn_low, w_out_attn, NT).astype(BF16)
    rows_g, rows_t = width // n_g, tok // n_g
    per_owner = n_e * LANES == width
    orders = halving_orders(n_g, n_e)
    *grad_bias, grad_qkv = attention_backward(
        me, qkv_rows, grad_mixed, rel_bias, lse, scale, n_g, n_e, per_owner
    )
    if not per_owner:
        bias = grad_bias[0].reshape(n_e, HEADS // n_e, n_g, rows_t, tok).transpose(0, 2, 1, 3, 4)
        grad_bias = own_blocks(bias.reshape(n_e, n_g, -1, tok), me_g, me_e, n_g, n_e)
    got = xor_send(grad_bias[1], *core)
    grad_a_one = sum(
        dot_f32(grad_qkv[i], w_qkv[:, i * width : (i + 1) * width], NT) for i in range(3)
    )
    bias = first_sums(after(grad_bias[0], grad_a_one), got, orders)
    grad_qkv_late = after(grad_qkv, bias[0][0])
    bias = send_all(bias)
    if per_owner:
        weights = weight_grads(me, a_one, mixed_heads, grad_qkv_late, grad_attn_low, n_g, n_e)
    else:
        flat = jnp.concatenate([grad_qkv_late[i] for i in range(3)], axis=1)
        full = [dot_f32(a_one, flat, TN), dot_f32(mixed_heads, grad_attn_low, TN)]
        full = [f.astype(BF16).reshape(n_g, rows_g, n_e, -1) for f in full]
        full = jnp.concatenate(full, axis=-1).transpose(2, 0, 1, 3)
        weights = own_blocks(full, me_g, me_e, n_g, n_e)
    out_full = out_grad(act, [after(deos[0], weights[0])] + deos[1:])
    got = xor_send(after(weights[1], *[way[1] for way in bias]), *core)
    weights = first_sums(after(weights[0], out_full), got, orders)
    first_keep = weights[0][0]
    expert_out = share(after(out_full, first_keep))
    weights = send_all(weights)
    output = combine(pos_cols, after(after_attn, first_keep), gated)
    grad_norm_one, grad_gain_one = norm_backward(grad_a_one, normed_one, inverse_one, norm_gains[0])
    grad_tokens = grad_after + grad_norm_one
    small = jnp.concatenate([grad_gain_one[None], grad_gain_two, grad_route])
    for axis, k in [("grp", k) for k in bits_of(n_g)] + [("ep", k) for k in bits_of(n_e)]:
        small = small + xor_send(small, axis, k)
    grad_w_gate = after(gate, first_keep).astype(F32)[None]
    wide = 3 * width // n_e
    merged = [[bias, weights]] if bias[0][0].shape == weights[0][0].shape else [[bias], [weights]]
    ways = [send_all(next_sums(sets)) for sets in merged]
    ways[0] = tied(ways[0], grad_w_gate, grad_tokens)
    while ways[0][0][2]:
        if len(ways[0][0][2]) == 1:
            ways[0] = tied(ways[0], output)
        ways = [send_all(next_sums([w])) for w in ways]
    grad_w_expert = expert_out.astype(F32)[None]
    ways[0] = tied(ways[0], grad_w_expert)
    if len(ways) == 1:
        g_bias, g_qkv, g_out = last_merged(ways[0], wide)
    else:
        g_bias, g_weights = [jnp.concatenate(last_sums(w)) for w in ways]
        g_qkv, g_out = g_weights[:, :wide], g_weights[:, wide:]
    g_bias = g_bias.reshape(HEADS // n_e, rows_t, tok)
    return (
        output,
        grad_tokens,
        g_qkv,
        g_out,
        g_bias,
        small[:2],
        small[2:].T,
        grad_w_gate,
        grad_w_expert,
    )


def solution(mesh):
    placed = (
        P(("grp", "ep"), None),
        P(("grp", "ep"), None),
        P(),
        P(),
        P(),
        P(),
        P(),
        P("ep", None, None),
        P("ep", None, None),
        P(("grp", "ep"), None),
        P(("grp", "ep"), None),
    )
    return jax.shard_map(
        body,
        mesh=mesh,
        in_specs=placed,
        out_specs=(
            P(("grp", "ep"), None),
            P(("grp", "ep"), None),
            P("grp", "ep"),
            P("grp", "ep"),
            P("ep", "grp", None),
            P(),
            P(),
            P("ep", "grp", None),
            P("ep", "grp", None),
        ),
        check_vma=False,
    )
```

```python
import functools
import math

import jax
import jax.numpy as jnp
from jax import lax
from jax.experimental import pallas as pl
from jax.experimental.pallas import tpu as pltpu
from jax.sharding import PartitionSpec as P

HEADS = 16
LENGTH = 512
EPSILON = 1e-06
LANES = 128
GELU_C = math.sqrt(2.0 / math.pi)
GELU_A = 0.044715
F32 = jnp.float32
BF16 = jnp.bfloat16
VMEM_LIMIT = 60 * 1024 * 1024


def params(**kw):
    return pltpu.CompilerParams(vmem_limit_bytes=VMEM_LIMIT, **kw)


def cost(flops, nbytes, trans=0):
    return pl.CostEstimate(flops=int(flops), bytes_accessed=int(nbytes), transcendentals=int(trans))


def dot_f32(a, b, dims):
    return lax.dot_general(a, b, (dims, ((), ())), preferred_element_type=F32)


NN = ((1,), (0,))
NT = ((1,), (1,))
TN = ((0,), (0,))


def xor_send(v, axis, k):
    n = lax.axis_size(axis)
    return lax.ppermute(v, axis, [(i, i ^ k) for i in range(n)])


def swap_rows(v):
    return lax.all_to_all(v, "ep", split_axis=0, concat_axis=0, tiled=True)


def bits_of(n):
    return [1 << i for i in range(n.bit_length() - 1)]


def after(value, *others):
    return lax.optimization_barrier((value, *others))[0]


def halving_orders(n_g, n_e):
    g_bits = [("grp", k) for k in bits_of(n_g)]
    e_bits = [("ep", k) for k in bits_of(n_e)]
    rest, first, others = g_bits[1:], e_bits[:1], e_bits[1:]
    return [first + rest + others, others + first + rest, rest + first + others]


def row_cuts(rows):
    unit = rows // 16
    return [0, 16 * round(7 * unit / 16), 16 * round(11 * unit / 16), rows]


def first_kernel(orders, cuts, k_ref, g_ref, *outs):
    r = pl.program_id(0)
    bit = lambda x, axis, k: (2 * x // k) % 2 if axis == "grp" else (r // k) % 2
    for x in range(k_ref.shape[1]):
        at = 0
        for order, lo, hi in zip(orders, cuts, cuts[1:]):
            if lo == hi:
                continue
            total = (k_ref[0, x, lo:hi, :].astype(F32) + g_ref[0, x, lo:hi, :].astype(F32)).astype(BF16)
            index = 0
            for step in order[1:]:
                index = 2 * index + bit(x, *step)
            goes = bit(x, *order[0])
            for side in range(2):

                @pl.when(goes == side)
                def _():
                    outs[at + side][index] = total

            at += 2


def first_sums(keep, got, orders):
    n_e, n_x, rows, cols = keep.shape
    cuts = row_cuts(rows)
    used = [(o, hi - lo) for o, lo, hi in zip(orders, cuts, cuts[1:]) if hi > lo]
    half = n_e * n_x // 2
    shapes = [jax.ShapeDtypeStruct((half, n, cols), BF16) for _, n in used for _ in range(2)]
    out = pl.pallas_call(
        functools.partial(first_kernel, orders, cuts),
        grid=(n_e,),
        in_specs=[pl.BlockSpec((1, n_x, rows, cols), lambda r: (r, 0, 0, 0))] * 2,
        out_specs=[pl.BlockSpec(s.shape, lambda r: (0, 0, 0)) for s in shapes],
        out_shape=shapes,
        compiler_params=params(),
        cost_estimate=cost(n_e * n_x * rows * cols, 6 * n_e * n_x * rows * cols),
        name="first_sums",
    )(keep, got)
    return [(out[2 * i], out[2 * i + 1], o) for i, (o, _) in enumerate(used)]


def split_kernel(n_way, n_set, n_small, *refs):
    ins, refs = refs[: 2 * n_way * n_set], refs[2 * n_way * n_set :]
    small, outs = refs[: 2 * n_small], refs[2 * n_small :]
    if n_small:
        outs[-1][...] = small[0][...] + small[1][...]
    for w in range(n_way):
        keep_ref, send_ref = outs[2 * w : 2 * w + 2]
        half, at = keep_ref.shape[0], 0
        for i in range(n_set):
            k_ref, g_ref = ins[2 * (w * n_set + i) : 2 * (w * n_set + i) + 2]
            to = at + k_ref.shape[1]
            keep_ref[:, at:to, :] = (k_ref[:half].astype(F32) + g_ref[:half].astype(F32)).astype(BF16)
            send_ref[:, at:to, :] = (k_ref[half:].astype(F32) + g_ref[half:].astype(F32)).astype(BF16)
            at = to


def next_sums(sets, small=()):
    ways = list(zip(*sets))
    shapes = []
    for way in ways:
        blocks, _, cols = way[0][0].shape
        shape = jax.ShapeDtypeStruct((blocks // 2, sum(one[0].shape[1] for one in way), cols), BF16)
        shapes += [shape, shape]
    ins = [v for way in ways for one in way for v in one[:2]]
    total = sum(math.prod(s.shape) for s in shapes)
    out = pl.pallas_call(
        functools.partial(split_kernel, len(ways), len(sets), len(small) // 2),
        out_shape=shapes + [jax.ShapeDtypeStruct(v.shape, v.dtype) for v in small[:1]],
        compiler_params=params(),
        cost_estimate=cost(total, 6 * total),
        name="split_sums",
    )(*ins, *small)
    ways = [(out[2 * i], out[2 * i + 1], way[0][2]) for i, way in enumerate(ways)]
    return ways, out[2 * len(ways) :]


def send_all(ways):
    return [(keep, xor_send(send, *order[0]), order[1:]) for keep, send, order in ways]


def last_sums(ways):
    return [(keep[0].astype(F32) + got[0].astype(F32)) for keep, got, _ in ways]


def last_kernel(*refs):
    ins, (bias_ref, qkv_ref, out_ref) = refs[:-3], refs[-3:]
    wide = qkv_ref.shape[1]
    at = 0
    for k_ref, g_ref in zip(ins[0::2], ins[1::2]):
        n = k_ref.shape[1] // 2
        total = k_ref[0].astype(F32) + g_ref[0].astype(F32)
        bias_ref[at : at + n, :] = total[:n]
        qkv_ref[at : at + n, :] = total[n:, :wide]
        out_ref[at : at + n, :] = total[n:, wide:]
        at += n


def last_merged(ways, wide):
    rows, cols = sum(w[0].shape[1] for w in ways) // 2, ways[0][0].shape[2]
    return pl.pallas_call(
        last_kernel,
        out_shape=[jax.ShapeDtypeStruct((rows, n), F32) for n in (cols, wide, cols - wide)],
        compiler_params=params(),
        cost_estimate=cost(2 * rows * cols, 16 * rows * cols),
        name="last_sums",
    )(*[v for w in ways for v in w[:2]])


def tied(ways, *others):
    return [(after(ways[0][0], *others), *ways[0][1:])] + ways[1:]


def place_kernel(experts, cap, chunks, routes_ref, v_ref, pos_ref, out_ref):
    tok = v_ref.shape[0]
    short = cap // chunks
    ids = lax.broadcasted_iota(jnp.int32, (LANES, tok), 0)
    named = [ids == routes_ref[k : k + 1, :] for k in range(2)]
    counts = jnp.where(named[0] | named[1], 1.0, 0.0).astype(BF16)
    before = lax.broadcasted_iota(jnp.int32, (tok, tok), 0) < lax.broadcasted_iota(
        jnp.int32, (tok, tok), 1
    )
    earlier = dot_f32(counts, jnp.where(before, 1.0, 0.0).astype(BF16), NN)
    for k in range(2):
        slot = jnp.sum(jnp.where(named[k], earlier, 0.0), axis=0, keepdims=True).astype(jnp.int32)
        owner = routes_ref[k : k + 1, :]
        pos_ref[k : k + 1, :] = owner * cap + slot
        chunk = jnp.zeros_like(slot)
        for c in range(1, chunks):
            chunk += jnp.where(slot >= c * short, 1, 0)
        pos_ref[2 + k : 3 + k, :] = chunk * (experts * short) + owner * short + slot - chunk * short
    first, second = pos_ref[0:1, :], pos_ref[1:2, :]
    rows = lax.broadcasted_iota(jnp.int32, (cap, tok), 0)
    for e in range(experts):
        here = rows + e * cap
        pick = jnp.where((here == first) | (here == second), 1.0, 0.0).astype(BF16)
        out_ref[e * cap : (e + 1) * cap, :] = dot_f32(pick, v_ref[...], NN).astype(BF16)


def place(routes_t, values, experts, cap, chunks):
    tok, width = values.shape
    return pl.pallas_call(
        functools.partial(place_kernel, experts, cap, chunks),
        out_shape=[
            jax.ShapeDtypeStruct((4, tok), jnp.int32),
            jax.ShapeDtypeStruct((experts * cap, width), BF16),
        ],
        compiler_params=params(),
        cost_estimate=cost(2 * experts * cap * tok * width, 2 * tok * width + 2 * experts * cap * width),
        name="place_rows",
    )(routes_t, values)


def dispatch_kernel(pos_ref, v_ref, *outs):
    tok = v_ref.shape[0]
    first, second = pos_ref[2:3, :], pos_ref[3:4, :]
    at = 0
    for out in outs:
        total = out.shape[0]
        step = total // 4
        rows = lax.broadcasted_iota(jnp.int32, (step, tok), 0)
        for b in range(4):
            here = rows + at
            pick = jnp.where((here == first) | (here == second), 1.0, 0.0).astype(BF16)
            out[b * step : (b + 1) * step, :] = dot_f32(pick, v_ref[...], NN).astype(BF16)
            at += step


def dispatch(pos, values, slots, chunks):
    tok, width = values.shape
    return pl.pallas_call(
        dispatch_kernel,
        out_shape=[jax.ShapeDtypeStruct((slots // chunks, width), BF16)] * chunks,
        compiler_params=params(),
        cost_estimate=cost(2 * slots * tok * width, 2 * tok * width + 2 * slots * width),
        name="dispatch_rows",
    )(pos, values)


def gathered(first, second, parts):
    total, at = None, 0
    for part in parts:
        n = part.shape[0]
        here = lax.broadcasted_iota(jnp.int32, (first.shape[0], n), 1) + at
        pick = jnp.where((here == first) | (here == second), 1.0, 0.0).astype(BF16)
        term = dot_f32(pick, part[...], NN)
        total = term if total is None else total + term
        at += n
    return total


def combine_kernel(pos_ref, x_ref, *refs):
    parts, out_ref = refs[:-1], refs[-1]
    out_ref[...] = x_ref[...] + gathered(pos_ref[:, 2:3], pos_ref[:, 3:4], parts)


def combine(pos_cols, after_attn, gated):
    tok, width = after_attn.shape
    blk = 256
    return pl.pallas_call(
        combine_kernel,
        grid=(tok // blk,),
        in_specs=[
            pl.BlockSpec((blk, 4), lambda i: (i, 0)),
            pl.BlockSpec((blk, width), lambda i: (i, 0)),
        ]
        + [pl.BlockSpec(g.shape, lambda i: (0, 0)) for g in gated],
        out_specs=pl.BlockSpec((blk, width), lambda i: (i, 0)),
        out_shape=jax.ShapeDtypeStruct((tok, width), F32),
        compiler_params=params(),
        cost_estimate=cost(4 * tok * gated[0].shape[0] * width, 10 * tok * width),
        name="combine_rows",
    )(pos_cols, after_attn, *gated)


def return_kernel(pos_ref, x_ref, cot_ref, gain_ref, *refs):
    parts, (dx_ref, low_ref, gg_ref) = refs[:-3], refs[-3:]
    grad = gathered(pos_ref[:, 2:3], pos_ref[:, 3:4], parts)
    x = x_ref[...]
    inverse = lax.rsqrt(jnp.mean(x * x, axis=-1, keepdims=True) + EPSILON)
    normed = x * inverse
    grad_normed = grad * gain_ref[...]
    dx = cot_ref[...].astype(F32) + inverse * (
        grad_normed - normed * jnp.mean(grad_normed * normed, axis=-1, keepdims=True)
    )
    dx_ref[...] = dx
    low_ref[...] = dx.astype(BF16)

    @pl.when(pl.program_id(0) == 0)
    def _():
        gg_ref[...] = jnp.zeros_like(gg_ref)

    gg_ref[...] += jnp.sum(grad * normed, axis=0, keepdims=True)


def return_grads(pos_cols, after_attn, cotangent, gain, parts):
    tok, width = after_attn.shape
    blk = 256
    row = pl.BlockSpec((blk, width), lambda i: (i, 0))
    one = pl.BlockSpec((1, width), lambda i: (0, 0))
    slots = sum(p.shape[0] for p in parts)
    return pl.pallas_call(
        return_kernel,
        grid=(tok // blk,),
        in_specs=[pl.BlockSpec((blk, 4), lambda i: (i, 0)), row, row, one]
        + [pl.BlockSpec(p.shape, lambda i: (0, 0)) for p in parts],
        out_specs=[row, row, one],
        out_shape=[
            jax.ShapeDtypeStruct((tok, width), F32),
            jax.ShapeDtypeStruct((tok, width), BF16),
            jax.ShapeDtypeStruct((1, width), F32),
        ],
        compiler_params=params(),
        cost_estimate=cost(2 * tok * slots * width, 16 * tok * width),
        name="return_rows",
    )(pos_cols, after_attn, cotangent, gain, *parts)


def expert_kernel(experts, aliased, *refs):
    me_ref, x_ref, c_ref, d_ref, wg_ref, wu_ref, wr_ref, wrt_ref = refs[:8]
    refs = refs[8 + (3 if aliased else 0) :]
    act_ref, dg_ref, du_ref, out_ref, deo_ref, own_ref, gr_ref = refs[:7]
    acc_ref, gate_ref, prob_ref, p_ref = refs[7:]
    j = pl.program_id(0)
    rows_all = x_ref.shape[0]
    n_src, _, short, tile = d_ref.shape
    width = x_ref.shape[1]
    lane = lax.broadcasted_iota(jnp.int32, (rows_all, LANES), 1)

    @pl.when(j == 0)
    def _():
        logits = dot_f32(x_ref[...], wr_ref[...], NN)
        logits = jnp.where(lane < experts, logits, -1e30)
        exps = jnp.exp(logits - jnp.max(logits, axis=-1, keepdims=True))
        probs = exps / jnp.sum(exps, axis=-1, keepdims=True)
        prob_ref[...] = probs
        own = jnp.sum(jnp.where(lane == me_ref[1], probs, 0.0), axis=-1, keepdims=True)
        p_ref[...] = jnp.broadcast_to(own, p_ref.shape)
        own_ref[...] = p_ref[...].reshape(n_src, 1, short, LANES)
        wide = jnp.concatenate([p_ref[...]] * (width // LANES), axis=1)
        deo_ref[...] = (c_ref[...].reshape(rows_all, width).astype(F32) * wide).astype(BF16)
        acc_ref[...] = jnp.zeros_like(acc_ref)
        gate_ref[...] = jnp.zeros_like(gate_ref)

    n_blk = n_src // 2
    for b in range(n_blk):
        rows = slice(2 * b * short, 2 * (b + 1) * short)
        x = x_ref[rows, :]
        z = dot_f32(x, wg_ref[...], NN)
        up = dot_f32(x, wu_ref[...], NN)
        back = d_ref[2 * b : 2 * b + 2].reshape(2 * short, tile).astype(F32)
        reps = tile // LANES
        own = jnp.concatenate([p_ref[rows, :]] * reps, axis=1)
        zz = z * z
        th = jnp.tanh(GELU_C * z * (1.0 + GELU_A * zz))
        half = 0.5 + 0.5 * th
        gelu = z * half
        slope = half + 0.5 * GELU_C * z * (1.0 - th * th) * (1.0 + 3.0 * GELU_A * zz)
        act = (gelu * up).astype(BF16)
        act_ref[rows, :] = act
        share = act.astype(F32) * back
        gate_ref[rows, :] += sum(share[:, i * LANES : (i + 1) * LANES] for i in range(reps))
        dact = back * own
        dg = (dact * up * slope).astype(BF16)
        du = (dact * gelu).astype(BF16)
        dg_ref[rows, :] = dg
        du_ref[rows, :] = du
        acc_ref[rows, :] += dot_f32(dg, wg_ref[...], NT) + dot_f32(du, wu_ref[...], NT)

    @pl.when(j == pl.num_programs(0) - 1)
    def _():
        dgate = jnp.sum(gate_ref[...], axis=-1, keepdims=True)
        dl = dgate * p_ref[...] * (jnp.where(lane == me_ref[1], 1.0, 0.0) - prob_ref[...])
        dl = dl.astype(BF16)
        out_ref[...] = (acc_ref[...] + dot_f32(dl, wrt_ref[...], NN)).astype(BF16)
        gr_ref[...] = dot_f32(dl, x_ref[...], TN)[: gr_ref.shape[0], :]


def expert_chunk(me, rows, cot, dact, w_gate_up, wr_pad, wr_pad_t, experts, c, total_rows, earlier):
    n_src, chunks, short, width = cot.shape
    ff = dact.shape[-1]
    tile = 256
    steps = ff // tile
    n_rows = rows.shape[0]
    whole = pl.BlockSpec(memory_space=pl.ANY)
    part = pl.BlockSpec((n_rows, tile), lambda j, m: (c, j))
    aliased = earlier is not None
    few = -(-experts // 8) * 8
    call = pl.pallas_call(
        functools.partial(expert_kernel, experts, aliased),
        grid_spec=pltpu.PrefetchScalarGridSpec(
            num_scalar_prefetch=1,
            grid=(steps,),
            in_specs=[
                pl.BlockSpec((n_rows, width), lambda j, m: (0, 0)),
                pl.BlockSpec((n_src, 1, short, width), lambda j, m: (0, c, 0, 0)),
                pl.BlockSpec((n_src, 1, short, tile), lambda j, m: (0, c, 0, j)),
                pl.BlockSpec((width, tile), lambda j, m: (0, j)),
                pl.BlockSpec((width, tile), lambda j, m: (0, j + steps)),
                pl.BlockSpec((width, LANES), lambda j, m: (0, 0)),
                pl.BlockSpec((LANES, width), lambda j, m: (0, 0)),
            ]
            + ([whole] * 3 if aliased else []),
            out_specs=[
                part,
                part,
                part,
                pl.BlockSpec((n_rows, width), lambda j, m: (0, 0)),
                pl.BlockSpec((n_rows, width), lambda j, m: (0, 0)),
                pl.BlockSpec((n_src, 1, short, LANES), lambda j, m: (0, 0, 0, 0)),
                pl.BlockSpec((few, width), lambda j, m: (0, 0)),
            ],
            scratch_shapes=[
                pltpu.VMEM((n_rows, width), F32),
                pltpu.VMEM((n_rows, LANES), F32),
                pltpu.VMEM((n_rows, LANES), F32),
                pltpu.VMEM((n_rows, LANES), F32),
            ],
        ),
        out_shape=[jax.ShapeDtypeStruct((total_rows, ff), BF16)] * 3
        + [
            jax.ShapeDtypeStruct((n_rows, width), BF16),
            jax.ShapeDtypeStruct((n_rows, width), BF16),
            jax.ShapeDtypeStruct((n_src, 1, short, LANES), F32),
            jax.ShapeDtypeStruct((few, width), F32),
        ],
        input_output_aliases={8: 0, 9: 1, 10: 2} if aliased else {},
        compiler_params=params(),
        cost_estimate=cost(
            8 * n_rows * width * ff, 4 * width * ff + 10 * n_rows * ff + 4 * n_rows * width, n_rows * ff
        ),
        name="expert_rows",
    )
    out = call(me, rows, cot, dact, w_gate_up, w_gate_up, wr_pad, wr_pad_t, *(earlier if aliased else ()))
    return out[:3], out[3:]


def gated_kernel(act_ref, w_ref, own_ref, out_ref):
    n_rows, tile = out_ref.shape
    own = jnp.concatenate([own_ref[...].reshape(n_rows, LANES)] * (tile // LANES), axis=1)
    out_ref[...] = (dot_f32(act_ref[...], w_ref[...], NN) * own).astype(BF16)


def gated_rows(act, w_eo, own, c, chunks):
    total, ff = act.shape
    width = w_eo.shape[1]
    n_rows, tile = total // chunks, 256
    return pl.pallas_call(
        gated_kernel,
        grid=(width // tile,),
        in_specs=[
            pl.BlockSpec((n_rows, ff), lambda j: (c, 0)),
            pl.BlockSpec((ff, tile), lambda j: (0, j)),
            pl.BlockSpec(own.shape, lambda j: (0, 0, 0, 0)),
        ],
        out_specs=pl.BlockSpec((n_rows, tile), lambda j: (0, j)),
        out_shape=jax.ShapeDtypeStruct((n_rows, width), BF16),
        compiler_params=params(),
        cost_estimate=cost(2 * n_rows * ff * width, 2 * n_rows * (ff + width) + 2 * ff * width),
        name="gated_rows",
    )(act, w_eo, own)


def share_rows(me_g, n_g, full_ref, keep_ref, send_ref):
    rows = full_ref.shape[0] // n_g
    for r_g in range(n_g):
        at = pl.multiple_of((me_g ^ r_g) * rows, rows)
        out = send_ref if r_g & 1 else keep_ref
        block = full_ref[pl.ds(at, rows), :].astype(BF16)
        if len(out.shape) == 4:
            out[0, r_g // 2] = block
        else:
            out[r_g // 2] = block


def weight_kernel(n_g, me_ref, a_ref, o_ref, b0_ref, b1_ref, b2_ref, d_ref, keep_ref, send_ref, full_ref, at_ref, ot_ref):
    @pl.when(pl.program_id(0) == 0)
    def _():
        at_ref[...] = a_ref[...].T
        ot_ref[...] = o_ref[...].T

    for i, b in enumerate((b0_ref, b1_ref, b2_ref)):
        full_ref[:, i * LANES : (i + 1) * LANES] = dot_f32(at_ref[...], b[0], NN)
    full_ref[:, 3 * LANES :] = dot_f32(ot_ref[...], d_ref[...], NN)
    share_rows(me_ref[0], n_g, full_ref, keep_ref, send_ref)


def weight_grads(me, a_one, mixed, grad_qkv, grad_low, n_g, n_e):
    tok, width = a_one.shape
    heads_wide = width // LANES
    block = pl.BlockSpec((1, n_g // 2, width // n_g, 4 * LANES), lambda r, m: (r, 0, 0, 0))

    def plane(t):
        def index(r, m):
            at = 3 * (m[1] ^ r) + t
            return (at // heads_wide, 0, at % heads_wide)

        return pl.BlockSpec((1, tok, LANES), index)

    return pl.pallas_call(
        functools.partial(weight_kernel, n_g),
        grid_spec=pltpu.PrefetchScalarGridSpec(
            num_scalar_prefetch=1,
            grid=(n_e,),
            in_specs=[
                pl.BlockSpec((tok, width), lambda r, m: (0, 0)),
                pl.BlockSpec((tok, width), lambda r, m: (0, 0)),
                plane(0),
                plane(1),
                plane(2),
                pl.BlockSpec((tok, LANES), lambda r, m: (0, m[1] ^ r)),
            ],
            out_specs=[block, block],
            scratch_shapes=[
                pltpu.VMEM((width, 4 * LANES), F32),
                pltpu.VMEM((width, tok), BF16),
                pltpu.VMEM((width, tok), BF16),
            ],
        ),
        out_shape=[jax.ShapeDtypeStruct((n_e, n_g // 2, width // n_g, 4 * LANES), BF16)] * 2,
        compiler_params=params(),
        cost_estimate=cost(8 * tok * width * width, 12 * tok * width + 8 * width * width),
        name="weight_grads",
    )(me, a_one, mixed, grad_qkv, grad_qkv, grad_qkv, grad_low)


def relative(v, axis, me, n):
    return jnp.stack([lax.dynamic_index_in_dim(v, me ^ r, axis, keepdims=False) for r in range(n)], axis)


def own_blocks(view, me_g, me_e, n_g, n_e):
    view = relative(relative(view, 0, me_e, n_e), 1, me_g, n_g)
    return view[:, 0::2], view[:, 1::2]


def gate_up_kernel(half, n_part, *refs):
    parts, (g_ref, u_ref, out_ref, t_ref) = refs[:n_part], refs[n_part:]
    j = pl.program_id(0)

    @pl.when(j == 0)
    def _():
        at = 0
        for part in parts:
            t_ref[:, at : at + part.shape[0]] = part[...].T
            at += part.shape[0]

    @pl.when(j < half)
    def _():
        out_ref[...] = dot_f32(t_ref[...], g_ref[...], NN).astype(BF16)

    @pl.when(j >= half)
    def _():
        out_ref[...] = dot_f32(t_ref[...], u_ref[...], NN).astype(BF16)


def gate_up_grad(parts, dg, du):
    total, ff = dg.shape
    width = parts[0].shape[1]
    tile = 256
    half = ff // tile
    return pl.pallas_call(
        functools.partial(gate_up_kernel, half, len(parts)),
        grid=(2 * half,),
        in_specs=[pl.BlockSpec(p.shape, lambda j: (0, 0)) for p in parts]
        + [
            pl.BlockSpec((total, tile), lambda j: (0, jnp.minimum(j, half - 1))),
            pl.BlockSpec((total, tile), lambda j: (0, jnp.maximum(j - half, 0))),
        ],
        out_specs=pl.BlockSpec((width, tile), lambda j: (0, j)),
        scratch_shapes=[pltpu.VMEM((width, total), BF16)],
        out_shape=jax.ShapeDtypeStruct((width, 2 * ff), BF16),
        compiler_params=params(),
        cost_estimate=cost(4 * total * width * ff, 2 * total * (width + 2 * ff) + 4 * width * ff),
        name="gate_up_grad",
    )(*parts, dg, du)


def out_grad_kernel(n_part, act_ref, *refs):
    parts, out_ref = refs[:n_part], refs[n_part]
    total, at = None, 0
    for part in parts:
        n = part.shape[0]
        term = dot_f32(act_ref[at : at + n, :], part[...], TN)
        total = term if total is None else total + term
        at += n
    out_ref[...] = total.astype(BF16)


def out_grad(act, parts):
    total, ff = act.shape
    width = parts[0].shape[1]
    tile = 256
    return pl.pallas_call(
        functools.partial(out_grad_kernel, len(parts)),
        grid=(ff // tile,),
        in_specs=[pl.BlockSpec((total, tile), lambda j: (0, j))]
        + [pl.BlockSpec(p.shape, lambda j: (0, 0)) for p in parts],
        out_specs=pl.BlockSpec((tile, width), lambda j: (j, 0)),
        out_shape=jax.ShapeDtypeStruct((ff, width), BF16),
        compiler_params=params(),
        cost_estimate=cost(2 * total * width * ff, 2 * total * (width + ff) + 2 * width * ff),
        name="out_grad",
    )(act, *parts)


def fill_mask(start, length, mask_ref):
    tok = mask_ref.shape[0]
    query = lax.broadcasted_iota(jnp.int32, (tok, tok), 0)
    key = lax.broadcasted_iota(jnp.int32, (tok, tok), 1)
    end = start + length
    inside = (query >= start) & (query < end) & (key >= start) & (key < end)
    mask_ref[...] = jnp.where((key <= query) | inside, 0.0, -1e30)


def half_lanes(v, h):
    lane = lax.broadcasted_iota(jnp.int32, v.shape, 1)
    return jnp.where((lane >= LANES // 2) == (h == 1), v, jnp.zeros_like(v))


def forward_kernel(blk, scale, s_ref, q_ref, k_ref, v_ref, b_ref, o_ref, lse_ref, mask_ref):
    tok = q_ref.shape[0]
    pair = pl.program_id(0)

    @pl.when(pair == 0)
    def _():
        fill_mask(s_ref[2], s_ref[3], mask_ref)
        lse_ref[...] = jnp.zeros_like(lse_ref)

    lane = lax.broadcasted_iota(jnp.int32, (blk, LANES), 1)
    values = [half_lanes(v_ref[...], h) for h in range(2)]
    for i in range(tok // blk):
        rows = slice(i * blk, (i + 1) * blk)
        mixed, lse = None, lse_ref[rows, :]
        for h in range(2):
            q = half_lanes(q_ref[rows, :] * scale, h)
            s = dot_f32(q, k_ref[...], NT) + b_ref[h, rows, :].astype(F32) + mask_ref[rows, :]
            top = jnp.max(s, axis=-1, keepdims=True)
            e = jnp.exp(s - top)
            total = jnp.sum(e, axis=-1, keepdims=True)
            p = (e * (1.0 / total)).astype(BF16)
            o = dot_f32(p, values[h], NN)
            mixed = o if mixed is None else mixed + o
            lse = jnp.where(lane == 2 * pair + h, top + jnp.log(total), lse)
        o_ref[rows, :] = mixed.astype(BF16)
        lse_ref[rows, :] = lse


def attention_forward(scalars, qkv, rel_bias, scale):
    tok, width = qkv.shape[0], qkv.shape[1] // 3
    pairs = width // LANES
    column = lambda p: pl.BlockSpec((tok, LANES), lambda i, m: (0, p * pairs + i))
    return pl.pallas_call(
        functools.partial(forward_kernel, 128, scale),
        grid_spec=pltpu.PrefetchScalarGridSpec(
            num_scalar_prefetch=1,
            grid=(pairs,),
            in_specs=[
                column(0),
                column(1),
                column(2),
                pl.BlockSpec((2, tok, tok), lambda i, m: (i, 0, 0)),
            ],
            out_specs=[
                pl.BlockSpec((tok, LANES), lambda i, m: (0, i)),
                pl.BlockSpec((tok, LANES), lambda i, m: (0, 0)),
            ],
            scratch_shapes=[pltpu.VMEM((tok, tok), F32)],
        ),
        out_shape=[
            jax.ShapeDtypeStruct((tok, width), BF16),
            jax.ShapeDtypeStruct((tok, LANES), F32),
        ],
        compiler_params=params(),
        cost_estimate=cost(8 * tok * tok * width, 8 * tok * width + 32 * tok * tok, 16 * tok * tok),
        name="attention_forward",
    )(scalars, qkv, qkv, qkv, rel_bias)


def backward_kernel(n_g, scale, per_owner, s_ref, q_ref, k_ref, v_ref, do_ref, b_ref, lse_ref, *refs):
    outs, (dqkv_ref, mask_ref) = refs[:-2], refs[-2:]
    tok = q_ref.shape[0]
    rows = tok // n_g
    pair = s_ref[1] ^ pl.program_id(0) if per_owner else pl.program_id(0)

    @pl.when(pl.program_id(0) == 0)
    def _():
        fill_mask(s_ref[2], s_ref[3], mask_ref)

    lane = lax.broadcasted_iota(jnp.int32, (rows, LANES), 1)
    keys = [half_lanes(k_ref[...], h) for h in range(2)]
    grad_k = grad_v = None
    for r_g in range(n_g):
        at = pl.multiple_of((s_ref[0] ^ r_g) * rows, rows) if per_owner else r_g * rows
        here = pl.ds(at, rows)
        grad_q = None
        for h in range(2):
            q = half_lanes(q_ref[here, :] * scale, h)
            do = half_lanes(do_ref[here, :], h)
            lse = jnp.sum(jnp.where(lane == 2 * pair + h, lse_ref[here, :], 0.0), axis=-1, keepdims=True)
            s = dot_f32(q, k_ref[...], NT) + b_ref[h, here, :].astype(F32) + mask_ref[here, :]
            p = jnp.exp(s - lse)
            dp = dot_f32(do, v_ref[...], NT)
            ds = p * (dp - jnp.sum(p * dp, axis=-1, keepdims=True))
            ds = ds.astype(BF16)
            if per_owner:
                outs[r_g & 1][0, r_g // 2, h * rows : (h + 1) * rows, :] = ds
            else:
                outs[0][h, here, :] = ds
            dv = dot_f32(p.astype(BF16), do, TN)
            dk = dot_f32(ds, q, TN)
            dq = dot_f32(ds, keys[h], NN)
            grad_v = dv if grad_v is None else grad_v + dv
            grad_k = dk if grad_k is None else grad_k + dk
            grad_q = dq if grad_q is None else grad_q + dq
        dqkv_ref[0, here, :] = (grad_q * scale).astype(BF16)
    dqkv_ref[1] = grad_k.astype(BF16)
    dqkv_ref[2] = grad_v.astype(BF16)


def attention_backward(scalars, qkv, grad_mixed, rel_bias, lse, scale, n_g, n_e, per_owner):
    tok, width = grad_mixed.shape
    pairs = width // LANES
    turn = (lambda i, m: m[1] ^ i) if per_owner else (lambda i, m: i)
    column = lambda p: pl.BlockSpec((tok, LANES), lambda i, m: (0, p * pairs + turn(i, m)))
    if per_owner:
        block = pl.BlockSpec((1, n_g // 2, 2 * tok // n_g, tok), lambda i, m: (i, 0, 0, 0))
        bias_specs = [block, block]
        bias_shapes = [jax.ShapeDtypeStruct((n_e, n_g // 2, 2 * tok // n_g, tok), BF16)] * 2
    else:
        bias_specs = [pl.BlockSpec((2, tok, tok), lambda i, m: (i, 0, 0))]
        bias_shapes = [jax.ShapeDtypeStruct((2 * pairs, tok, tok), BF16)]
    return pl.pallas_call(
        functools.partial(backward_kernel, n_g, scale, per_owner),
        grid_spec=pltpu.PrefetchScalarGridSpec(
            num_scalar_prefetch=1,
            grid=(pairs,),
            in_specs=[
                column(0),
                column(1),
                column(2),
                column(0),
                pl.BlockSpec((2, tok, tok), lambda i, m: (turn(i, m), 0, 0)),
                pl.BlockSpec((tok, LANES), lambda i, m: (0, 0)),
            ],
            out_specs=bias_specs + [pl.BlockSpec((3, tok, LANES), lambda i, m: (0, 0, turn(i, m)))],
            scratch_shapes=[pltpu.VMEM((tok, tok), F32)],
        ),
        out_shape=bias_shapes + [jax.ShapeDtypeStruct((3, tok, width), BF16)],
        compiler_params=params(),
        cost_estimate=cost(20 * tok * tok * width, 16 * tok * width + 64 * tok * tok, 16 * tok * tok),
        name="attention_backward",
    )(scalars, qkv, qkv, qkv, grad_mixed, rel_bias, lse)


def norm_forward(values):
    inverse = lax.rsqrt(jnp.mean(values * values, axis=-1, keepdims=True) + EPSILON)
    return (values * inverse, inverse)


def norm_backward(grad_out, normed, inverse, norm_gain):
    grad_normed = grad_out * norm_gain
    grad_gain = jnp.sum(grad_out * normed, axis=0)
    grad_input = inverse * (
        grad_normed - normed * jnp.mean(grad_normed * normed, axis=-1, keepdims=True)
    )
    return (grad_input, grad_gain)


def body(
    tokens,
    cotangent,
    w_qkv,
    w_out_attn,
    rel_bias,
    norm_gains,
    w_router,
    w_gate_up,
    w_expert_out,
    routes,
    spans,
):
    tok, width = tokens.shape
    n_g, n_e = lax.axis_size("grp"), lax.axis_size("ep")
    assert w_gate_up.shape[0] == 1 and spans.shape[0] == 1 and tok == LENGTH
    assert n_g & (n_g - 1) == 0 and n_e & (n_e - 1) == 0 and n_g > 1 and n_e > 3
    assert width == HEADS * LANES // 2
    experts = n_e
    cap = 5 * routes.shape[1] * tok // (4 * experts)
    chunks = 2 if cap % 32 == 0 else 1
    short = cap // chunks
    slots = experts * cap
    scale = 1.0 / math.sqrt(width // HEADS)
    me_g, me_e = lax.axis_index("grp"), lax.axis_index("ep")
    me = jnp.stack([me_g, me_e, spans[0, 0], spans[0, 1]]).astype(jnp.int32)
    w_gu, w_eo = w_gate_up[0], w_expert_out[0]

    pos, cot_out = place(routes.T, cotangent, experts, cap, chunks)
    pos_cols = pos.T
    tokens = after(tokens, cot_out)
    cot_rows = swap_rows(cot_out)

    hidden = tokens.astype(F32)
    normed_one, inverse_one = norm_forward(hidden)
    a_one = (normed_one * norm_gains[0]).astype(BF16)
    qkv_rows = dot_f32(a_one, w_qkv, NN).astype(BF16)
    mixed_heads, lse = attention_forward(me, qkv_rows, rel_bias, scale)
    after_attn = hidden + dot_f32(mixed_heads, w_out_attn, NN)
    normed_two, _ = norm_forward(after_attn)
    a_two = (normed_two * norm_gains[1]).astype(BF16)

    parts = dispatch(pos, after(a_two, cot_rows), slots, chunks)
    dact = dot_f32(cot_rows, w_eo, NT).astype(BF16)
    parts = [swap_rows(p if c == 0 else after(p, dact)) for c, p in enumerate(parts)]
    dact = dact.reshape(n_e, chunks, short, -1)
    cot_view = cot_rows.reshape(n_e, chunks, short, width)
    wr_pad = jnp.pad(w_router, ((0, 0), (0, LANES - experts)))
    wr_pad_t = wr_pad.T
    state, back, deos, owns, grad_route = None, [], [], [], 0.0
    for c in range(chunks):
        state, (dxe, deo, own, gr) = expert_chunk(
            me, parts[c], cot_view, dact, w_gu, wr_pad, wr_pad_t, experts, c, slots, state
        )
        back.append(swap_rows(dxe))
        deos.append(deo)
        owns.append(own)
        grad_route = grad_route + gr[:experts]
    act, dg, du = state

    core = ("grp", 1)
    share = lambda v: lax.psum_scatter(v, "grp", scatter_dimension=0, tiled=True)
    act = after(act, *back[:-1])
    gated = [gated_rows(act, w_eo, own, c, chunks) for c, own in enumerate(owns)]
    gate_full = gate_up_grad(parts, after(dg, *gated), du)
    gate = share(after(gate_full, *back))

    grad_after, grad_attn_low, grad_gain_two = return_grads(
        pos_cols, after(after_attn, gate_full), cotangent, norm_gains[1:], back
    )
    gated = [swap_rows(after(gated[0], *back))] + gated[1:]
    gated[1:] = [swap_rows(after(g, gated[0])) for g in gated[1:]]
    grad_mixed = dot_f32(grad_attn_low, w_out_attn, NT).astype(BF16)
    rows_g, rows_t = width // n_g, tok // n_g
    per_owner = n_e * LANES == width
    orders = halving_orders(n_g, n_e)
    *grad_bias, grad_qkv = attention_backward(
        me, qkv_rows, grad_mixed, rel_bias, lse, scale, n_g, n_e, per_owner
    )
    if not per_owner:
        bias = grad_bias[0].reshape(n_e, HEADS // n_e, n_g, rows_t, tok).transpose(0, 2, 1, 3, 4)
        grad_bias = own_blocks(bias.reshape(n_e, n_g, -1, tok), me_g, me_e, n_g, n_e)
    got = xor_send(after(grad_bias[1], gated[0]), *core)
    grad_a_one = sum(
        dot_f32(grad_qkv[i], w_qkv[:, i * width : (i + 1) * width], NT) for i in range(3)
    )
    bias = first_sums(after(grad_bias[0], grad_a_one), got, orders)
    grad_qkv_late = after(grad_qkv, bias[0][0])
    bias = send_all(bias)
    if per_owner:
        weights = weight_grads(me, a_one, mixed_heads, grad_qkv_late, grad_attn_low, n_g, n_e)
    else:
        flat = jnp.concatenate([grad_qkv_late[i] for i in range(3)], axis=1)
        full = [dot_f32(a_one, flat, TN), dot_f32(mixed_heads, grad_attn_low, TN)]
        full = [f.astype(BF16).reshape(n_g, rows_g, n_e, -1) for f in full]
        full = jnp.concatenate(full, axis=-1).transpose(2, 0, 1, 3)
        weights = own_blocks(full, me_g, me_e, n_g, n_e)
    out_full = out_grad(act, [after(deos[0], weights[0])] + deos[1:])
    grad_norm_one, grad_gain_one = norm_backward(grad_a_one, normed_one, inverse_one, norm_gains[0])
    small = jnp.concatenate([grad_gain_one[None], grad_gain_two, grad_route])
    small_steps = [core] + orders[0]
    small_got = xor_send(small, *core)
    got = xor_send(after(weights[1], *[way[1] for way in bias], *gated), *core)
    small = small + after(small_got, out_full)
    weights = first_sums(after(weights[0], out_full, small), got, orders)
    first_keep = weights[0][0]
    expert_out = share(after(out_full, first_keep))
    weights = send_all(weights)
    output = combine(pos_cols, after(after_attn, first_keep), gated)
    grad_tokens = grad_after + grad_norm_one
    grad_w_gate = after(gate, first_keep).astype(F32)[None]
    wide = 3 * width // n_e
    merged = [[bias, weights]] if bias[0][0].shape == weights[0][0].shape else [[bias], [weights]]
    ways, pair = None, (small, xor_send(small, *small_steps[1]))
    for i, step in enumerate(small_steps[2:]):
        done = []
        for j, sets in enumerate(merged):
            one, new = next_sums(sets, () if j else pair)
            done.append(send_all(one))
            pair = (new[0], xor_send(new[0], *step)) if new else pair
        if i == 0:
            done[0] = tied(done[0], grad_w_gate, grad_tokens)
        if i == len(small_steps) - 4:
            done[0] = tied(done[0], output)
        merged = [[one] for one in done]
    ways = done
    small = pair[0] + pair[1]
    grad_w_expert = expert_out.astype(F32)[None]
    ways[0] = tied(ways[0], grad_w_expert)
    if len(ways) == 1:
        g_bias, g_qkv, g_out = last_merged(ways[0], wide)
    else:
        g_bias, g_weights = [jnp.concatenate(last_sums(w)) for w in ways]
        g_qkv, g_out = g_weights[:, :wide], g_weights[:, wide:]
    g_bias = g_bias.reshape(HEADS // n_e, rows_t, tok)
    return (
        output,
        grad_tokens,
        g_qkv,
        g_out,
        g_bias,
        small[:2],
        small[2:].T,
        grad_w_gate,
        grad_w_expert,
    )


def solution(mesh):
    placed = (
        P(("grp", "ep"), None),
        P(("grp", "ep"), None),
        P(),
        P(),
        P(),
        P(),
        P(),
        P("ep", None, None),
        P("ep", None, None),
        P(("grp", "ep"), None),
        P(("grp", "ep"), None),
    )
    return jax.shard_map(
        body,
        mesh=mesh,
        in_specs=placed,
        out_specs=(
            P(("grp", "ep"), None),
            P(("grp", "ep"), None),
            P("grp", "ep"),
            P("grp", "ep"),
            P("ep", "grp", None),
            P(),
            P(),
            P("ep", "grp", None),
            P("ep", "grp", None),
        ),
        check_vma=False,
    )
```

```python
import functools
import math

import jax
import jax.numpy as jnp
from jax import lax
from jax.experimental import pallas as pl
from jax.experimental.pallas import tpu as pltpu
from jax.sharding import PartitionSpec as P

HEADS = 16
LENGTH = 512
EPSILON = 1e-06
LANES = 128
GELU_C = math.sqrt(2.0 / math.pi)
GELU_A = 0.044715
F32 = jnp.float32
BF16 = jnp.bfloat16
VMEM_LIMIT = 60 * 1024 * 1024


def params(**kw):
    return pltpu.CompilerParams(vmem_limit_bytes=VMEM_LIMIT, **kw)


def cost(flops, nbytes, trans=0):
    return pl.CostEstimate(flops=int(flops), bytes_accessed=int(nbytes), transcendentals=int(trans))


def dot_f32(a, b, dims):
    return lax.dot_general(a, b, (dims, ((), ())), preferred_element_type=F32)


NN = ((1,), (0,))
NT = ((1,), (1,))
TN = ((0,), (0,))


def xor_send(v, axis, k):
    n = lax.axis_size(axis)
    return lax.ppermute(v, axis, [(i, i ^ k) for i in range(n)])


def swap_rows(v):
    return lax.all_to_all(v, "ep", split_axis=0, concat_axis=0, tiled=True)


def bits_of(n):
    return [1 << i for i in range(n.bit_length() - 1)]


def after(value, *others):
    return lax.optimization_barrier((value, *others))[0]


def halving_orders(n_g, n_e):
    g_bits = [("grp", k) for k in bits_of(n_g)]
    e_bits = [("ep", k) for k in bits_of(n_e)]
    rest, first, others = g_bits[1:], e_bits[:1], e_bits[1:]
    near, far = others[:1], others[1:]
    return [first + near + rest + far, near + first + far + rest, rest + first + others]


def row_cuts(rows):
    unit = rows // 16
    return [0, 16 * round(7 * unit / 16), 16 * round(3 * unit / 4), rows]


def first_kernel(orders, cuts, k_ref, g_ref, *outs):
    r = pl.program_id(0)
    bit = lambda x, axis, k: (2 * x // k) % 2 if axis == "grp" else (r // k) % 2
    for x in range(k_ref.shape[1]):
        at = 0
        for order, lo, hi in zip(orders, cuts, cuts[1:]):
            if lo == hi:
                continue
            index = 0
            for step in order[1:]:
                index = 2 * index + bit(x, *step)
            goes = bit(x, *order[0])
            for side in range(2):

                @pl.when(goes == side)
                def _():
                    total = k_ref[0, x, lo:hi, :].astype(F32) + g_ref[0, x, lo:hi, :].astype(F32)
                    outs[at + side][index] = total.astype(BF16)

            at += 2


def first_sums(keep, got, orders):
    n_e, n_x, rows, cols = keep.shape
    cuts = row_cuts(rows)
    used = [(o, hi - lo) for o, lo, hi in zip(orders, cuts, cuts[1:]) if hi > lo]
    half = n_e * n_x // 2
    shapes = [jax.ShapeDtypeStruct((half, n, cols), BF16) for _, n in used for _ in range(2)]
    out = pl.pallas_call(
        functools.partial(first_kernel, orders, cuts),
        grid=(n_e,),
        in_specs=[pl.BlockSpec((1, n_x, rows, cols), lambda r: (r, 0, 0, 0))] * 2,
        out_specs=[pl.BlockSpec(s.shape, lambda r: (0, 0, 0)) for s in shapes],
        out_shape=shapes,
        compiler_params=params(),
        cost_estimate=cost(n_e * n_x * rows * cols, 6 * n_e * n_x * rows * cols),
        name="first_sums",
    )(keep, got)
    return [(out[2 * i], out[2 * i + 1], o) for i, (o, _) in enumerate(used)]


def split_kernel(n_way, n_set, n_small, *refs):
    ins, refs = refs[: 2 * n_way * n_set], refs[2 * n_way * n_set :]
    small, outs = refs[: 2 * n_small], refs[2 * n_small :]
    if n_small:
        outs[-1][...] = small[0][...] + small[1][...]
    for w in range(n_way):
        keep_ref, send_ref = outs[2 * w : 2 * w + 2]
        half, at = keep_ref.shape[0], 0
        for i in range(n_set):
            k_ref, g_ref = ins[2 * (w * n_set + i) : 2 * (w * n_set + i) + 2]
            to = at + k_ref.shape[1]
            keep_ref[:, at:to, :] = (k_ref[:half].astype(F32) + g_ref[:half].astype(F32)).astype(BF16)
            send_ref[:, at:to, :] = (k_ref[half:].astype(F32) + g_ref[half:].astype(F32)).astype(BF16)
            at = to


def next_sums(sets, small=()):
    ways = list(zip(*sets))
    shapes = []
    for way in ways:
        blocks, _, cols = way[0][0].shape
        shape = jax.ShapeDtypeStruct((blocks // 2, sum(one[0].shape[1] for one in way), cols), BF16)
        shapes += [shape, shape]
    ins = [v for way in ways for one in way for v in one[:2]]
    total = sum(math.prod(s.shape) for s in shapes)
    out = pl.pallas_call(
        functools.partial(split_kernel, len(ways), len(sets), len(small) // 2),
        out_shape=shapes + [jax.ShapeDtypeStruct(v.shape, v.dtype) for v in small[:1]],
        compiler_params=params(),
        cost_estimate=cost(total, 6 * total),
        name="split_sums",
    )(*ins, *small)
    ways = [(out[2 * i], out[2 * i + 1], way[0][2]) for i, way in enumerate(ways)]
    return ways, out[2 * len(ways) :]


def send_all(ways):
    return [(keep, xor_send(send, *order[0]), order[1:]) for keep, send, order in ways]


def last_sums(ways):
    return [(keep[0].astype(F32) + got[0].astype(F32)) for keep, got, _ in ways]


def last_kernel(*refs):
    ins, (bias_ref, qkv_ref, out_ref) = refs[:-3], refs[-3:]
    wide = qkv_ref.shape[1]
    at = 0
    for k_ref, g_ref in zip(ins[0::2], ins[1::2]):
        n = k_ref.shape[1] // 2
        total = k_ref[0].astype(F32) + g_ref[0].astype(F32)
        bias_ref[at : at + n, :] = total[:n]
        qkv_ref[at : at + n, :] = total[n:, :wide]
        out_ref[at : at + n, :] = total[n:, wide:]
        at += n


def last_merged(ways, wide):
    rows, cols = sum(w[0].shape[1] for w in ways) // 2, ways[0][0].shape[2]
    return pl.pallas_call(
        last_kernel,
        out_shape=[jax.ShapeDtypeStruct((rows, n), F32) for n in (cols, wide, cols - wide)],
        compiler_params=params(),
        cost_estimate=cost(2 * rows * cols, 16 * rows * cols),
        name="last_sums",
    )(*[v for w in ways for v in w[:2]])


def tied(ways, *others):
    return [(after(ways[0][0], *others), *ways[0][1:])] + ways[1:]


def place_kernel(experts, cap, chunks, routes_ref, v_ref, pos_ref, out_ref):
    tok = v_ref.shape[0]
    short = cap // chunks
    ids = lax.broadcasted_iota(jnp.int32, (LANES, tok), 0)
    named = [ids == routes_ref[k : k + 1, :] for k in range(2)]
    counts = jnp.where(named[0] | named[1], 1.0, 0.0).astype(BF16)
    before = lax.broadcasted_iota(jnp.int32, (tok, tok), 0) < lax.broadcasted_iota(
        jnp.int32, (tok, tok), 1
    )
    earlier = dot_f32(counts, jnp.where(before, 1.0, 0.0).astype(BF16), NN)
    for k in range(2):
        slot = jnp.sum(jnp.where(named[k], earlier, 0.0), axis=0, keepdims=True).astype(jnp.int32)
        owner = routes_ref[k : k + 1, :]
        pos_ref[k : k + 1, :] = owner * cap + slot
        chunk = jnp.zeros_like(slot)
        for c in range(1, chunks):
            chunk += jnp.where(slot >= c * short, 1, 0)
        pos_ref[2 + k : 3 + k, :] = chunk * (experts * short) + owner * short + slot - chunk * short
    first, second = pos_ref[0:1, :], pos_ref[1:2, :]
    rows = lax.broadcasted_iota(jnp.int32, (cap, tok), 0)
    for e in range(experts):
        here = rows + e * cap
        pick = jnp.where((here == first) | (here == second), 1.0, 0.0).astype(BF16)
        out_ref[e * cap : (e + 1) * cap, :] = dot_f32(pick, v_ref[...], NN).astype(BF16)


def place(routes_t, values, experts, cap, chunks):
    tok, width = values.shape
    return pl.pallas_call(
        functools.partial(place_kernel, experts, cap, chunks),
        out_shape=[
            jax.ShapeDtypeStruct((4, tok), jnp.int32),
            jax.ShapeDtypeStruct((experts * cap, width), BF16),
        ],
        compiler_params=params(),
        cost_estimate=cost(2 * experts * cap * tok * width, 2 * tok * width + 2 * experts * cap * width),
        name="place_rows",
    )(routes_t, values)


def dispatch_kernel(pos_ref, v_ref, *outs):
    tok = v_ref.shape[0]
    first, second = pos_ref[2:3, :], pos_ref[3:4, :]
    at = 0
    for out in outs:
        total = out.shape[0]
        step = total // 4
        rows = lax.broadcasted_iota(jnp.int32, (step, tok), 0)
        for b in range(4):
            here = rows + at
            pick = jnp.where((here == first) | (here == second), 1.0, 0.0).astype(BF16)
            out[b * step : (b + 1) * step, :] = dot_f32(pick, v_ref[...], NN).astype(BF16)
            at += step


def dispatch(pos, values, slots, chunks):
    tok, width = values.shape
    return pl.pallas_call(
        dispatch_kernel,
        out_shape=[jax.ShapeDtypeStruct((slots // chunks, width), BF16)] * chunks,
        compiler_params=params(),
        cost_estimate=cost(2 * slots * tok * width, 2 * tok * width + 2 * slots * width),
        name="dispatch_rows",
    )(pos, values)


def gathered(first, second, parts):
    total, at = None, 0
    for part in parts:
        n = part.shape[0]
        here = lax.broadcasted_iota(jnp.int32, (first.shape[0], n), 1) + at
        pick = jnp.where((here == first) | (here == second), 1.0, 0.0).astype(BF16)
        term = dot_f32(pick, part[...], NN)
        total = term if total is None else total + term
        at += n
    return total


def combine_kernel(pos_ref, x_ref, *refs):
    parts, out_ref = refs[:-1], refs[-1]
    out_ref[...] = x_ref[...] + gathered(pos_ref[:, 2:3], pos_ref[:, 3:4], parts)


def combine(pos_cols, after_attn, gated):
    tok, width = after_attn.shape
    blk = 256
    return pl.pallas_call(
        combine_kernel,
        grid=(tok // blk,),
        in_specs=[
            pl.BlockSpec((blk, 4), lambda i: (i, 0)),
            pl.BlockSpec((blk, width), lambda i: (i, 0)),
        ]
        + [pl.BlockSpec(g.shape, lambda i: (0, 0)) for g in gated],
        out_specs=pl.BlockSpec((blk, width), lambda i: (i, 0)),
        out_shape=jax.ShapeDtypeStruct((tok, width), F32),
        compiler_params=params(),
        cost_estimate=cost(4 * tok * gated[0].shape[0] * width, 10 * tok * width),
        name="combine_rows",
    )(pos_cols, after_attn, *gated)


def return_kernel(pos_ref, x_ref, cot_ref, gain_ref, *refs):
    parts, (dx_ref, low_ref, gg_ref) = refs[:-3], refs[-3:]
    grad = gathered(pos_ref[:, 2:3], pos_ref[:, 3:4], parts)
    x = x_ref[...]
    inverse = lax.rsqrt(jnp.mean(x * x, axis=-1, keepdims=True) + EPSILON)
    normed = x * inverse
    grad_normed = grad * gain_ref[...]
    dx = cot_ref[...].astype(F32) + inverse * (
        grad_normed - normed * jnp.mean(grad_normed * normed, axis=-1, keepdims=True)
    )
    dx_ref[...] = dx
    low_ref[...] = dx.astype(BF16)

    @pl.when(pl.program_id(0) == 0)
    def _():
        gg_ref[...] = jnp.zeros_like(gg_ref)

    gg_ref[...] += jnp.sum(grad * normed, axis=0, keepdims=True)


def return_grads(pos_cols, after_attn, cotangent, gain, parts):
    tok, width = after_attn.shape
    blk = 256
    row = pl.BlockSpec((blk, width), lambda i: (i, 0))
    one = pl.BlockSpec((1, width), lambda i: (0, 0))
    slots = sum(p.shape[0] for p in parts)
    return pl.pallas_call(
        return_kernel,
        grid=(tok // blk,),
        in_specs=[pl.BlockSpec((blk, 4), lambda i: (i, 0)), row, row, one]
        + [pl.BlockSpec(p.shape, lambda i: (0, 0)) for p in parts],
        out_specs=[row, row, one],
        out_shape=[
            jax.ShapeDtypeStruct((tok, width), F32),
            jax.ShapeDtypeStruct((tok, width), BF16),
            jax.ShapeDtypeStruct((1, width), F32),
        ],
        compiler_params=params(),
        cost_estimate=cost(2 * tok * slots * width, 16 * tok * width),
        name="return_rows",
    )(pos_cols, after_attn, cotangent, gain, *parts)


def expert_kernel(experts, aliased, *refs):
    me_ref, x_ref, c_ref, d_ref, wg_ref, wu_ref, wr_ref, wrt_ref = refs[:8]
    refs = refs[8 + (3 if aliased else 0) :]
    act_ref, dg_ref, du_ref, out_ref, deo_ref, own_ref, gr_ref = refs[:7]
    acc_ref, gate_ref, prob_ref, p_ref = refs[7:]
    j = pl.program_id(0)
    rows_all = x_ref.shape[0]
    n_src, _, short, tile = d_ref.shape
    width = x_ref.shape[1]
    lane = lax.broadcasted_iota(jnp.int32, (rows_all, LANES), 1)

    @pl.when(j == 0)
    def _():
        logits = dot_f32(x_ref[...], wr_ref[...], NN)
        logits = jnp.where(lane < experts, logits, -1e30)
        exps = jnp.exp(logits - jnp.max(logits, axis=-1, keepdims=True))
        probs = exps / jnp.sum(exps, axis=-1, keepdims=True)
        prob_ref[...] = probs
        own = jnp.sum(jnp.where(lane == me_ref[1], probs, 0.0), axis=-1, keepdims=True)
        p_ref[...] = jnp.broadcast_to(own, p_ref.shape)
        own_ref[...] = p_ref[...].reshape(n_src, 1, short, LANES)
        wide = jnp.concatenate([p_ref[...]] * (width // LANES), axis=1)
        deo_ref[...] = (c_ref[...].reshape(rows_all, width).astype(F32) * wide).astype(BF16)
        acc_ref[...] = jnp.zeros_like(acc_ref)
        gate_ref[...] = jnp.zeros_like(gate_ref)

    n_blk = n_src // 2
    for b in range(n_blk):
        rows = slice(2 * b * short, 2 * (b + 1) * short)
        x = x_ref[rows, :]
        z = dot_f32(x, wg_ref[...], NN)
        up = dot_f32(x, wu_ref[...], NN)
        back = d_ref[2 * b : 2 * b + 2].reshape(2 * short, tile).astype(F32)
        reps = tile // LANES
        own = jnp.concatenate([p_ref[rows, :]] * reps, axis=1)
        zz = z * z
        th = jnp.tanh(GELU_C * z * (1.0 + GELU_A * zz))
        half = 0.5 + 0.5 * th
        gelu = z * half
        slope = half + 0.5 * GELU_C * z * (1.0 - th * th) * (1.0 + 3.0 * GELU_A * zz)
        act = (gelu * up).astype(BF16)
        act_ref[rows, :] = act
        share = act.astype(F32) * back
        gate_ref[rows, :] += sum(share[:, i * LANES : (i + 1) * LANES] for i in range(reps))
        dact = back * own
        dg = (dact * up * slope).astype(BF16)
        du = (dact * gelu).astype(BF16)
        dg_ref[rows, :] = dg
        du_ref[rows, :] = du
        acc_ref[rows, :] += dot_f32(dg, wg_ref[...], NT) + dot_f32(du, wu_ref[...], NT)

    @pl.when(j == pl.num_programs(0) - 1)
    def _():
        dgate = jnp.sum(gate_ref[...], axis=-1, keepdims=True)
        dl = dgate * p_ref[...] * (jnp.where(lane == me_ref[1], 1.0, 0.0) - prob_ref[...])
        dl = dl.astype(BF16)
        out_ref[...] = (acc_ref[...] + dot_f32(dl, wrt_ref[...], NN)).astype(BF16)
        gr_ref[...] = dot_f32(dl, x_ref[...], TN)[: gr_ref.shape[0], :]


def expert_chunk(me, rows, cot, dact, w_gate_up, wr_pad, wr_pad_t, experts, c, total_rows, earlier):
    n_src, chunks, short, width = cot.shape
    ff = dact.shape[-1]
    tile = 256
    steps = ff // tile
    n_rows = rows.shape[0]
    whole = pl.BlockSpec(memory_space=pl.ANY)
    part = pl.BlockSpec((n_rows, tile), lambda j, m: (c, j))
    aliased = earlier is not None
    few = -(-experts // 8) * 8
    call = pl.pallas_call(
        functools.partial(expert_kernel, experts, aliased),
        grid_spec=pltpu.PrefetchScalarGridSpec(
            num_scalar_prefetch=1,
            grid=(steps,),
            in_specs=[
                pl.BlockSpec((n_rows, width), lambda j, m: (0, 0)),
                pl.BlockSpec((n_src, 1, short, width), lambda j, m: (0, c, 0, 0)),
                pl.BlockSpec((n_src, 1, short, tile), lambda j, m: (0, c, 0, j)),
                pl.BlockSpec((width, tile), lambda j, m: (0, j)),
                pl.BlockSpec((width, tile), lambda j, m: (0, j + steps)),
                pl.BlockSpec((width, LANES), lambda j, m: (0, 0)),
                pl.BlockSpec((LANES, width), lambda j, m: (0, 0)),
            ]
            + ([whole] * 3 if aliased else []),
            out_specs=[
                part,
                part,
                part,
                pl.BlockSpec((n_rows, width), lambda j, m: (0, 0)),
                pl.BlockSpec((n_rows, width), lambda j, m: (0, 0)),
                pl.BlockSpec((n_src, 1, short, LANES), lambda j, m: (0, 0, 0, 0)),
                pl.BlockSpec((few, width), lambda j, m: (0, 0)),
            ],
            scratch_shapes=[
                pltpu.VMEM((n_rows, width), F32),
                pltpu.VMEM((n_rows, LANES), F32),
                pltpu.VMEM((n_rows, LANES), F32),
                pltpu.VMEM((n_rows, LANES), F32),
            ],
        ),
        out_shape=[jax.ShapeDtypeStruct((total_rows, ff), BF16)] * 3
        + [
            jax.ShapeDtypeStruct((n_rows, width), BF16),
            jax.ShapeDtypeStruct((n_rows, width), BF16),
            jax.ShapeDtypeStruct((n_src, 1, short, LANES), F32),
            jax.ShapeDtypeStruct((few, width), F32),
        ],
        input_output_aliases={8: 0, 9: 1, 10: 2} if aliased else {},
        compiler_params=params(),
        cost_estimate=cost(
            8 * n_rows * width * ff, 4 * width * ff + 10 * n_rows * ff + 4 * n_rows * width, n_rows * ff
        ),
        name="expert_rows",
    )
    out = call(me, rows, cot, dact, w_gate_up, w_gate_up, wr_pad, wr_pad_t, *(earlier if aliased else ()))
    return out[:3], out[3:]


def gated_kernel(act_ref, w_ref, own_ref, out_ref):
    n_rows, tile = out_ref.shape
    own = jnp.concatenate([own_ref[...].reshape(n_rows, LANES)] * (tile // LANES), axis=1)
    out_ref[...] = (dot_f32(act_ref[...], w_ref[...], NN) * own).astype(BF16)


def gated_rows(act, w_eo, own, c, chunks):
    total, ff = act.shape
    width = w_eo.shape[1]
    n_rows, tile = total // chunks, 256
    return pl.pallas_call(
        gated_kernel,
        grid=(width // tile,),
        in_specs=[
            pl.BlockSpec((n_rows, ff), lambda j: (c, 0)),
            pl.BlockSpec((ff, tile), lambda j: (0, j)),
            pl.BlockSpec(own.shape, lambda j: (0, 0, 0, 0)),
        ],
        out_specs=pl.BlockSpec((n_rows, tile), lambda j: (0, j)),
        out_shape=jax.ShapeDtypeStruct((n_rows, width), BF16),
        compiler_params=params(),
        cost_estimate=cost(2 * n_rows * ff * width, 2 * n_rows * (ff + width) + 2 * ff * width),
        name="gated_rows",
    )(act, w_eo, own)


def share_rows(me_g, n_g, full_ref, keep_ref, send_ref):
    rows = full_ref.shape[0] // n_g
    for r_g in range(n_g):
        at = pl.multiple_of((me_g ^ r_g) * rows, rows)
        out = send_ref if r_g & 1 else keep_ref
        block = full_ref[pl.ds(at, rows), :].astype(BF16)
        if len(out.shape) == 4:
            out[0, r_g // 2] = block
        else:
            out[r_g // 2] = block


def weight_kernel(n_g, me_ref, a_ref, o_ref, b0_ref, b1_ref, b2_ref, d_ref, keep_ref, send_ref, full_ref, at_ref, ot_ref):
    @pl.when(pl.program_id(0) == 0)
    def _():
        at_ref[...] = a_ref[...].T
        ot_ref[...] = o_ref[...].T

    b = jnp.concatenate([b0_ref[0], b1_ref[0], b2_ref[0]], axis=1)
    full_ref[:, : 3 * LANES] = dot_f32(at_ref[...], b, NN)
    full_ref[:, 3 * LANES :] = dot_f32(ot_ref[...], d_ref[...], NN)
    share_rows(me_ref[0], n_g, full_ref, keep_ref, send_ref)


def weight_grads(me, a_one, mixed, grad_qkv, grad_low, n_g, n_e):
    tok, width = a_one.shape
    heads_wide = width // LANES
    block = pl.BlockSpec((1, n_g // 2, width // n_g, 4 * LANES), lambda r, m: (r, 0, 0, 0))

    def plane(t):
        def index(r, m):
            at = 3 * (m[1] ^ r) + t
            return (at // heads_wide, 0, at % heads_wide)

        return pl.BlockSpec((1, tok, LANES), index)

    return pl.pallas_call(
        functools.partial(weight_kernel, n_g),
        grid_spec=pltpu.PrefetchScalarGridSpec(
            num_scalar_prefetch=1,
            grid=(n_e,),
            in_specs=[
                pl.BlockSpec((tok, width), lambda r, m: (0, 0)),
                pl.BlockSpec((tok, width), lambda r, m: (0, 0)),
                plane(0),
                plane(1),
                plane(2),
                pl.BlockSpec((tok, LANES), lambda r, m: (0, m[1] ^ r)),
            ],
            out_specs=[block, block],
            scratch_shapes=[
                pltpu.VMEM((width, 4 * LANES), F32),
                pltpu.VMEM((width, tok), BF16),
                pltpu.VMEM((width, tok), BF16),
            ],
        ),
        out_shape=[jax.ShapeDtypeStruct((n_e, n_g // 2, width // n_g, 4 * LANES), BF16)] * 2,
        compiler_params=params(),
        cost_estimate=cost(8 * tok * width * width, 12 * tok * width + 8 * width * width),
        name="weight_grads",
    )(me, a_one, mixed, grad_qkv, grad_qkv, grad_qkv, grad_low)


def relative(v, axis, me, n):
    return jnp.stack([lax.dynamic_index_in_dim(v, me ^ r, axis, keepdims=False) for r in range(n)], axis)


def own_blocks(view, me_g, me_e, n_g, n_e):
    view = relative(relative(view, 0, me_e, n_e), 1, me_g, n_g)
    return view[:, 0::2], view[:, 1::2]


def gate_up_kernel(half, n_part, *refs):
    parts, (g_ref, u_ref, out_ref, t_ref) = refs[:n_part], refs[n_part:]
    j = pl.program_id(0)

    @pl.when(j == 0)
    def _():
        at = 0
        for part in parts:
            t_ref[:, at : at + part.shape[0]] = part[...].T
            at += part.shape[0]

    @pl.when(j < half)
    def _():
        out_ref[...] = dot_f32(t_ref[...], g_ref[...], NN).astype(BF16)

    @pl.when(j >= half)
    def _():
        out_ref[...] = dot_f32(t_ref[...], u_ref[...], NN).astype(BF16)


def gate_up_grad(parts, dg, du):
    total, ff = dg.shape
    width = parts[0].shape[1]
    tile = 256
    half = ff // tile
    return pl.pallas_call(
        functools.partial(gate_up_kernel, half, len(parts)),
        grid=(2 * half,),
        in_specs=[pl.BlockSpec(p.shape, lambda j: (0, 0)) for p in parts]
        + [
            pl.BlockSpec((total, tile), lambda j: (0, jnp.minimum(j, half - 1))),
            pl.BlockSpec((total, tile), lambda j: (0, jnp.maximum(j - half, 0))),
        ],
        out_specs=pl.BlockSpec((width, tile), lambda j: (0, j)),
        scratch_shapes=[pltpu.VMEM((width, total), BF16)],
        out_shape=jax.ShapeDtypeStruct((width, 2 * ff), BF16),
        compiler_params=params(),
        cost_estimate=cost(4 * total * width * ff, 2 * total * (width + 2 * ff) + 4 * width * ff),
        name="gate_up_grad",
    )(*parts, dg, du)


def out_grad_kernel(n_part, act_ref, *refs):
    parts, out_ref = refs[:n_part], refs[n_part]
    total, at = None, 0
    for part in parts:
        n = part.shape[0]
        term = dot_f32(act_ref[at : at + n, :], part[...], TN)
        total = term if total is None else total + term
        at += n
    out_ref[...] = total.astype(BF16)


def out_grad(act, parts):
    total, ff = act.shape
    width = parts[0].shape[1]
    tile = 256
    return pl.pallas_call(
        functools.partial(out_grad_kernel, len(parts)),
        grid=(ff // tile,),
        in_specs=[pl.BlockSpec((total, tile), lambda j: (0, j))]
        + [pl.BlockSpec(p.shape, lambda j: (0, 0)) for p in parts],
        out_specs=pl.BlockSpec((tile, width), lambda j: (j, 0)),
        out_shape=jax.ShapeDtypeStruct((ff, width), BF16),
        compiler_params=params(),
        cost_estimate=cost(2 * total * width * ff, 2 * total * (width + ff) + 2 * width * ff),
        name="out_grad",
    )(act, *parts)


def fill_mask(start, length, mask_ref):
    tok = mask_ref.shape[0]
    query = lax.broadcasted_iota(jnp.int32, (tok, tok), 0)
    key = lax.broadcasted_iota(jnp.int32, (tok, tok), 1)
    end = start + length
    inside = (query >= start) & (query < end) & (key >= start) & (key < end)
    mask_ref[...] = jnp.where((key <= query) | inside, 0.0, -1e30)


def half_lanes(v, h):
    lane = lax.broadcasted_iota(jnp.int32, v.shape, 1)
    return jnp.where((lane >= LANES // 2) == (h == 1), v, jnp.zeros_like(v))


def forward_kernel(blk, scale, s_ref, q_ref, k_ref, v_ref, b_ref, o_ref, lse_ref, mask_ref):
    tok = q_ref.shape[0]
    pair = pl.program_id(0)

    @pl.when(pair == 0)
    def _():
        fill_mask(s_ref[2], s_ref[3], mask_ref)
        lse_ref[...] = jnp.zeros_like(lse_ref)

    lane = lax.broadcasted_iota(jnp.int32, (blk, LANES), 1)
    values = [half_lanes(v_ref[...], h) for h in range(2)]
    for i in range(tok // blk):
        rows = slice(i * blk, (i + 1) * blk)
        mixed, lse = None, lse_ref[rows, :]
        for h in range(2):
            q = half_lanes(q_ref[rows, :] * scale, h)
            s = dot_f32(q, k_ref[...], NT) + b_ref[h, rows, :].astype(F32) + mask_ref[rows, :]
            top = jnp.max(s, axis=-1, keepdims=True)
            e = jnp.exp(s - top)
            total = jnp.sum(e, axis=-1, keepdims=True)
            p = (e * (1.0 / total)).astype(BF16)
            o = dot_f32(p, values[h], NN)
            mixed = o if mixed is None else mixed + o
            lse = jnp.where(lane == 2 * pair + h, top + jnp.log(total), lse)
        o_ref[rows, :] = mixed.astype(BF16)
        lse_ref[rows, :] = lse


def attention_forward(scalars, qkv, rel_bias, scale):
    tok, width = qkv.shape[0], qkv.shape[1] // 3
    pairs = width // LANES
    column = lambda p: pl.BlockSpec((tok, LANES), lambda i, m: (0, p * pairs + i))
    return pl.pallas_call(
        functools.partial(forward_kernel, 128, scale),
        grid_spec=pltpu.PrefetchScalarGridSpec(
            num_scalar_prefetch=1,
            grid=(pairs,),
            in_specs=[
                column(0),
                column(1),
                column(2),
                pl.BlockSpec((2, tok, tok), lambda i, m: (i, 0, 0)),
            ],
            out_specs=[
                pl.BlockSpec((tok, LANES), lambda i, m: (0, i)),
                pl.BlockSpec((tok, LANES), lambda i, m: (0, 0)),
            ],
            scratch_shapes=[pltpu.VMEM((tok, tok), F32)],
        ),
        out_shape=[
            jax.ShapeDtypeStruct((tok, width), BF16),
            jax.ShapeDtypeStruct((tok, LANES), F32),
        ],
        compiler_params=params(),
        cost_estimate=cost(8 * tok * tok * width, 8 * tok * width + 32 * tok * tok, 16 * tok * tok),
        name="attention_forward",
    )(scalars, qkv, qkv, qkv, rel_bias)


def backward_kernel(n_g, scale, per_owner, s_ref, q_ref, k_ref, v_ref, do_ref, b_ref, lse_ref, *refs):
    outs, (dqkv_ref, mask_ref) = refs[:-2], refs[-2:]
    tok = q_ref.shape[0]
    rows = tok // n_g
    pair = s_ref[1] ^ pl.program_id(0) if per_owner else pl.program_id(0)

    @pl.when(pl.program_id(0) == 0)
    def _():
        fill_mask(s_ref[2], s_ref[3], mask_ref)

    lane = lax.broadcasted_iota(jnp.int32, (rows, LANES), 1)
    keys = [half_lanes(k_ref[...], h) for h in range(2)]
    grad_k = grad_v = None
    for r_g in range(n_g):
        at = pl.multiple_of((s_ref[0] ^ r_g) * rows, rows) if per_owner else r_g * rows
        here = pl.ds(at, rows)
        grad_q = None
        for h in range(2):
            q = half_lanes(q_ref[here, :] * scale, h)
            do = half_lanes(do_ref[here, :], h)
            lse = jnp.sum(jnp.where(lane == 2 * pair + h, lse_ref[here, :], 0.0), axis=-1, keepdims=True)
            s = dot_f32(q, k_ref[...], NT) + b_ref[h, here, :].astype(F32) + mask_ref[here, :]
            p = jnp.exp(s - lse)
            dp = dot_f32(do, v_ref[...], NT)
            ds = p * (dp - jnp.sum(p * dp, axis=-1, keepdims=True))
            ds = ds.astype(BF16)
            if per_owner:
                outs[r_g & 1][0, r_g // 2, h * rows : (h + 1) * rows, :] = ds
            else:
                outs[0][h, here, :] = ds
            dv = dot_f32(p.astype(BF16), do, TN)
            dk = dot_f32(ds, q, TN)
            dq = dot_f32(ds, keys[h], NN)
            grad_v = dv if grad_v is None else grad_v + dv
            grad_k = dk if grad_k is None else grad_k + dk
            grad_q = dq if grad_q is None else grad_q + dq
        dqkv_ref[0, here, :] = (grad_q * scale).astype(BF16)
    dqkv_ref[1] = grad_k.astype(BF16)
    dqkv_ref[2] = grad_v.astype(BF16)


def attention_backward(scalars, qkv, grad_mixed, rel_bias, lse, scale, n_g, n_e, per_owner):
    tok, width = grad_mixed.shape
    pairs = width // LANES
    turn = (lambda i, m: m[1] ^ i) if per_owner else (lambda i, m: i)
    column = lambda p: pl.BlockSpec((tok, LANES), lambda i, m: (0, p * pairs + turn(i, m)))
    if per_owner:
        block = pl.BlockSpec((1, n_g // 2, 2 * tok // n_g, tok), lambda i, m: (i, 0, 0, 0))
        bias_specs = [block, block]
        bias_shapes = [jax.ShapeDtypeStruct((n_e, n_g // 2, 2 * tok // n_g, tok), BF16)] * 2
    else:
        bias_specs = [pl.BlockSpec((2, tok, tok), lambda i, m: (i, 0, 0))]
        bias_shapes = [jax.ShapeDtypeStruct((2 * pairs, tok, tok), BF16)]
    return pl.pallas_call(
        functools.partial(backward_kernel, n_g, scale, per_owner),
        grid_spec=pltpu.PrefetchScalarGridSpec(
            num_scalar_prefetch=1,
            grid=(pairs,),
            in_specs=[
                column(0),
                column(1),
                column(2),
                column(0),
                pl.BlockSpec((2, tok, tok), lambda i, m: (turn(i, m), 0, 0)),
                pl.BlockSpec((tok, LANES), lambda i, m: (0, 0)),
            ],
            out_specs=bias_specs + [pl.BlockSpec((3, tok, LANES), lambda i, m: (0, 0, turn(i, m)))],
            scratch_shapes=[pltpu.VMEM((tok, tok), F32)],
        ),
        out_shape=bias_shapes + [jax.ShapeDtypeStruct((3, tok, width), BF16)],
        compiler_params=params(),
        cost_estimate=cost(20 * tok * tok * width, 16 * tok * width + 64 * tok * tok, 16 * tok * tok),
        name="attention_backward",
    )(scalars, qkv, qkv, qkv, grad_mixed, rel_bias, lse)


def norm_forward(values):
    inverse = lax.rsqrt(jnp.mean(values * values, axis=-1, keepdims=True) + EPSILON)
    return (values * inverse, inverse)


def norm_backward(grad_out, normed, inverse, norm_gain):
    grad_normed = grad_out * norm_gain
    grad_gain = jnp.sum(grad_out * normed, axis=0)
    grad_input = inverse * (
        grad_normed - normed * jnp.mean(grad_normed * normed, axis=-1, keepdims=True)
    )
    return (grad_input, grad_gain)


def body(
    tokens,
    cotangent,
    w_qkv,
    w_out_attn,
    rel_bias,
    norm_gains,
    w_router,
    w_gate_up,
    w_expert_out,
    routes,
    spans,
):
    tok, width = tokens.shape
    n_g, n_e = lax.axis_size("grp"), lax.axis_size("ep")
    assert w_gate_up.shape[0] == 1 and spans.shape[0] == 1 and tok == LENGTH
    assert n_g & (n_g - 1) == 0 and n_e & (n_e - 1) == 0 and n_g > 1 and n_e > 3
    assert width == HEADS * LANES // 2
    experts = n_e
    cap = 5 * routes.shape[1] * tok // (4 * experts)
    chunks = 2 if cap % 32 == 0 else 1
    short = cap // chunks
    slots = experts * cap
    scale = 1.0 / math.sqrt(width // HEADS)
    me_g, me_e = lax.axis_index("grp"), lax.axis_index("ep")
    me = jnp.stack([me_g, me_e, spans[0, 0], spans[0, 1]]).astype(jnp.int32)
    w_gu, w_eo = w_gate_up[0], w_expert_out[0]

    pos, cot_out = place(routes.T, cotangent, experts, cap, chunks)
    pos_cols = pos.T
    tokens = after(tokens, cot_out)
    cot_rows = swap_rows(cot_out)

    hidden = tokens.astype(F32)
    normed_one, inverse_one = norm_forward(hidden)
    a_one = (normed_one * norm_gains[0]).astype(BF16)
    qkv_rows = dot_f32(a_one, w_qkv, NN).astype(BF16)
    mixed_heads, lse = attention_forward(me, qkv_rows, rel_bias, scale)
    after_attn = hidden + dot_f32(mixed_heads, w_out_attn, NN)
    normed_two, _ = norm_forward(after_attn)
    a_two = (normed_two * norm_gains[1]).astype(BF16)

    parts = dispatch(pos, after(a_two, cot_rows), slots, chunks)
    dact = dot_f32(cot_rows, w_eo, NT).astype(BF16)
    parts = [swap_rows(p if c == 0 else after(p, dact)) for c, p in enumerate(parts)]
    dact = dact.reshape(n_e, chunks, short, -1)
    cot_view = cot_rows.reshape(n_e, chunks, short, width)
    wr_pad = jnp.pad(w_router, ((0, 0), (0, LANES - experts)))
    wr_pad_t = wr_pad.T
    state, back, deos, owns, grad_route = None, [], [], [], 0.0
    for c in range(chunks):
        state, (dxe, deo, own, gr) = expert_chunk(
            me, parts[c], cot_view, dact, w_gu, wr_pad, wr_pad_t, experts, c, slots, state
        )
        back.append(swap_rows(dxe))
        deos.append(deo)
        owns.append(own)
        grad_route = grad_route + gr[:experts]
    act, dg, du = state

    core = ("grp", 1)
    share = lambda v: lax.psum_scatter(v, "grp", scatter_dimension=0, tiled=True)
    act = after(act, *back[:-1])
    gated = [gated_rows(act, w_eo, own, c, chunks) for c, own in enumerate(owns)]
    gate_full = gate_up_grad(parts, after(dg, *gated), du)
    gate = share(after(gate_full, *back))

    grad_after, grad_attn_low, grad_gain_two = return_grads(
        pos_cols, after(after_attn, gate_full), cotangent, norm_gains[1:], back
    )
    gated = [swap_rows(after(gated[0], *back))] + gated[1:]
    gated[1:] = [swap_rows(after(g, gated[0])) for g in gated[1:]]
    grad_mixed = dot_f32(grad_attn_low, w_out_attn, NT).astype(BF16)
    rows_g, rows_t = width // n_g, tok // n_g
    per_owner = n_e * LANES == width
    orders = halving_orders(n_g, n_e)
    *grad_bias, grad_qkv = attention_backward(
        me, qkv_rows, grad_mixed, rel_bias, lse, scale, n_g, n_e, per_owner
    )
    if not per_owner:
        bias = grad_bias[0].reshape(n_e, HEADS // n_e, n_g, rows_t, tok).transpose(0, 2, 1, 3, 4)
        grad_bias = own_blocks(bias.reshape(n_e, n_g, -1, tok), me_g, me_e, n_g, n_e)
    got = xor_send(after(grad_bias[1], gated[0]), *core)
    grad_a_one = sum(
        dot_f32(grad_qkv[i], w_qkv[:, i * width : (i + 1) * width], NT) for i in range(3)
    )
    bias = first_sums(after(grad_bias[0], grad_a_one), got, orders)
    grad_qkv_late = after(grad_qkv, bias[0][0])
    bias = send_all(bias)
    if per_owner:
        weights = weight_grads(me, a_one, mixed_heads, grad_qkv_late, grad_attn_low, n_g, n_e)
    else:
        flat = jnp.concatenate([grad_qkv_late[i] for i in range(3)], axis=1)
        full = [dot_f32(a_one, flat, TN), dot_f32(mixed_heads, grad_attn_low, TN)]
        full = [f.astype(BF16).reshape(n_g, rows_g, n_e, -1) for f in full]
        full = jnp.concatenate(full, axis=-1).transpose(2, 0, 1, 3)
        weights = own_blocks(full, me_g, me_e, n_g, n_e)
    out_full = out_grad(act, [after(deos[0], weights[0])] + deos[1:])
    grad_norm_one, grad_gain_one = norm_backward(grad_a_one, normed_one, inverse_one, norm_gains[0])
    small = jnp.concatenate([grad_gain_one[None], grad_gain_two, grad_route])
    small_steps = [core] + orders[0]
    small_got = xor_send(small, *core)
    got = xor_send(after(weights[1], *[way[1] for way in bias], *gated), *core)
    small = small + after(small_got, out_full)
    weights = first_sums(after(weights[0], out_full, small), got, orders)
    first_keep = weights[0][0]
    expert_out = share(after(out_full, first_keep))
    weights = send_all(weights)
    output = combine(pos_cols, after(after_attn, first_keep), gated)
    grad_tokens = grad_after + grad_norm_one
    grad_w_gate = after(gate, first_keep).astype(F32)[None]
    wide = 3 * width // n_e
    merged = [[bias, weights]] if bias[0][0].shape == weights[0][0].shape else [[bias], [weights]]
    ways, pair = None, (small, xor_send(small, *small_steps[1]))
    for i, step in enumerate(small_steps[2:]):
        done = []
        for j, sets in enumerate(merged):
            one, new = next_sums(sets, () if j else pair)
            done.append(send_all(one))
            pair = (new[0], xor_send(new[0], *step)) if new else pair
        if i == 0:
            done[0] = tied(done[0], grad_w_gate, grad_tokens)
        if i == len(small_steps) - 4:
            done[0] = tied(done[0], output)
        merged = [[one] for one in done]
    ways = done
    small = pair[0] + pair[1]
    grad_w_expert = expert_out.astype(F32)[None]
    ways[0] = tied(ways[0], grad_w_expert)
    if len(ways) == 1:
        g_bias, g_qkv, g_out = last_merged(ways[0], wide)
    else:
        g_bias, g_weights = [jnp.concatenate(last_sums(w)) for w in ways]
        g_qkv, g_out = g_weights[:, :wide], g_weights[:, wide:]
    g_bias = g_bias.reshape(HEADS // n_e, rows_t, tok)
    return (
        output,
        grad_tokens,
        g_qkv,
        g_out,
        g_bias,
        small[:2],
        small[2:].T,
        grad_w_gate,
        grad_w_expert,
    )


def solution(mesh):
    placed = (
        P(("grp", "ep"), None),
        P(("grp", "ep"), None),
        P(),
        P(),
        P(),
        P(),
        P(),
        P("ep", None, None),
        P("ep", None, None),
        P(("grp", "ep"), None),
        P(("grp", "ep"), None),
    )
    return jax.shard_map(
        body,
        mesh=mesh,
        in_specs=placed,
        out_specs=(
            P(("grp", "ep"), None),
            P(("grp", "ep"), None),
            P("grp", "ep"),
            P("grp", "ep"),
            P("ep", "grp", None),
            P(),
            P(),
            P("ep", "grp", None),
            P("ep", "grp", None),
        ),
        check_vma=False,
    )
```

```python
import functools
import math

import jax
import jax.numpy as jnp
from jax import lax
from jax.experimental import pallas as pl
from jax.experimental.pallas import tpu as pltpu
from jax.sharding import PartitionSpec as P

HEADS = 16
LENGTH = 512
EPSILON = 1e-06
LANES = 128
GELU_C = math.sqrt(2.0 / math.pi)
GELU_A = 0.044715
F32 = jnp.float32
BF16 = jnp.bfloat16
VMEM_LIMIT = 60 * 1024 * 1024


def params(**kw):
    return pltpu.CompilerParams(vmem_limit_bytes=VMEM_LIMIT, **kw)


def cost(flops, nbytes, trans=0):
    return pl.CostEstimate(flops=int(flops), bytes_accessed=int(nbytes), transcendentals=int(trans))


def dot_f32(a, b, dims):
    return lax.dot_general(a, b, (dims, ((), ())), preferred_element_type=F32)


NN = ((1,), (0,))
NT = ((1,), (1,))
TN = ((0,), (0,))


def xor_send(v, axis, k):
    n = lax.axis_size(axis)
    return lax.ppermute(v, axis, [(i, i ^ k) for i in range(n)])


def swap_rows(v):
    return lax.all_to_all(v, "ep", split_axis=0, concat_axis=0, tiled=True)


def bits_of(n):
    return [1 << i for i in range(n.bit_length() - 1)]


def after(value, *others):
    return lax.optimization_barrier((value, *others))[0]


def halving_orders(n_g, n_e):
    g_bits = [("grp", k) for k in bits_of(n_g)]
    e_bits = [("ep", k) for k in bits_of(n_e)]
    rest, first, others = g_bits[1:], e_bits[:1], e_bits[1:]
    near, far = others[:1], others[1:]
    return [first + near + rest + far, near + first + far + rest, rest + first + others]


def row_cuts(rows):
    unit = rows // 16
    return [0, 16 * round(7 * unit / 16), 16 * round(3 * unit / 4), rows]


def first_kernel(orders, cuts, k_ref, g_ref, *outs):
    n_e, n_x = k_ref.shape[:2]
    at = 0
    for order, lo, hi in zip(orders, cuts, cuts[1:]):
        if lo == hi:
            continue
        for r in range(n_e):
            for x in range(n_x):
                bits = [(2 * x // k) % 2 if axis == "grp" else (r // k) % 2 for axis, k in order]
                index = 0
                for bit in bits[1:]:
                    index = 2 * index + bit
                total = k_ref[r, x, lo:hi, :].astype(F32) + g_ref[r, x, lo:hi, :].astype(F32)
                outs[at + bits[0]][index] = total.astype(BF16)
        at += 2


def first_sums(keep, got, orders):
    n_e, n_x, rows, cols = keep.shape
    cuts = row_cuts(rows)
    used = [(o, hi - lo) for o, lo, hi in zip(orders, cuts, cuts[1:]) if hi > lo]
    half = n_e * n_x // 2
    shapes = [jax.ShapeDtypeStruct((half, n, cols), BF16) for _, n in used for _ in range(2)]
    out = pl.pallas_call(
        functools.partial(first_kernel, orders, cuts),
        out_shape=shapes,
        compiler_params=params(),
        cost_estimate=cost(n_e * n_x * rows * cols, 6 * n_e * n_x * rows * cols),
        name="first_sums",
    )(keep, got)
    return [(out[2 * i], out[2 * i + 1], o) for i, (o, _) in enumerate(used)]


def split_kernel(n_way, n_set, n_small, *refs):
    ins, refs = refs[: 2 * n_way * n_set], refs[2 * n_way * n_set :]
    small, outs = refs[: 2 * n_small], refs[2 * n_small :]
    if n_small:
        outs[-1][...] = small[0][...] + small[1][...]
    for w in range(n_way):
        keep_ref, send_ref = outs[2 * w : 2 * w + 2]
        half, at = keep_ref.shape[0], 0
        for i in range(n_set):
            k_ref, g_ref = ins[2 * (w * n_set + i) : 2 * (w * n_set + i) + 2]
            to = at + k_ref.shape[1]
            keep_ref[:, at:to, :] = (k_ref[:half].astype(F32) + g_ref[:half].astype(F32)).astype(BF16)
            send_ref[:, at:to, :] = (k_ref[half:].astype(F32) + g_ref[half:].astype(F32)).astype(BF16)
            at = to


def next_sums(sets, small=()):
    ways = list(zip(*sets))
    shapes = []
    for way in ways:
        blocks, _, cols = way[0][0].shape
        shape = jax.ShapeDtypeStruct((blocks // 2, sum(one[0].shape[1] for one in way), cols), BF16)
        shapes += [shape, shape]
    ins = [v for way in ways for one in way for v in one[:2]]
    total = sum(math.prod(s.shape) for s in shapes)
    out = pl.pallas_call(
        functools.partial(split_kernel, len(ways), len(sets), len(small) // 2),
        out_shape=shapes + [jax.ShapeDtypeStruct(v.shape, v.dtype) for v in small[:1]],
        compiler_params=params(),
        cost_estimate=cost(total, 6 * total),
        name="split_sums",
    )(*ins, *small)
    ways = [(out[2 * i], out[2 * i + 1], way[0][2]) for i, way in enumerate(ways)]
    return ways, out[2 * len(ways) :]


def send_all(ways):
    return [(keep, xor_send(send, *order[0]), order[1:]) for keep, send, order in ways]


def last_sums(ways):
    return [(keep[0].astype(F32) + got[0].astype(F32)) for keep, got, _ in ways]


def last_kernel(*refs):
    ins, (bias_ref, qkv_ref, out_ref) = refs[:-3], refs[-3:]
    wide = qkv_ref.shape[1]
    at = 0
    for k_ref, g_ref in zip(ins[0::2], ins[1::2]):
        n = k_ref.shape[1] // 2
        total = k_ref[0].astype(F32) + g_ref[0].astype(F32)
        bias_ref[at : at + n, :] = total[:n]
        qkv_ref[at : at + n, :] = total[n:, :wide]
        out_ref[at : at + n, :] = total[n:, wide:]
        at += n


def last_merged(ways, wide):
    rows, cols = sum(w[0].shape[1] for w in ways) // 2, ways[0][0].shape[2]
    return pl.pallas_call(
        last_kernel,
        out_shape=[jax.ShapeDtypeStruct((rows, n), F32) for n in (cols, wide, cols - wide)],
        compiler_params=params(),
        cost_estimate=cost(2 * rows * cols, 16 * rows * cols),
        name="last_sums",
    )(*[v for w in ways for v in w[:2]])


def tied(ways, *others):
    return [(after(ways[0][0], *others), *ways[0][1:])] + ways[1:]


def place_kernel(experts, cap, chunks, routes_ref, v_ref, pos_ref, out_ref):
    tok = v_ref.shape[0]
    short = cap // chunks
    ids = lax.broadcasted_iota(jnp.int32, (LANES, tok), 0)
    named = [ids == routes_ref[k : k + 1, :] for k in range(2)]
    counts = jnp.where(named[0] | named[1], 1.0, 0.0).astype(BF16)
    before = lax.broadcasted_iota(jnp.int32, (tok, tok), 0) < lax.broadcasted_iota(
        jnp.int32, (tok, tok), 1
    )
    earlier = dot_f32(counts, jnp.where(before, 1.0, 0.0).astype(BF16), NN)
    for k in range(2):
        slot = jnp.sum(jnp.where(named[k], earlier, 0.0), axis=0, keepdims=True).astype(jnp.int32)
        owner = routes_ref[k : k + 1, :]
        pos_ref[k : k + 1, :] = owner * cap + slot
        chunk = jnp.zeros_like(slot)
        for c in range(1, chunks):
            chunk += jnp.where(slot >= c * short, 1, 0)
        pos_ref[2 + k : 3 + k, :] = chunk * (experts * short) + owner * short + slot - chunk * short
    first, second = pos_ref[0:1, :], pos_ref[1:2, :]
    rows = lax.broadcasted_iota(jnp.int32, (cap, tok), 0)
    for e in range(experts):
        here = rows + e * cap
        pick = jnp.where((here == first) | (here == second), 1.0, 0.0).astype(BF16)
        out_ref[e * cap : (e + 1) * cap, :] = dot_f32(pick, v_ref[...], NN).astype(BF16)


def place(routes_t, values, experts, cap, chunks):
    tok, width = values.shape
    return pl.pallas_call(
        functools.partial(place_kernel, experts, cap, chunks),
        out_shape=[
            jax.ShapeDtypeStruct((4, tok), jnp.int32),
            jax.ShapeDtypeStruct((experts * cap, width), BF16),
        ],
        compiler_params=params(),
        cost_estimate=cost(2 * experts * cap * tok * width, 2 * tok * width + 2 * experts * cap * width),
        name="place_rows",
    )(routes_t, values)


def dispatch_kernel(pos_ref, v_ref, *outs):
    tok = v_ref.shape[0]
    first, second = pos_ref[2:3, :], pos_ref[3:4, :]
    at = 0
    for out in outs:
        total = out.shape[0]
        step = total // 4
        rows = lax.broadcasted_iota(jnp.int32, (step, tok), 0)
        for b in range(4):
            here = rows + at
            pick = jnp.where((here == first) | (here == second), 1.0, 0.0).astype(BF16)
            out[b * step : (b + 1) * step, :] = dot_f32(pick, v_ref[...], NN).astype(BF16)
            at += step


def dispatch(pos, values, slots, chunks):
    tok, width = values.shape
    return pl.pallas_call(
        dispatch_kernel,
        out_shape=[jax.ShapeDtypeStruct((slots // chunks, width), BF16)] * chunks,
        compiler_params=params(),
        cost_estimate=cost(2 * slots * tok * width, 2 * tok * width + 2 * slots * width),
        name="dispatch_rows",
    )(pos, values)


def gathered(first, second, parts):
    total, at = None, 0
    for part in parts:
        n = part.shape[0]
        here = lax.broadcasted_iota(jnp.int32, (first.shape[0], n), 1) + at
        pick = jnp.where((here == first) | (here == second), 1.0, 0.0).astype(BF16)
        term = dot_f32(pick, part[...], NN)
        total = term if total is None else total + term
        at += n
    return total


def combine_kernel(pos_ref, x_ref, *refs):
    parts, out_ref = refs[:-1], refs[-1]
    out_ref[...] = x_ref[...] + gathered(pos_ref[:, 2:3], pos_ref[:, 3:4], parts)


def combine(pos_cols, after_attn, gated):
    tok, width = after_attn.shape
    blk = 256
    return pl.pallas_call(
        combine_kernel,
        grid=(tok // blk,),
        in_specs=[
            pl.BlockSpec((blk, 4), lambda i: (i, 0)),
            pl.BlockSpec((blk, width), lambda i: (i, 0)),
        ]
        + [pl.BlockSpec(g.shape, lambda i: (0, 0)) for g in gated],
        out_specs=pl.BlockSpec((blk, width), lambda i: (i, 0)),
        out_shape=jax.ShapeDtypeStruct((tok, width), F32),
        compiler_params=params(),
        cost_estimate=cost(4 * tok * gated[0].shape[0] * width, 10 * tok * width),
        name="combine_rows",
    )(pos_cols, after_attn, *gated)


def return_kernel(pos_ref, x_ref, cot_ref, gain_ref, *refs):
    parts, (dx_ref, low_ref, gg_ref) = refs[:-3], refs[-3:]
    grad = gathered(pos_ref[:, 2:3], pos_ref[:, 3:4], parts)
    x = x_ref[...]
    inverse = lax.rsqrt(jnp.mean(x * x, axis=-1, keepdims=True) + EPSILON)
    normed = x * inverse
    grad_normed = grad * gain_ref[...]
    dx = cot_ref[...].astype(F32) + inverse * (
        grad_normed - normed * jnp.mean(grad_normed * normed, axis=-1, keepdims=True)
    )
    dx_ref[...] = dx
    low_ref[...] = dx.astype(BF16)

    @pl.when(pl.program_id(0) == 0)
    def _():
        gg_ref[...] = jnp.zeros_like(gg_ref)

    gg_ref[...] += jnp.sum(grad * normed, axis=0, keepdims=True)


def return_grads(pos_cols, after_attn, cotangent, gain, parts):
    tok, width = after_attn.shape
    blk = 256
    row = pl.BlockSpec((blk, width), lambda i: (i, 0))
    one = pl.BlockSpec((1, width), lambda i: (0, 0))
    slots = sum(p.shape[0] for p in parts)
    return pl.pallas_call(
        return_kernel,
        grid=(tok // blk,),
        in_specs=[pl.BlockSpec((blk, 4), lambda i: (i, 0)), row, row, one]
        + [pl.BlockSpec(p.shape, lambda i: (0, 0)) for p in parts],
        out_specs=[row, row, one],
        out_shape=[
            jax.ShapeDtypeStruct((tok, width), F32),
            jax.ShapeDtypeStruct((tok, width), BF16),
            jax.ShapeDtypeStruct((1, width), F32),
        ],
        compiler_params=params(),
        cost_estimate=cost(2 * tok * slots * width, 16 * tok * width),
        name="return_rows",
    )(pos_cols, after_attn, cotangent, gain, *parts)


def expert_kernel(experts, aliased, *refs):
    me_ref, x_ref, c_ref, d_ref, wg_ref, wu_ref, wr_ref, wrt_ref = refs[:8]
    refs = refs[8 + (3 if aliased else 0) :]
    act_ref, dg_ref, du_ref, out_ref, deo_ref, own_ref, gr_ref = refs[:7]
    acc_ref, gate_ref, prob_ref, p_ref = refs[7:]
    j = pl.program_id(0)
    rows_all = x_ref.shape[0]
    n_src, _, short, tile = d_ref.shape
    width = x_ref.shape[1]
    lane = lax.broadcasted_iota(jnp.int32, (rows_all, LANES), 1)

    @pl.when(j == 0)
    def _():
        logits = dot_f32(x_ref[...], wr_ref[...], NN)
        logits = jnp.where(lane < experts, logits, -1e30)
        exps = jnp.exp(logits - jnp.max(logits, axis=-1, keepdims=True))
        probs = exps / jnp.sum(exps, axis=-1, keepdims=True)
        prob_ref[...] = probs
        own = jnp.sum(jnp.where(lane == me_ref[1], probs, 0.0), axis=-1, keepdims=True)
        p_ref[...] = jnp.broadcast_to(own, p_ref.shape)
        own_ref[...] = p_ref[...].reshape(n_src, 1, short, LANES)
        wide = jnp.concatenate([p_ref[...]] * (width // LANES), axis=1)
        deo_ref[...] = (c_ref[...].reshape(rows_all, width).astype(F32) * wide).astype(BF16)
        acc_ref[...] = jnp.zeros_like(acc_ref)
        gate_ref[...] = jnp.zeros_like(gate_ref)

    group = 4
    reps = tile // LANES

    def forward(b):
        x = x_ref[group * b * short : group * (b + 1) * short, :]
        return dot_f32(x, wg_ref[...], NN), dot_f32(x, wu_ref[...], NN)

    n_blk = n_src // group
    ahead = forward(0)
    for b in range(n_blk):
        rows = slice(group * b * short, group * (b + 1) * short)
        z, up = ahead
        ahead = forward(b + 1) if b + 1 < n_blk else None
        back = d_ref[group * b : group * (b + 1)].reshape(group * short, tile).astype(F32)
        own = jnp.concatenate([p_ref[rows, :]] * reps, axis=1)
        zz = z * z
        th = jnp.tanh(GELU_C * z * (1.0 + GELU_A * zz))
        half = 0.5 + 0.5 * th
        gelu = z * half
        slope = half + 0.5 * GELU_C * z * (1.0 - th * th) * (1.0 + 3.0 * GELU_A * zz)
        act = (gelu * up).astype(BF16)
        act_ref[rows, :] = act
        share = act.astype(F32) * back
        gate_ref[rows, :] += sum(share[:, i * LANES : (i + 1) * LANES] for i in range(reps))
        dact = back * own
        dg = (dact * up * slope).astype(BF16)
        du = (dact * gelu).astype(BF16)
        dg_ref[rows, :] = dg
        du_ref[rows, :] = du
        acc_ref[rows, :] += dot_f32(dg, wg_ref[...], NT) + dot_f32(du, wu_ref[...], NT)

    @pl.when(j == pl.num_programs(0) - 1)
    def _():
        dgate = jnp.sum(gate_ref[...], axis=-1, keepdims=True)
        dl = dgate * p_ref[...] * (jnp.where(lane == me_ref[1], 1.0, 0.0) - prob_ref[...])
        dl = dl.astype(BF16)
        out_ref[...] = (acc_ref[...] + dot_f32(dl, wrt_ref[...], NN)).astype(BF16)
        gr_ref[...] = dot_f32(dl, x_ref[...], TN)[: gr_ref.shape[0], :]


def expert_chunk(me, rows, cot, dact, w_gate_up, wr_pad, wr_pad_t, experts, c, total_rows, earlier):
    n_src, chunks, short, width = cot.shape
    ff = dact.shape[-1]
    tile = 256
    steps = ff // tile
    n_rows = rows.shape[0]
    whole = pl.BlockSpec(memory_space=pl.ANY)
    part = pl.BlockSpec((n_rows, tile), lambda j, m: (c, j))
    aliased = earlier is not None
    few = -(-experts // 8) * 8
    call = pl.pallas_call(
        functools.partial(expert_kernel, experts, aliased),
        grid_spec=pltpu.PrefetchScalarGridSpec(
            num_scalar_prefetch=1,
            grid=(steps,),
            in_specs=[
                pl.BlockSpec((n_rows, width), lambda j, m: (0, 0)),
                pl.BlockSpec((n_src, 1, short, width), lambda j, m: (0, c, 0, 0)),
                pl.BlockSpec((n_src, 1, short, tile), lambda j, m: (0, c, 0, j)),
                pl.BlockSpec((width, tile), lambda j, m: (0, j)),
                pl.BlockSpec((width, tile), lambda j, m: (0, j + steps)),
                pl.BlockSpec((width, LANES), lambda j, m: (0, 0)),
                pl.BlockSpec((LANES, width), lambda j, m: (0, 0)),
            ]
            + ([whole] * 3 if aliased else []),
            out_specs=[
                part,
                part,
                part,
                pl.BlockSpec((n_rows, width), lambda j, m: (0, 0)),
                pl.BlockSpec((n_rows, width), lambda j, m: (0, 0)),
                pl.BlockSpec((n_src, 1, short, LANES), lambda j, m: (0, 0, 0, 0)),
                pl.BlockSpec((few, width), lambda j, m: (0, 0)),
            ],
            scratch_shapes=[
                pltpu.VMEM((n_rows, width), F32),
                pltpu.VMEM((n_rows, LANES), F32),
                pltpu.VMEM((n_rows, LANES), F32),
                pltpu.VMEM((n_rows, LANES), F32),
            ],
        ),
        out_shape=[jax.ShapeDtypeStruct((total_rows, ff), BF16)] * 3
        + [
            jax.ShapeDtypeStruct((n_rows, width), BF16),
            jax.ShapeDtypeStruct((n_rows, width), BF16),
            jax.ShapeDtypeStruct((n_src, 1, short, LANES), F32),
            jax.ShapeDtypeStruct((few, width), F32),
        ],
        input_output_aliases={8: 0, 9: 1, 10: 2} if aliased else {},
        compiler_params=params(),
        cost_estimate=cost(
            8 * n_rows * width * ff, 4 * width * ff + 10 * n_rows * ff + 4 * n_rows * width, n_rows * ff
        ),
        name="expert_rows",
    )
    out = call(me, rows, cot, dact, w_gate_up, w_gate_up, wr_pad, wr_pad_t, *(earlier if aliased else ()))
    return out[:3], out[3:]


def gated_kernel(act_ref, w_ref, own_ref, out_ref):
    n_rows, tile = out_ref.shape
    own = jnp.concatenate([own_ref[...].reshape(n_rows, LANES)] * (tile // LANES), axis=1)
    out_ref[...] = (dot_f32(act_ref[...], w_ref[...], NN) * own).astype(BF16)


def gated_rows(act, w_eo, own, c, chunks):
    total, ff = act.shape
    width = w_eo.shape[1]
    n_rows, tile = total // chunks, 256
    return pl.pallas_call(
        gated_kernel,
        grid=(width // tile,),
        in_specs=[
            pl.BlockSpec((n_rows, ff), lambda j: (c, 0)),
            pl.BlockSpec((ff, tile), lambda j: (0, j)),
            pl.BlockSpec(own.shape, lambda j: (0, 0, 0, 0)),
        ],
        out_specs=pl.BlockSpec((n_rows, tile), lambda j: (0, j)),
        out_shape=jax.ShapeDtypeStruct((n_rows, width), BF16),
        compiler_params=params(),
        cost_estimate=cost(2 * n_rows * ff * width, 2 * n_rows * (ff + width) + 2 * ff * width),
        name="gated_rows",
    )(act, w_eo, own)


def share_rows(me_g, n_g, full_ref, keep_ref, send_ref):
    rows = full_ref.shape[0] // n_g
    for r_g in range(n_g):
        at = pl.multiple_of((me_g ^ r_g) * rows, rows)
        out = send_ref if r_g & 1 else keep_ref
        block = full_ref[pl.ds(at, rows), :].astype(BF16)
        if len(out.shape) == 4:
            out[0, r_g // 2] = block
        else:
            out[r_g // 2] = block


def weight_kernel(n_g, me_ref, a_ref, o_ref, b0_ref, b1_ref, b2_ref, d_ref, keep_ref, send_ref, full_ref, at_ref, ot_ref):
    @pl.when(pl.program_id(0) == 0)
    def _():
        at_ref[...] = a_ref[...].T
        ot_ref[...] = o_ref[...].T

    b = jnp.concatenate([b0_ref[0], b1_ref[0], b2_ref[0]], axis=1)
    full_ref[:, : 3 * LANES] = dot_f32(at_ref[...], b, NN)
    full_ref[:, 3 * LANES :] = dot_f32(ot_ref[...], d_ref[...], NN)
    share_rows(me_ref[0], n_g, full_ref, keep_ref, send_ref)


def weight_grads(me, a_one, mixed, grad_qkv, grad_low, n_g, n_e):
    tok, width = a_one.shape
    heads_wide = width // LANES
    block = pl.BlockSpec((1, n_g // 2, width // n_g, 4 * LANES), lambda r, m: (r, 0, 0, 0))

    def plane(t):
        def index(r, m):
            at = 3 * (m[1] ^ r) + t
            return (at // heads_wide, 0, at % heads_wide)

        return pl.BlockSpec((1, tok, LANES), index)

    return pl.pallas_call(
        functools.partial(weight_kernel, n_g),
        grid_spec=pltpu.PrefetchScalarGridSpec(
            num_scalar_prefetch=1,
            grid=(n_e,),
            in_specs=[
                pl.BlockSpec((tok, width), lambda r, m: (0, 0)),
                pl.BlockSpec((tok, width), lambda r, m: (0, 0)),
                plane(0),
                plane(1),
                plane(2),
                pl.BlockSpec((tok, LANES), lambda r, m: (0, m[1] ^ r)),
            ],
            out_specs=[block, block],
            scratch_shapes=[
                pltpu.VMEM((width, 4 * LANES), F32),
                pltpu.VMEM((width, tok), BF16),
                pltpu.VMEM((width, tok), BF16),
            ],
        ),
        out_shape=[jax.ShapeDtypeStruct((n_e, n_g // 2, width // n_g, 4 * LANES), BF16)] * 2,
        compiler_params=params(),
        cost_estimate=cost(8 * tok * width * width, 12 * tok * width + 8 * width * width),
        name="weight_grads",
    )(me, a_one, mixed, grad_qkv, grad_qkv, grad_qkv, grad_low)


def relative(v, axis, me, n):
    return jnp.stack([lax.dynamic_index_in_dim(v, me ^ r, axis, keepdims=False) for r in range(n)], axis)


def own_blocks(view, me_g, me_e, n_g, n_e):
    view = relative(relative(view, 0, me_e, n_e), 1, me_g, n_g)
    return view[:, 0::2], view[:, 1::2]


def gate_up_kernel(half, n_part, *refs):
    parts, (g_ref, u_ref, out_ref, t_ref) = refs[:n_part], refs[n_part:]
    j = pl.program_id(0)

    @pl.when(j == 0)
    def _():
        at = 0
        for part in parts:
            t_ref[:, at : at + part.shape[0]] = part[...].T
            at += part.shape[0]

    @pl.when(j < half)
    def _():
        out_ref[...] = dot_f32(t_ref[...], g_ref[...], NN).astype(BF16)

    @pl.when(j >= half)
    def _():
        out_ref[...] = dot_f32(t_ref[...], u_ref[...], NN).astype(BF16)


def gate_up_grad(parts, dg, du):
    total, ff = dg.shape
    width = parts[0].shape[1]
    tile = 256
    half = ff // tile
    return pl.pallas_call(
        functools.partial(gate_up_kernel, half, len(parts)),
        grid=(2 * half,),
        in_specs=[pl.BlockSpec(p.shape, lambda j: (0, 0)) for p in parts]
        + [
            pl.BlockSpec((total, tile), lambda j: (0, jnp.minimum(j, half - 1))),
            pl.BlockSpec((total, tile), lambda j: (0, jnp.maximum(j - half, 0))),
        ],
        out_specs=pl.BlockSpec((width, tile), lambda j: (0, j)),
        scratch_shapes=[pltpu.VMEM((width, total), BF16)],
        out_shape=jax.ShapeDtypeStruct((width, 2 * ff), BF16),
        compiler_params=params(),
        cost_estimate=cost(4 * total * width * ff, 2 * total * (width + 2 * ff) + 4 * width * ff),
        name="gate_up_grad",
    )(*parts, dg, du)


def out_grad_kernel(n_part, act_ref, *refs):
    parts, out_ref = refs[:n_part], refs[n_part]
    total, at = None, 0
    for part in parts:
        n = part.shape[0]
        term = dot_f32(act_ref[at : at + n, :], part[...], TN)
        total = term if total is None else total + term
        at += n
    out_ref[...] = total.astype(BF16)


def out_grad(act, parts):
    total, ff = act.shape
    width = parts[0].shape[1]
    tile = 256
    return pl.pallas_call(
        functools.partial(out_grad_kernel, len(parts)),
        grid=(ff // tile,),
        in_specs=[pl.BlockSpec((total, tile), lambda j: (0, j))]
        + [pl.BlockSpec(p.shape, lambda j: (0, 0)) for p in parts],
        out_specs=pl.BlockSpec((tile, width), lambda j: (j, 0)),
        out_shape=jax.ShapeDtypeStruct((ff, width), BF16),
        compiler_params=params(),
        cost_estimate=cost(2 * total * width * ff, 2 * total * (width + ff) + 2 * width * ff),
        name="out_grad",
    )(act, *parts)


def fill_mask(start, length, mask_ref):
    tok = mask_ref.shape[0]
    query = lax.broadcasted_iota(jnp.int32, (tok, tok), 0)
    key = lax.broadcasted_iota(jnp.int32, (tok, tok), 1)
    end = start + length
    inside = (query >= start) & (query < end) & (key >= start) & (key < end)
    mask_ref[...] = jnp.where((key <= query) | inside, 0.0, -1e30)


def half_lanes(v, h):
    lane = lax.broadcasted_iota(jnp.int32, v.shape, 1)
    return jnp.where((lane >= LANES // 2) == (h == 1), v, jnp.zeros_like(v))


def forward_kernel(blk, scale, s_ref, q_ref, k_ref, v_ref, b_ref, o_ref, lse_ref, mask_ref):
    tok = q_ref.shape[0]
    pair = pl.program_id(0)

    @pl.when(pair == 0)
    def _():
        fill_mask(s_ref[2], s_ref[3], mask_ref)
        lse_ref[...] = jnp.zeros_like(lse_ref)

    lane = lax.broadcasted_iota(jnp.int32, (blk, LANES), 1)
    values = [half_lanes(v_ref[...], h) for h in range(2)]
    for i in range(tok // blk):
        rows = slice(i * blk, (i + 1) * blk)
        mixed, lse = None, lse_ref[rows, :]
        for h in range(2):
            q = half_lanes(q_ref[rows, :] * scale, h)
            s = dot_f32(q, k_ref[...], NT) + b_ref[h, rows, :].astype(F32) + mask_ref[rows, :]
            top = jnp.max(s, axis=-1, keepdims=True)
            e = jnp.exp(s - top)
            total = jnp.sum(e, axis=-1, keepdims=True)
            p = (e * (1.0 / total)).astype(BF16)
            o = dot_f32(p, values[h], NN)
            mixed = o if mixed is None else mixed + o
            lse = jnp.where(lane == 2 * pair + h, top + jnp.log(total), lse)
        o_ref[rows, :] = mixed.astype(BF16)
        lse_ref[rows, :] = lse


def attention_forward(scalars, qkv, rel_bias, scale):
    tok, width = qkv.shape[0], qkv.shape[1] // 3
    pairs = width // LANES
    column = lambda p: pl.BlockSpec((tok, LANES), lambda i, m: (0, p * pairs + i))
    return pl.pallas_call(
        functools.partial(forward_kernel, 256, scale),
        grid_spec=pltpu.PrefetchScalarGridSpec(
            num_scalar_prefetch=1,
            grid=(pairs,),
            in_specs=[
                column(0),
                column(1),
                column(2),
                pl.BlockSpec((2, tok, tok), lambda i, m: (i, 0, 0)),
            ],
            out_specs=[
                pl.BlockSpec((tok, LANES), lambda i, m: (0, i)),
                pl.BlockSpec((tok, LANES), lambda i, m: (0, 0)),
            ],
            scratch_shapes=[pltpu.VMEM((tok, tok), F32)],
        ),
        out_shape=[
            jax.ShapeDtypeStruct((tok, width), BF16),
            jax.ShapeDtypeStruct((tok, LANES), F32),
        ],
        compiler_params=params(),
        cost_estimate=cost(8 * tok * tok * width, 8 * tok * width + 32 * tok * tok, 16 * tok * tok),
        name="attention_forward",
    )(scalars, qkv, qkv, qkv, rel_bias)


def backward_kernel(n_g, scale, per_owner, s_ref, q_ref, k_ref, v_ref, do_ref, b_ref, lse_ref, *refs):
    outs, (dqkv_ref, mask_ref, low_ref) = refs[:-3], refs[-3:]
    tok = q_ref.shape[0]
    rows = tok // n_g
    pair = s_ref[1] ^ pl.program_id(0) if per_owner else pl.program_id(0)

    @pl.when(pl.program_id(0) == 0)
    def _():
        fill_mask(s_ref[2], s_ref[3], mask_ref)

    both = 2 * rows
    lane = lax.broadcasted_iota(jnp.int32, (both, LANES), 1)
    keys = [half_lanes(k_ref[...], h) for h in range(2)]
    grad_k = grad_v = None
    for x in range(n_g // 2):
        turn = (s_ref[0] // 2) ^ x if per_owner else x
        here = pl.ds(pl.multiple_of(turn * both, both), both)
        grad_q = None
        for h in range(2):
            q = half_lanes(q_ref[here, :] * scale, h)
            do = half_lanes(do_ref[here, :], h)
            lse = jnp.sum(jnp.where(lane == 2 * pair + h, lse_ref[here, :], 0.0), axis=-1, keepdims=True)
            s = dot_f32(q, k_ref[...], NT) + b_ref[h, here, :].astype(F32) + mask_ref[here, :]
            p = jnp.exp(s - lse)
            dp = dot_f32(do, v_ref[...], NT)
            ds = p * (dp - jnp.sum(p * dp, axis=-1, keepdims=True))
            ds = ds.astype(BF16)
            if per_owner:
                low_ref[h] = ds
                for side in range(2):
                    half = pl.ds(pl.multiple_of(((s_ref[0] % 2) ^ side) * rows, rows), rows)
                    outs[side][0, x, h * rows : (h + 1) * rows, :] = low_ref[h, half, :]
            else:
                outs[0][h, here, :] = ds
            dv = dot_f32(p.astype(BF16), do, TN)
            dk = dot_f32(ds, q, TN)
            dq = dot_f32(ds, keys[h], NN)
            grad_v = dv if grad_v is None else grad_v + dv
            grad_k = dk if grad_k is None else grad_k + dk
            grad_q = dq if grad_q is None else grad_q + dq
        dqkv_ref[0, here, :] = (grad_q * scale).astype(BF16)
    dqkv_ref[1] = grad_k.astype(BF16)
    dqkv_ref[2] = grad_v.astype(BF16)


def attention_backward(scalars, qkv, grad_mixed, rel_bias, lse, scale, n_g, n_e, per_owner):
    tok, width = grad_mixed.shape
    pairs = width // LANES
    turn = (lambda i, m: m[1] ^ i) if per_owner else (lambda i, m: i)
    column = lambda p: pl.BlockSpec((tok, LANES), lambda i, m: (0, p * pairs + turn(i, m)))
    if per_owner:
        block = pl.BlockSpec((1, n_g // 2, 2 * tok // n_g, tok), lambda i, m: (i, 0, 0, 0))
        bias_specs = [block, block]
        bias_shapes = [jax.ShapeDtypeStruct((n_e, n_g // 2, 2 * tok // n_g, tok), BF16)] * 2
    else:
        bias_specs = [pl.BlockSpec((2, tok, tok), lambda i, m: (i, 0, 0))]
        bias_shapes = [jax.ShapeDtypeStruct((2 * pairs, tok, tok), BF16)]
    return pl.pallas_call(
        functools.partial(backward_kernel, n_g, scale, per_owner),
        grid_spec=pltpu.PrefetchScalarGridSpec(
            num_scalar_prefetch=1,
            grid=(pairs,),
            in_specs=[
                column(0),
                column(1),
                column(2),
                column(0),
                pl.BlockSpec((2, tok, tok), lambda i, m: (turn(i, m), 0, 0)),
                pl.BlockSpec((tok, LANES), lambda i, m: (0, 0)),
            ],
            out_specs=bias_specs + [pl.BlockSpec((3, tok, LANES), lambda i, m: (0, 0, turn(i, m)))],
            scratch_shapes=[pltpu.VMEM((tok, tok), F32), pltpu.VMEM((2, 2 * tok // n_g, tok), BF16)],
        ),
        out_shape=bias_shapes + [jax.ShapeDtypeStruct((3, tok, width), BF16)],
        compiler_params=params(),
        cost_estimate=cost(20 * tok * tok * width, 16 * tok * width + 64 * tok * tok, 16 * tok * tok),
        name="attention_backward",
    )(scalars, qkv, qkv, qkv, grad_mixed, rel_bias, lse)


def norm_forward(values):
    inverse = lax.rsqrt(jnp.mean(values * values, axis=-1, keepdims=True) + EPSILON)
    return (values * inverse, inverse)


def norm_backward(grad_out, normed, inverse, norm_gain):
    grad_normed = grad_out * norm_gain
    grad_gain = jnp.sum(grad_out * normed, axis=0)
    grad_input = inverse * (
        grad_normed - normed * jnp.mean(grad_normed * normed, axis=-1, keepdims=True)
    )
    return (grad_input, grad_gain)


def body(
    tokens,
    cotangent,
    w_qkv,
    w_out_attn,
    rel_bias,
    norm_gains,
    w_router,
    w_gate_up,
    w_expert_out,
    routes,
    spans,
):
    tok, width = tokens.shape
    n_g, n_e = lax.axis_size("grp"), lax.axis_size("ep")
    assert w_gate_up.shape[0] == 1 and spans.shape[0] == 1 and tok == LENGTH
    assert n_g & (n_g - 1) == 0 and n_e & (n_e - 1) == 0 and n_g > 1 and n_e > 3
    assert width == HEADS * LANES // 2
    experts = n_e
    cap = 5 * routes.shape[1] * tok // (4 * experts)
    chunks = 2 if cap % 32 == 0 else 1
    short = cap // chunks
    slots = experts * cap
    scale = 1.0 / math.sqrt(width // HEADS)
    me_g, me_e = lax.axis_index("grp"), lax.axis_index("ep")
    me = jnp.stack([me_g, me_e, spans[0, 0], spans[0, 1]]).astype(jnp.int32)
    w_gu, w_eo = w_gate_up[0], w_expert_out[0]

    pos, cot_out = place(routes.T, cotangent, experts, cap, chunks)
    pos_cols = pos.T
    tokens = after(tokens, cot_out)
    cot_rows = swap_rows(cot_out)

    hidden = tokens.astype(F32)
    normed_one, inverse_one = norm_forward(hidden)
    a_one = (normed_one * norm_gains[0]).astype(BF16)
    qkv_rows = dot_f32(a_one, w_qkv, NN).astype(BF16)
    mixed_heads, lse = attention_forward(me, qkv_rows, rel_bias, scale)
    after_attn = hidden + dot_f32(mixed_heads, w_out_attn, NN)
    normed_two, _ = norm_forward(after_attn)
    a_two = (normed_two * norm_gains[1]).astype(BF16)

    parts = dispatch(pos, after(a_two, cot_rows), slots, chunks)
    dact = dot_f32(cot_rows, w_eo, NT).astype(BF16)
    parts = [swap_rows(p if c == 0 else after(p, dact)) for c, p in enumerate(parts)]
    dact = dact.reshape(n_e, chunks, short, -1)
    cot_view = cot_rows.reshape(n_e, chunks, short, width)
    wr_pad = jnp.pad(w_router, ((0, 0), (0, LANES - experts)))
    wr_pad_t = wr_pad.T
    state, back, deos, owns, grad_route = None, [], [], [], 0.0
    for c in range(chunks):
        state, (dxe, deo, own, gr) = expert_chunk(
            me, parts[c], cot_view, dact, w_gu, wr_pad, wr_pad_t, experts, c, slots, state
        )
        back.append(swap_rows(dxe))
        deos.append(deo)
        owns.append(own)
        grad_route = grad_route + gr[:experts]
    act, dg, du = state

    core = ("grp", 1)
    share = lambda v: lax.psum_scatter(v, "grp", scatter_dimension=0, tiled=True)
    act = after(act, *back[:-1])
    gated = [gated_rows(act, w_eo, own, c, chunks) for c, own in enumerate(owns)]
    gate_full = gate_up_grad(parts, after(dg, *gated), du)
    gate = share(after(gate_full, *back))

    grad_after, grad_attn_low, grad_gain_two = return_grads(
        pos_cols, after(after_attn, gate_full), cotangent, norm_gains[1:], back
    )
    gated = [swap_rows(after(gated[0], *back))] + gated[1:]
    gated[1:] = [swap_rows(after(g, gated[0])) for g in gated[1:]]
    grad_mixed = dot_f32(grad_attn_low, w_out_attn, NT).astype(BF16)
    rows_g, rows_t = width // n_g, tok // n_g
    per_owner = n_e * LANES == width
    orders = halving_orders(n_g, n_e)
    *grad_bias, grad_qkv = attention_backward(
        me, qkv_rows, grad_mixed, rel_bias, lse, scale, n_g, n_e, per_owner
    )
    if not per_owner:
        bias = grad_bias[0].reshape(n_e, HEADS // n_e, n_g, rows_t, tok).transpose(0, 2, 1, 3, 4)
        grad_bias = own_blocks(bias.reshape(n_e, n_g, -1, tok), me_g, me_e, n_g, n_e)
    got = xor_send(after(grad_bias[1], gated[0]), *core)
    grad_a_one = sum(
        dot_f32(grad_qkv[i], w_qkv[:, i * width : (i + 1) * width], NT) for i in range(3)
    )
    bias = first_sums(after(grad_bias[0], grad_a_one), got, orders)
    grad_qkv_late = after(grad_qkv, bias[0][0])
    bias = send_all(bias)
    if per_owner:
        weights = weight_grads(me, a_one, mixed_heads, grad_qkv_late, grad_attn_low, n_g, n_e)
    else:
        flat = jnp.concatenate([grad_qkv_late[i] for i in range(3)], axis=1)
        full = [dot_f32(a_one, flat, TN), dot_f32(mixed_heads, grad_attn_low, TN)]
        full = [f.astype(BF16).reshape(n_g, rows_g, n_e, -1) for f in full]
        full = jnp.concatenate(full, axis=-1).transpose(2, 0, 1, 3)
        weights = own_blocks(full, me_g, me_e, n_g, n_e)
    out_full = out_grad(act, [after(deos[0], weights[0])] + deos[1:])
    grad_norm_one, grad_gain_one = norm_backward(grad_a_one, normed_one, inverse_one, norm_gains[0])
    small = jnp.concatenate([grad_gain_one[None], grad_gain_two, grad_route])
    small_steps = [core] + orders[0]
    small_got = xor_send(small, *core)
    got = xor_send(after(weights[1], *[way[1] for way in bias], *gated), *core)
    small = small + after(small_got, out_full)
    weights = first_sums(after(weights[0], out_full, small), got, orders)
    first_keep = weights[0][0]
    expert_out = share(after(out_full, first_keep))
    weights = send_all(weights)
    output = combine(pos_cols, after(after_attn, first_keep), gated)
    grad_tokens = grad_after + grad_norm_one
    grad_w_gate = after(gate, first_keep).astype(F32)[None]
    wide = 3 * width // n_e
    merged = [[bias, weights]] if bias[0][0].shape == weights[0][0].shape else [[bias], [weights]]
    ways, pair = None, (small, xor_send(small, *small_steps[1]))
    for i, step in enumerate(small_steps[2:]):
        done = []
        for j, sets in enumerate(merged):
            one, new = next_sums(sets, () if j else pair)
            done.append(send_all(one))
            pair = (new[0], xor_send(new[0], *step)) if new else pair
        if i == 0:
            done[0] = tied(done[0], grad_w_gate, grad_tokens)
        if i == len(small_steps) - 4:
            done[0] = tied(done[0], output)
        merged = [[one] for one in done]
    ways = done
    small = pair[0] + pair[1]
    grad_w_expert = expert_out.astype(F32)[None]
    ways[0] = tied(ways[0], grad_w_expert)
    if len(ways) == 1:
        g_bias, g_qkv, g_out = last_merged(ways[0], wide)
    else:
        g_bias, g_weights = [jnp.concatenate(last_sums(w)) for w in ways]
        g_qkv, g_out = g_weights[:, :wide], g_weights[:, wide:]
    g_bias = g_bias.reshape(HEADS // n_e, rows_t, tok)
    return (
        output,
        grad_tokens,
        g_qkv,
        g_out,
        g_bias,
        small[:2],
        small[2:].T,
        grad_w_gate,
        grad_w_expert,
    )


def solution(mesh):
    placed = (
        P(("grp", "ep"), None),
        P(("grp", "ep"), None),
        P(),
        P(),
        P(),
        P(),
        P(),
        P("ep", None, None),
        P("ep", None, None),
        P(("grp", "ep"), None),
        P(("grp", "ep"), None),
    )
    return jax.shard_map(
        body,
        mesh=mesh,
        in_specs=placed,
        out_specs=(
            P(("grp", "ep"), None),
            P(("grp", "ep"), None),
            P("grp", "ep"),
            P("grp", "ep"),
            P("ep", "grp", None),
            P(),
            P(),
            P("ep", "grp", None),
            P("ep", "grp", None),
        ),
        check_vma=False,
    )
```

```python
import functools
import math

import jax
import jax.numpy as jnp
from jax import lax
from jax.experimental import pallas as pl
from jax.experimental.pallas import tpu as pltpu
from jax.sharding import PartitionSpec as P

HEADS = 16
LENGTH = 512
EPSILON = 1e-06
LANES = 128
GELU_C = math.sqrt(2.0 / math.pi)
GELU_A = 0.044715
F32 = jnp.float32
BF16 = jnp.bfloat16
VMEM_LIMIT = 60 * 1024 * 1024


def params(**kw):
    return pltpu.CompilerParams(vmem_limit_bytes=VMEM_LIMIT, **kw)


def cost(flops, nbytes, trans=0):
    return pl.CostEstimate(flops=int(flops), bytes_accessed=int(nbytes), transcendentals=int(trans))


def dot_f32(a, b, dims):
    return lax.dot_general(a, b, (dims, ((), ())), preferred_element_type=F32)


NN = ((1,), (0,))
NT = ((1,), (1,))
TN = ((0,), (0,))


def xor_send(v, axis, k):
    n = lax.axis_size(axis)
    return lax.ppermute(v, axis, [(i, i ^ k) for i in range(n)])


def swap_rows(v):
    return lax.all_to_all(v, "ep", split_axis=0, concat_axis=0, tiled=True)


def bits_of(n):
    return [1 << i for i in range(n.bit_length() - 1)]


def after(value, *others):
    return lax.optimization_barrier((value, *others))[0]


def halving_orders(n_g, n_e):
    g_bits = [("grp", k) for k in bits_of(n_g)]
    e_bits = [("ep", k) for k in bits_of(n_e)]
    rest, first, others = g_bits[1:], e_bits[:1], e_bits[1:]
    near, far = others[:1], others[1:]
    return [first + near + rest + far, near + first + far + rest, rest + first + others]


def row_cuts(rows):
    unit = rows // 16
    return [0, 16 * round(7 * unit / 16), 16 * round(3 * unit / 4), rows]


def first_kernel(orders, cuts, k_ref, g_ref, *outs):
    n_e, n_x = k_ref.shape[:2]
    at = 0
    for order, lo, hi in zip(orders, cuts, cuts[1:]):
        if lo == hi:
            continue
        for r in range(n_e):
            for x in range(n_x):
                bits = [(2 * x // k) % 2 if axis == "grp" else (r // k) % 2 for axis, k in order]
                index = 0
                for bit in bits[1:]:
                    index = 2 * index + bit
                total = k_ref[r, x, lo:hi, :].astype(F32) + g_ref[r, x, lo:hi, :].astype(F32)
                outs[at + bits[0]][index] = total.astype(BF16)
        at += 2


def first_sums(keep, got, orders):
    n_e, n_x, rows, cols = keep.shape
    cuts = row_cuts(rows)
    used = [(o, hi - lo) for o, lo, hi in zip(orders, cuts, cuts[1:]) if hi > lo]
    half = n_e * n_x // 2
    shapes = [jax.ShapeDtypeStruct((half, n, cols), BF16) for _, n in used for _ in range(2)]
    out = pl.pallas_call(
        functools.partial(first_kernel, orders, cuts),
        out_shape=shapes,
        compiler_params=params(),
        cost_estimate=cost(n_e * n_x * rows * cols, 6 * n_e * n_x * rows * cols),
        name="first_sums",
    )(keep, got)
    return [(out[2 * i], out[2 * i + 1], o) for i, (o, _) in enumerate(used)]


def split_kernel(n_way, n_set, n_small, *refs):
    ins, refs = refs[: 2 * n_way * n_set], refs[2 * n_way * n_set :]
    small, outs = refs[: 2 * n_small], refs[2 * n_small :]
    if n_small:
        outs[-1][...] = small[0][...] + small[1][...]
    for w in range(n_way):
        keep_ref, send_ref = outs[2 * w : 2 * w + 2]
        half, at = keep_ref.shape[0], 0
        for i in range(n_set):
            k_ref, g_ref = ins[2 * (w * n_set + i) : 2 * (w * n_set + i) + 2]
            to = at + k_ref.shape[1]
            keep_ref[:, at:to, :] = (k_ref[:half].astype(F32) + g_ref[:half].astype(F32)).astype(BF16)
            send_ref[:, at:to, :] = (k_ref[half:].astype(F32) + g_ref[half:].astype(F32)).astype(BF16)
            at = to


def next_sums(sets, small=()):
    ways = list(zip(*sets))
    shapes = []
    for way in ways:
        blocks, _, cols = way[0][0].shape
        shape = jax.ShapeDtypeStruct((blocks // 2, sum(one[0].shape[1] for one in way), cols), BF16)
        shapes += [shape, shape]
    ins = [v for way in ways for one in way for v in one[:2]]
    total = sum(math.prod(s.shape) for s in shapes)
    out = pl.pallas_call(
        functools.partial(split_kernel, len(ways), len(sets), len(small) // 2),
        out_shape=shapes + [jax.ShapeDtypeStruct(v.shape, v.dtype) for v in small[:1]],
        compiler_params=params(),
        cost_estimate=cost(total, 6 * total),
        name="split_sums",
    )(*ins, *small)
    ways = [(out[2 * i], out[2 * i + 1], way[0][2]) for i, way in enumerate(ways)]
    return ways, out[2 * len(ways) :]


def send_all(ways):
    return [(keep, xor_send(send, *order[0]), order[1:]) for keep, send, order in ways]


def last_sums(ways):
    return [(keep[0].astype(F32) + got[0].astype(F32)) for keep, got, _ in ways]


def last_kernel(*refs):
    ins, (bias_ref, qkv_ref, out_ref) = refs[:-3], refs[-3:]
    wide = qkv_ref.shape[1]
    at = 0
    for k_ref, g_ref in zip(ins[0::2], ins[1::2]):
        n = k_ref.shape[1] // 2
        total = k_ref[0].astype(F32) + g_ref[0].astype(F32)
        bias_ref[at : at + n, :] = total[:n]
        qkv_ref[at : at + n, :] = total[n:, :wide]
        out_ref[at : at + n, :] = total[n:, wide:]
        at += n


def last_merged(ways, wide):
    rows, cols = sum(w[0].shape[1] for w in ways) // 2, ways[0][0].shape[2]
    return pl.pallas_call(
        last_kernel,
        out_shape=[jax.ShapeDtypeStruct((rows, n), F32) for n in (cols, wide, cols - wide)],
        compiler_params=params(),
        cost_estimate=cost(2 * rows * cols, 16 * rows * cols),
        name="last_sums",
    )(*[v for w in ways for v in w[:2]])


def tied(ways, *others):
    return [(after(ways[0][0], *others), *ways[0][1:])] + ways[1:]


def place_kernel(experts, cap, chunks, routes_ref, v_ref, pos_ref, out_ref):
    tok = v_ref.shape[0]
    short = cap // chunks
    ids = lax.broadcasted_iota(jnp.int32, (LANES, tok), 0)
    named = [ids == routes_ref[k : k + 1, :] for k in range(2)]
    counts = jnp.where(named[0] | named[1], 1.0, 0.0).astype(BF16)
    before = lax.broadcasted_iota(jnp.int32, (tok, tok), 0) < lax.broadcasted_iota(
        jnp.int32, (tok, tok), 1
    )
    earlier = dot_f32(counts, jnp.where(before, 1.0, 0.0).astype(BF16), NN)
    for k in range(2):
        slot = jnp.sum(jnp.where(named[k], earlier, 0.0), axis=0, keepdims=True).astype(jnp.int32)
        owner = routes_ref[k : k + 1, :]
        pos_ref[k : k + 1, :] = owner * cap + slot
        chunk = jnp.zeros_like(slot)
        for c in range(1, chunks):
            chunk += jnp.where(slot >= c * short, 1, 0)
        pos_ref[2 + k : 3 + k, :] = chunk * (experts * short) + owner * short + slot - chunk * short
    first, second = pos_ref[0:1, :], pos_ref[1:2, :]
    rows = lax.broadcasted_iota(jnp.int32, (cap, tok), 0)
    for e in range(experts):
        here = rows + e * cap
        pick = jnp.where((here == first) | (here == second), 1.0, 0.0).astype(BF16)
        out_ref[e * cap : (e + 1) * cap, :] = dot_f32(pick, v_ref[...], NN).astype(BF16)


def place(routes_t, values, experts, cap, chunks):
    tok, width = values.shape
    return pl.pallas_call(
        functools.partial(place_kernel, experts, cap, chunks),
        out_shape=[
            jax.ShapeDtypeStruct((4, tok), jnp.int32),
            jax.ShapeDtypeStruct((experts * cap, width), BF16),
        ],
        compiler_params=params(),
        cost_estimate=cost(2 * experts * cap * tok * width, 2 * tok * width + 2 * experts * cap * width),
        name="place_rows",
    )(routes_t, values)


def dispatch_kernel(pos_ref, v_ref, *outs):
    tok = v_ref.shape[0]
    first, second = pos_ref[2:3, :], pos_ref[3:4, :]
    at = 0
    for out in outs:
        total = out.shape[0]
        step = total // 4
        rows = lax.broadcasted_iota(jnp.int32, (step, tok), 0)
        for b in range(4):
            here = rows + at
            pick = jnp.where((here == first) | (here == second), 1.0, 0.0).astype(BF16)
            out[b * step : (b + 1) * step, :] = dot_f32(pick, v_ref[...], NN).astype(BF16)
            at += step


def dispatch(pos, values, slots, chunks):
    tok, width = values.shape
    return pl.pallas_call(
        dispatch_kernel,
        out_shape=[jax.ShapeDtypeStruct((slots // chunks, width), BF16)] * chunks,
        compiler_params=params(),
        cost_estimate=cost(2 * slots * tok * width, 2 * tok * width + 2 * slots * width),
        name="dispatch_rows",
    )(pos, values)


def gathered(first, second, parts):
    total, at = None, 0
    for part in parts:
        n = part.shape[0]
        here = lax.broadcasted_iota(jnp.int32, (first.shape[0], n), 1) + at
        pick = jnp.where((here == first) | (here == second), 1.0, 0.0).astype(BF16)
        term = dot_f32(pick, part[...], NN)
        total = term if total is None else total + term
        at += n
    return total


def combine_kernel(pos_ref, x_ref, *refs):
    parts, out_ref = refs[:-1], refs[-1]
    out_ref[...] = x_ref[...] + gathered(pos_ref[:, 2:3], pos_ref[:, 3:4], parts)


def combine(pos_cols, after_attn, gated):
    tok, width = after_attn.shape
    blk = 256
    return pl.pallas_call(
        combine_kernel,
        grid=(tok // blk,),
        in_specs=[
            pl.BlockSpec((blk, 4), lambda i: (i, 0)),
            pl.BlockSpec((blk, width), lambda i: (i, 0)),
        ]
        + [pl.BlockSpec(g.shape, lambda i: (0, 0)) for g in gated],
        out_specs=pl.BlockSpec((blk, width), lambda i: (i, 0)),
        out_shape=jax.ShapeDtypeStruct((tok, width), F32),
        compiler_params=params(),
        cost_estimate=cost(4 * tok * gated[0].shape[0] * width, 10 * tok * width),
        name="combine_rows",
    )(pos_cols, after_attn, *gated)


def return_kernel(pos_ref, x_ref, cot_ref, gain_ref, *refs):
    parts, (dx_ref, low_ref, gg_ref) = refs[:-3], refs[-3:]
    grad = gathered(pos_ref[:, 2:3], pos_ref[:, 3:4], parts)
    x = x_ref[...]
    inverse = lax.rsqrt(jnp.mean(x * x, axis=-1, keepdims=True) + EPSILON)
    normed = x * inverse
    grad_normed = grad * gain_ref[...]
    dx = cot_ref[...].astype(F32) + inverse * (
        grad_normed - normed * jnp.mean(grad_normed * normed, axis=-1, keepdims=True)
    )
    dx_ref[...] = dx
    low_ref[...] = dx.astype(BF16)

    @pl.when(pl.program_id(0) == 0)
    def _():
        gg_ref[...] = jnp.zeros_like(gg_ref)

    gg_ref[...] += jnp.sum(grad * normed, axis=0, keepdims=True)


def return_grads(pos_cols, after_attn, cotangent, gain, parts):
    tok, width = after_attn.shape
    blk = 256
    row = pl.BlockSpec((blk, width), lambda i: (i, 0))
    one = pl.BlockSpec((1, width), lambda i: (0, 0))
    slots = sum(p.shape[0] for p in parts)
    return pl.pallas_call(
        return_kernel,
        grid=(tok // blk,),
        in_specs=[pl.BlockSpec((blk, 4), lambda i: (i, 0)), row, row, one]
        + [pl.BlockSpec(p.shape, lambda i: (0, 0)) for p in parts],
        out_specs=[row, row, one],
        out_shape=[
            jax.ShapeDtypeStruct((tok, width), F32),
            jax.ShapeDtypeStruct((tok, width), BF16),
            jax.ShapeDtypeStruct((1, width), F32),
        ],
        compiler_params=params(),
        cost_estimate=cost(2 * tok * slots * width, 16 * tok * width),
        name="return_rows",
    )(pos_cols, after_attn, cotangent, gain, *parts)


def expert_kernel(experts, aliased, *refs):
    me_ref, x_ref, c_ref, d_ref, wg_ref, wu_ref, wr_ref, wrt_ref = refs[:8]
    refs = refs[8 + (3 if aliased else 0) :]
    act_ref, dg_ref, du_ref, out_ref, deo_ref, own_ref, gr_ref = refs[:7]
    acc_ref, gate_ref, prob_ref, p_ref = refs[7:]
    j = pl.program_id(0)
    rows_all = x_ref.shape[0]
    n_src, _, short, tile = d_ref.shape
    width = x_ref.shape[1]
    lane = lax.broadcasted_iota(jnp.int32, (rows_all, LANES), 1)

    @pl.when(j == 0)
    def _():
        logits = dot_f32(x_ref[...], wr_ref[...], NN)
        logits = jnp.where(lane < experts, logits, -1e30)
        exps = jnp.exp(logits - jnp.max(logits, axis=-1, keepdims=True))
        probs = exps / jnp.sum(exps, axis=-1, keepdims=True)
        prob_ref[...] = probs
        own = jnp.sum(jnp.where(lane == me_ref[1], probs, 0.0), axis=-1, keepdims=True)
        p_ref[...] = jnp.broadcast_to(own, p_ref.shape)
        own_ref[...] = p_ref[...].reshape(n_src, 1, short, LANES)
        wide = jnp.concatenate([p_ref[...]] * (width // LANES), axis=1)
        deo_ref[...] = (c_ref[...].reshape(rows_all, width).astype(F32) * wide).astype(BF16)
        acc_ref[...] = jnp.zeros_like(acc_ref)
        gate_ref[...] = jnp.zeros_like(gate_ref)

    group = 4
    reps = tile // LANES

    def forward(b):
        x = x_ref[group * b * short : group * (b + 1) * short, :]
        return dot_f32(x, wg_ref[...], NN), dot_f32(x, wu_ref[...], NN)

    n_blk = n_src // group
    ahead = forward(0)
    for b in range(n_blk):
        rows = slice(group * b * short, group * (b + 1) * short)
        z, up = ahead
        ahead = forward(b + 1) if b + 1 < n_blk else None
        back = d_ref[group * b : group * (b + 1)].reshape(group * short, tile).astype(F32)
        own = jnp.concatenate([p_ref[rows, :]] * reps, axis=1)
        zz = z * z
        th = jnp.tanh(GELU_C * z * (1.0 + GELU_A * zz))
        half = 0.5 + 0.5 * th
        gelu = z * half
        slope = half + 0.5 * GELU_C * z * (1.0 - th * th) * (1.0 + 3.0 * GELU_A * zz)
        act = (gelu * up).astype(BF16)
        act_ref[rows, :] = act
        share = act.astype(F32) * back
        gate_ref[rows, :] += sum(share[:, i * LANES : (i + 1) * LANES] for i in range(reps))
        dact = back * own
        dg = (dact * up * slope).astype(BF16)
        du = (dact * gelu).astype(BF16)
        dg_ref[rows, :] = dg
        du_ref[rows, :] = du
        acc_ref[rows, :] += dot_f32(dg, wg_ref[...], NT) + dot_f32(du, wu_ref[...], NT)

    @pl.when(j == pl.num_programs(0) - 1)
    def _():
        dgate = jnp.sum(gate_ref[...], axis=-1, keepdims=True)
        dl = dgate * p_ref[...] * (jnp.where(lane == me_ref[1], 1.0, 0.0) - prob_ref[...])
        dl = dl.astype(BF16)
        out_ref[...] = (acc_ref[...] + dot_f32(dl, wrt_ref[...], NN)).astype(BF16)
        gr_ref[...] = dot_f32(dl, x_ref[...], TN)[: gr_ref.shape[0], :]


def expert_chunk(me, rows, cot, dact, w_gate_up, wr_pad, wr_pad_t, experts, c, total_rows, earlier):
    n_src, chunks, short, width = cot.shape
    ff = dact.shape[-1]
    tile = 256
    steps = ff // tile
    n_rows = rows.shape[0]
    whole = pl.BlockSpec(memory_space=pl.ANY)
    part = pl.BlockSpec((n_rows, tile), lambda j, m: (c, j))
    aliased = earlier is not None
    few = -(-experts // 8) * 8
    call = pl.pallas_call(
        functools.partial(expert_kernel, experts, aliased),
        grid_spec=pltpu.PrefetchScalarGridSpec(
            num_scalar_prefetch=1,
            grid=(steps,),
            in_specs=[
                pl.BlockSpec((n_rows, width), lambda j, m: (0, 0)),
                pl.BlockSpec((n_src, 1, short, width), lambda j, m: (0, c, 0, 0)),
                pl.BlockSpec((n_src, 1, short, tile), lambda j, m: (0, c, 0, j)),
                pl.BlockSpec((width, tile), lambda j, m: (0, j)),
                pl.BlockSpec((width, tile), lambda j, m: (0, j + steps)),
                pl.BlockSpec((width, LANES), lambda j, m: (0, 0)),
                pl.BlockSpec((LANES, width), lambda j, m: (0, 0)),
            ]
            + ([whole] * 3 if aliased else []),
            out_specs=[
                part,
                part,
                part,
                pl.BlockSpec((n_rows, width), lambda j, m: (0, 0)),
                pl.BlockSpec((n_rows, width), lambda j, m: (0, 0)),
                pl.BlockSpec((n_src, 1, short, LANES), lambda j, m: (0, 0, 0, 0)),
                pl.BlockSpec((few, width), lambda j, m: (0, 0)),
            ],
            scratch_shapes=[
                pltpu.VMEM((n_rows, width), F32),
                pltpu.VMEM((n_rows, LANES), F32),
                pltpu.VMEM((n_rows, LANES), F32),
                pltpu.VMEM((n_rows, LANES), F32),
            ],
        ),
        out_shape=[jax.ShapeDtypeStruct((total_rows, ff), BF16)] * 3
        + [
            jax.ShapeDtypeStruct((n_rows, width), BF16),
            jax.ShapeDtypeStruct((n_rows, width), BF16),
            jax.ShapeDtypeStruct((n_src, 1, short, LANES), F32),
            jax.ShapeDtypeStruct((few, width), F32),
        ],
        input_output_aliases={8: 0, 9: 1, 10: 2} if aliased else {},
        compiler_params=params(),
        cost_estimate=cost(
            8 * n_rows * width * ff, 4 * width * ff + 10 * n_rows * ff + 4 * n_rows * width, n_rows * ff
        ),
        name="expert_rows",
    )
    out = call(me, rows, cot, dact, w_gate_up, w_gate_up, wr_pad, wr_pad_t, *(earlier if aliased else ()))
    return out[:3], out[3:]


def gated_kernel(chunks, act_ref, w_ref, *refs):
    owns, outs = refs[:chunks], refs[chunks:]
    for c in range(chunks):

        @pl.when(pl.program_id(0) == c)
        def _():
            n_rows, width = outs[c].shape
            own = jnp.concatenate([owns[c][...].reshape(n_rows, LANES)] * (width // LANES), axis=1)
            outs[c][...] = (dot_f32(act_ref[...], w_ref[...], NN) * own).astype(BF16)


def gated_rows(act, w_eo, owns):
    total, ff = act.shape
    width, chunks = w_eo.shape[1], len(owns)
    n_rows = total // chunks
    return pl.pallas_call(
        functools.partial(gated_kernel, chunks),
        grid=(chunks,),
        in_specs=[
            pl.BlockSpec((n_rows, ff), lambda c: (c, 0)),
            pl.BlockSpec((ff, width), lambda c: (0, 0)),
        ]
        + [pl.BlockSpec(o.shape, lambda c: (0, 0, 0, 0)) for o in owns],
        out_specs=[pl.BlockSpec((n_rows, width), lambda c: (0, 0))] * chunks,
        out_shape=[jax.ShapeDtypeStruct((n_rows, width), BF16)] * chunks,
        compiler_params=params(),
        cost_estimate=cost(2 * total * ff * width, 2 * total * (ff + width) + 2 * ff * width),
        name="gated_rows",
    )(act, w_eo, *owns)


def share_rows(me_g, n_g, full_ref, keep_ref, send_ref):
    rows = full_ref.shape[0] // n_g
    for r_g in range(n_g):
        at = pl.multiple_of((me_g ^ r_g) * rows, rows)
        out = send_ref if r_g & 1 else keep_ref
        block = full_ref[pl.ds(at, rows), :].astype(BF16)
        if len(out.shape) == 4:
            out[0, r_g // 2] = block
        else:
            out[r_g // 2] = block


def weight_kernel(n_g, me_ref, a_ref, o_ref, b0_ref, b1_ref, b2_ref, d_ref, keep_ref, send_ref, full_ref, at_ref, ot_ref):
    @pl.when(pl.program_id(0) == 0)
    def _():
        at_ref[...] = a_ref[...].T
        ot_ref[...] = o_ref[...].T

    b = jnp.concatenate([b0_ref[0], b1_ref[0], b2_ref[0]], axis=1)
    full_ref[:, : 3 * LANES] = dot_f32(at_ref[...], b, NN)
    full_ref[:, 3 * LANES :] = dot_f32(ot_ref[...], d_ref[...], NN)
    share_rows(me_ref[0], n_g, full_ref, keep_ref, send_ref)


def weight_grads(me, a_one, mixed, grad_qkv, grad_low, n_g, n_e):
    tok, width = a_one.shape
    heads_wide = width // LANES
    block = pl.BlockSpec((1, n_g // 2, width // n_g, 4 * LANES), lambda r, m: (r, 0, 0, 0))

    def plane(t):
        def index(r, m):
            at = 3 * (m[1] ^ r) + t
            return (at // heads_wide, 0, at % heads_wide)

        return pl.BlockSpec((1, tok, LANES), index)

    return pl.pallas_call(
        functools.partial(weight_kernel, n_g),
        grid_spec=pltpu.PrefetchScalarGridSpec(
            num_scalar_prefetch=1,
            grid=(n_e,),
            in_specs=[
                pl.BlockSpec((tok, width), lambda r, m: (0, 0)),
                pl.BlockSpec((tok, width), lambda r, m: (0, 0)),
                plane(0),
                plane(1),
                plane(2),
                pl.BlockSpec((tok, LANES), lambda r, m: (0, m[1] ^ r)),
            ],
            out_specs=[block, block],
            scratch_shapes=[
                pltpu.VMEM((width, 4 * LANES), F32),
                pltpu.VMEM((width, tok), BF16),
                pltpu.VMEM((width, tok), BF16),
            ],
        ),
        out_shape=[jax.ShapeDtypeStruct((n_e, n_g // 2, width // n_g, 4 * LANES), BF16)] * 2,
        compiler_params=params(),
        cost_estimate=cost(8 * tok * width * width, 12 * tok * width + 8 * width * width),
        name="weight_grads",
    )(me, a_one, mixed, grad_qkv, grad_qkv, grad_qkv, grad_low)


def relative(v, axis, me, n):
    return jnp.stack([lax.dynamic_index_in_dim(v, me ^ r, axis, keepdims=False) for r in range(n)], axis)


def own_blocks(view, me_g, me_e, n_g, n_e):
    view = relative(relative(view, 0, me_e, n_e), 1, me_g, n_g)
    return view[:, 0::2], view[:, 1::2]


def gate_up_kernel(half, n_part, *refs):
    parts, (g_ref, u_ref, out_ref, t_ref) = refs[:n_part], refs[n_part:]
    j = pl.program_id(0)

    @pl.when(j == 0)
    def _():
        at = 0
        for part in parts:
            t_ref[:, at : at + part.shape[0]] = part[...].T
            at += part.shape[0]

    @pl.when(j < half)
    def _():
        out_ref[...] = dot_f32(t_ref[...], g_ref[...], NN).astype(BF16)

    @pl.when(j >= half)
    def _():
        out_ref[...] = dot_f32(t_ref[...], u_ref[...], NN).astype(BF16)


def gate_up_grad(parts, dg, du):
    total, ff = dg.shape
    width = parts[0].shape[1]
    tile = 256
    half = ff // tile
    return pl.pallas_call(
        functools.partial(gate_up_kernel, half, len(parts)),
        grid=(2 * half,),
        in_specs=[pl.BlockSpec(p.shape, lambda j: (0, 0)) for p in parts]
        + [
            pl.BlockSpec((total, tile), lambda j: (0, jnp.minimum(j, half - 1))),
            pl.BlockSpec((total, tile), lambda j: (0, jnp.maximum(j - half, 0))),
        ],
        out_specs=pl.BlockSpec((width, tile), lambda j: (0, j)),
        scratch_shapes=[pltpu.VMEM((width, total), BF16)],
        out_shape=jax.ShapeDtypeStruct((width, 2 * ff), BF16),
        compiler_params=params(),
        cost_estimate=cost(4 * total * width * ff, 2 * total * (width + 2 * ff) + 4 * width * ff),
        name="gate_up_grad",
    )(*parts, dg, du)


def out_grad_kernel(n_part, act_ref, *refs):
    parts, out_ref = refs[:n_part], refs[n_part]
    total, at = None, 0
    for part in parts:
        n = part.shape[0]
        term = dot_f32(act_ref[at : at + n, :], part[...], TN)
        total = term if total is None else total + term
        at += n
    out_ref[...] = total.astype(BF16)


def out_grad(act, parts):
    total, ff = act.shape
    width = parts[0].shape[1]
    tile = 256
    return pl.pallas_call(
        functools.partial(out_grad_kernel, len(parts)),
        grid=(ff // tile,),
        in_specs=[pl.BlockSpec((total, tile), lambda j: (0, j))]
        + [pl.BlockSpec(p.shape, lambda j: (0, 0)) for p in parts],
        out_specs=pl.BlockSpec((tile, width), lambda j: (j, 0)),
        out_shape=jax.ShapeDtypeStruct((ff, width), BF16),
        compiler_params=params(),
        cost_estimate=cost(2 * total * width * ff, 2 * total * (width + ff) + 2 * width * ff),
        name="out_grad",
    )(act, *parts)


def fill_mask(start, length, mask_ref):
    tok = mask_ref.shape[0]
    query = lax.broadcasted_iota(jnp.int32, (tok, tok), 0)
    key = lax.broadcasted_iota(jnp.int32, (tok, tok), 1)
    end = start + length
    inside = (query >= start) & (query < end) & (key >= start) & (key < end)
    mask_ref[...] = jnp.where((key <= query) | inside, 0.0, -1e30)


def half_lanes(v, h):
    lane = lax.broadcasted_iota(jnp.int32, v.shape, 1)
    return jnp.where((lane >= LANES // 2) == (h == 1), v, jnp.zeros_like(v))


def forward_kernel(blk, scale, s_ref, q_ref, k_ref, v_ref, b_ref, o_ref, lse_ref, mask_ref):
    tok = q_ref.shape[0]
    pair = pl.program_id(0)

    @pl.when(pair == 0)
    def _():
        fill_mask(s_ref[2], s_ref[3], mask_ref)
        lse_ref[...] = jnp.zeros_like(lse_ref)

    lane = lax.broadcasted_iota(jnp.int32, (blk, LANES), 1)
    values = [half_lanes(v_ref[...], h) for h in range(2)]
    for i in range(tok // blk):
        rows = slice(i * blk, (i + 1) * blk)
        mixed, lse = None, lse_ref[rows, :]
        for h in range(2):
            q = half_lanes(q_ref[rows, :] * scale, h)
            s = dot_f32(q, k_ref[...], NT) + b_ref[h, rows, :].astype(F32) + mask_ref[rows, :]
            top = jnp.max(s, axis=-1, keepdims=True)
            e = jnp.exp(s - top)
            total = jnp.sum(e, axis=-1, keepdims=True)
            p = (e * (1.0 / total)).astype(BF16)
            o = dot_f32(p, values[h], NN)
            mixed = o if mixed is None else mixed + o
            lse = jnp.where(lane == 2 * pair + h, top + jnp.log(total), lse)
        o_ref[rows, :] = mixed.astype(BF16)
        lse_ref[rows, :] = lse


def attention_forward(scalars, qkv, rel_bias, scale):
    tok, width = qkv.shape[0], qkv.shape[1] // 3
    pairs = width // LANES
    column = lambda p: pl.BlockSpec((tok, LANES), lambda i, m: (0, p * pairs + i))
    return pl.pallas_call(
        functools.partial(forward_kernel, 256, scale),
        grid_spec=pltpu.PrefetchScalarGridSpec(
            num_scalar_prefetch=1,
            grid=(pairs,),
            in_specs=[
                column(0),
                column(1),
                column(2),
                pl.BlockSpec((2, tok, tok), lambda i, m: (i, 0, 0)),
            ],
            out_specs=[
                pl.BlockSpec((tok, LANES), lambda i, m: (0, i)),
                pl.BlockSpec((tok, LANES), lambda i, m: (0, 0)),
            ],
            scratch_shapes=[pltpu.VMEM((tok, tok), F32)],
        ),
        out_shape=[
            jax.ShapeDtypeStruct((tok, width), BF16),
            jax.ShapeDtypeStruct((tok, LANES), F32),
        ],
        compiler_params=params(),
        cost_estimate=cost(8 * tok * tok * width, 8 * tok * width + 32 * tok * tok, 16 * tok * tok),
        name="attention_forward",
    )(scalars, qkv, qkv, qkv, rel_bias)


def backward_kernel(n_g, scale, per_owner, s_ref, q_ref, k_ref, v_ref, do_ref, b_ref, lse_ref, *refs):
    outs, (dqkv_ref, mask_ref, low_ref) = refs[:-3], refs[-3:]
    tok = q_ref.shape[0]
    rows = tok // n_g
    pair = s_ref[1] ^ pl.program_id(0) if per_owner else pl.program_id(0)

    @pl.when(pl.program_id(0) == 0)
    def _():
        fill_mask(s_ref[2], s_ref[3], mask_ref)

    lane = lax.broadcasted_iota(jnp.int32, (tok, LANES), 1)
    keys = [half_lanes(k_ref[...], h) for h in range(2)]
    grad_k = grad_v = grad_q = None
    for h in range(2):
        q = half_lanes(q_ref[...] * scale, h)
        do = half_lanes(do_ref[...], h)
        lse = jnp.sum(jnp.where(lane == 2 * pair + h, lse_ref[...], 0.0), axis=-1, keepdims=True)
        s = dot_f32(q, k_ref[...], NT) + b_ref[h].astype(F32) + mask_ref[...]
        p = jnp.exp(s - lse)
        dp = dot_f32(do, v_ref[...], NT)
        ds = p * (dp - jnp.sum(p * dp, axis=-1, keepdims=True))
        ds = ds.astype(BF16)
        if per_owner:
            low_ref[h] = ds
            for r_g in range(n_g):
                here = pl.ds(pl.multiple_of((s_ref[0] ^ r_g) * rows, rows), rows)
                outs[r_g & 1][0, r_g // 2, h * rows : (h + 1) * rows, :] = low_ref[h, here, :]
        else:
            outs[0][h] = ds
        dv = dot_f32(p.astype(BF16), do, TN)
        dk = dot_f32(ds, q, TN)
        dq = dot_f32(ds, keys[h], NN)
        grad_v = dv if h == 0 else grad_v + dv
        grad_k = dk if h == 0 else grad_k + dk
        grad_q = dq if h == 0 else grad_q + dq
    dqkv_ref[0] = (grad_q * scale).astype(BF16)
    dqkv_ref[1] = grad_k.astype(BF16)
    dqkv_ref[2] = grad_v.astype(BF16)


def attention_backward(scalars, qkv, grad_mixed, rel_bias, lse, scale, n_g, n_e, per_owner):
    tok, width = grad_mixed.shape
    pairs = width // LANES
    turn = (lambda i, m: m[1] ^ i) if per_owner else (lambda i, m: i)
    column = lambda p: pl.BlockSpec((tok, LANES), lambda i, m: (0, p * pairs + turn(i, m)))
    if per_owner:
        block = pl.BlockSpec((1, n_g // 2, 2 * tok // n_g, tok), lambda i, m: (i, 0, 0, 0))
        bias_specs = [block, block]
        bias_shapes = [jax.ShapeDtypeStruct((n_e, n_g // 2, 2 * tok // n_g, tok), BF16)] * 2
    else:
        bias_specs = [pl.BlockSpec((2, tok, tok), lambda i, m: (i, 0, 0))]
        bias_shapes = [jax.ShapeDtypeStruct((2 * pairs, tok, tok), BF16)]
    return pl.pallas_call(
        functools.partial(backward_kernel, n_g, scale, per_owner),
        grid_spec=pltpu.PrefetchScalarGridSpec(
            num_scalar_prefetch=1,
            grid=(pairs,),
            in_specs=[
                column(0),
                column(1),
                column(2),
                column(0),
                pl.BlockSpec((2, tok, tok), lambda i, m: (turn(i, m), 0, 0)),
                pl.BlockSpec((tok, LANES), lambda i, m: (0, 0)),
            ],
            out_specs=bias_specs + [pl.BlockSpec((3, tok, LANES), lambda i, m: (0, 0, turn(i, m)))],
            scratch_shapes=[pltpu.VMEM((tok, tok), F32), pltpu.VMEM((2, tok, tok), BF16)],
        ),
        out_shape=bias_shapes + [jax.ShapeDtypeStruct((3, tok, width), BF16)],
        compiler_params=params(),
        cost_estimate=cost(20 * tok * tok * width, 16 * tok * width + 64 * tok * tok, 16 * tok * tok),
        name="attention_backward",
    )(scalars, qkv, qkv, qkv, grad_mixed, rel_bias, lse)


def norm_forward(values):
    inverse = lax.rsqrt(jnp.mean(values * values, axis=-1, keepdims=True) + EPSILON)
    return (values * inverse, inverse)


def norm_backward(grad_out, normed, inverse, norm_gain):
    grad_normed = grad_out * norm_gain
    grad_gain = jnp.sum(grad_out * normed, axis=0)
    grad_input = inverse * (
        grad_normed - normed * jnp.mean(grad_normed * normed, axis=-1, keepdims=True)
    )
    return (grad_input, grad_gain)


def body(
    tokens,
    cotangent,
    w_qkv,
    w_out_attn,
    rel_bias,
    norm_gains,
    w_router,
    w_gate_up,
    w_expert_out,
    routes,
    spans,
):
    tok, width = tokens.shape
    n_g, n_e = lax.axis_size("grp"), lax.axis_size("ep")
    assert w_gate_up.shape[0] == 1 and spans.shape[0] == 1 and tok == LENGTH
    assert n_g & (n_g - 1) == 0 and n_e & (n_e - 1) == 0 and n_g > 1 and n_e > 3
    assert width == HEADS * LANES // 2
    experts = n_e
    cap = 5 * routes.shape[1] * tok // (4 * experts)
    chunks = 2 if cap % 32 == 0 else 1
    short = cap // chunks
    slots = experts * cap
    scale = 1.0 / math.sqrt(width // HEADS)
    me_g, me_e = lax.axis_index("grp"), lax.axis_index("ep")
    me = jnp.stack([me_g, me_e, spans[0, 0], spans[0, 1]]).astype(jnp.int32)
    w_gu, w_eo = w_gate_up[0], w_expert_out[0]

    pos, cot_out = place(routes.T, cotangent, experts, cap, chunks)
    pos_cols = pos.T
    tokens = after(tokens, cot_out)
    cot_rows = swap_rows(cot_out)

    hidden = tokens.astype(F32)
    normed_one, inverse_one = norm_forward(hidden)
    a_one = (normed_one * norm_gains[0]).astype(BF16)
    qkv_rows = dot_f32(a_one, w_qkv, NN).astype(BF16)
    mixed_heads, lse = attention_forward(me, qkv_rows, rel_bias, scale)
    after_attn = hidden + dot_f32(mixed_heads, w_out_attn, NN)
    normed_two, _ = norm_forward(after_attn)
    a_two = (normed_two * norm_gains[1]).astype(BF16)

    parts = dispatch(pos, after(a_two, cot_rows), slots, chunks)
    dact = dot_f32(cot_rows, w_eo, NT).astype(BF16)
    parts = [swap_rows(p if c == 0 else after(p, dact)) for c, p in enumerate(parts)]
    dact = dact.reshape(n_e, chunks, short, -1)
    cot_view = cot_rows.reshape(n_e, chunks, short, width)
    wr_pad = jnp.pad(w_router, ((0, 0), (0, LANES - experts)))
    wr_pad_t = wr_pad.T
    state, back, deos, owns, grad_route = None, [], [], [], 0.0
    for c in range(chunks):
        state, (dxe, deo, own, gr) = expert_chunk(
            me, parts[c], cot_view, dact, w_gu, wr_pad, wr_pad_t, experts, c, slots, state
        )
        back.append(swap_rows(dxe))
        deos.append(deo)
        owns.append(own)
        grad_route = grad_route + gr[:experts]
    act, dg, du = state

    core = ("grp", 1)
    share = lambda v: lax.psum_scatter(v, "grp", scatter_dimension=0, tiled=True)
    act = after(act, *back[:-1])
    gated = list(gated_rows(act, w_eo, owns))
    gate_full = gate_up_grad(parts, after(dg, *gated), du)
    gate = share(after(gate_full, *back))

    grad_after, grad_attn_low, grad_gain_two = return_grads(
        pos_cols, after(after_attn, gate_full), cotangent, norm_gains[1:], back
    )
    gated = [swap_rows(after(gated[0], *back))] + gated[1:]
    gated[1:] = [swap_rows(after(g, gated[0])) for g in gated[1:]]
    grad_mixed = dot_f32(grad_attn_low, w_out_attn, NT).astype(BF16)
    rows_g, rows_t = width // n_g, tok // n_g
    per_owner = n_e * LANES == width
    orders = halving_orders(n_g, n_e)
    *grad_bias, grad_qkv = attention_backward(
        me, qkv_rows, grad_mixed, rel_bias, lse, scale, n_g, n_e, per_owner
    )
    if not per_owner:
        bias = grad_bias[0].reshape(n_e, HEADS // n_e, n_g, rows_t, tok).transpose(0, 2, 1, 3, 4)
        grad_bias = own_blocks(bias.reshape(n_e, n_g, -1, tok), me_g, me_e, n_g, n_e)
    got = xor_send(after(grad_bias[1], gated[0]), *core)
    grad_a_one = sum(
        dot_f32(grad_qkv[i], w_qkv[:, i * width : (i + 1) * width], NT) for i in range(3)
    )
    bias = first_sums(after(grad_bias[0], grad_a_one), got, orders)
    grad_qkv_late = after(grad_qkv, bias[0][0])
    bias = send_all(bias)
    if per_owner:
        weights = weight_grads(me, a_one, mixed_heads, grad_qkv_late, grad_attn_low, n_g, n_e)
    else:
        flat = jnp.concatenate([grad_qkv_late[i] for i in range(3)], axis=1)
        full = [dot_f32(a_one, flat, TN), dot_f32(mixed_heads, grad_attn_low, TN)]
        full = [f.astype(BF16).reshape(n_g, rows_g, n_e, -1) for f in full]
        full = jnp.concatenate(full, axis=-1).transpose(2, 0, 1, 3)
        weights = own_blocks(full, me_g, me_e, n_g, n_e)
    out_full = out_grad(act, [after(deos[0], weights[0])] + deos[1:])
    grad_norm_one, grad_gain_one = norm_backward(grad_a_one, normed_one, inverse_one, norm_gains[0])
    small = jnp.concatenate([grad_gain_one[None], grad_gain_two, grad_route])
    small_steps = [core] + orders[0]
    small_got = xor_send(small, *core)
    got = xor_send(after(weights[1], *[way[1] for way in bias[:2]], *gated), *core)
    small = small + after(small_got, out_full)
    weights = first_sums(after(weights[0], out_full, small, *[way[1] for way in bias[2:]]), got, orders)
    first_keep = weights[0][0]
    expert_out = share(after(out_full, first_keep))
    weights = send_all(weights)
    output = combine(pos_cols, after(after_attn, first_keep), gated)
    grad_tokens = grad_after + grad_norm_one
    grad_w_gate = after(gate, first_keep).astype(F32)[None]
    wide = 3 * width // n_e
    merged = [[bias, weights]] if bias[0][0].shape == weights[0][0].shape else [[bias], [weights]]
    ways, pair = None, (small, xor_send(small, *small_steps[1]))
    for i, step in enumerate(small_steps[2:]):
        done = []
        for j, sets in enumerate(merged):
            one, new = next_sums(sets, () if j else pair)
            done.append(send_all(one))
            pair = (new[0], xor_send(new[0], *step)) if new else pair
        if i == 0:
            done[0] = tied(done[0], grad_w_gate, grad_tokens)
        if i == len(small_steps) - 4:
            done[0] = tied(done[0], output)
        merged = [[one] for one in done]
    ways = done
    small = pair[0] + pair[1]
    grad_w_expert = expert_out.astype(F32)[None]
    ways[0] = tied(ways[0], grad_w_expert)
    if len(ways) == 1:
        g_bias, g_qkv, g_out = last_merged(ways[0], wide)
    else:
        g_bias, g_weights = [jnp.concatenate(last_sums(w)) for w in ways]
        g_qkv, g_out = g_weights[:, :wide], g_weights[:, wide:]
    g_bias = g_bias.reshape(HEADS // n_e, rows_t, tok)
    return (
        output,
        grad_tokens,
        g_qkv,
        g_out,
        g_bias,
        small[:2],
        small[2:].T,
        grad_w_gate,
        grad_w_expert,
    )


def solution(mesh):
    placed = (
        P(("grp", "ep"), None),
        P(("grp", "ep"), None),
        P(),
        P(),
        P(),
        P(),
        P(),
        P("ep", None, None),
        P("ep", None, None),
        P(("grp", "ep"), None),
        P(("grp", "ep"), None),
    )
    return jax.shard_map(
        body,
        mesh=mesh,
        in_specs=placed,
        out_specs=(
            P(("grp", "ep"), None),
            P(("grp", "ep"), None),
            P("grp", "ep"),
            P("grp", "ep"),
            P("ep", "grp", None),
            P(),
            P(),
            P("ep", "grp", None),
            P("ep", "grp", None),
        ),
        check_vma=False,
    )
```
